32 devices in a mesh: level: 4 (over y, x), basin: 8 (over z, core).
Axes of the slice: x: 2, y: 2, z: 4, core: 2. Of those that a mesh axis runs over, the one named last changes fastest.
Arguments:
- runoff: float32 [4, 64, 8192], P('level', None, 'basin'), may hold values from 0 to 0.1
- travel: float32 [4, 8192], P('level', 'basin'), may hold values from 1 to 8
- downstream: int32 [4, 8192], P('level', 'basin'), may hold values from -1 to 127, as said below
- inflow_src: int32 [4, 8192], P('level', 'basin'), may hold values from -1 to 63, as said below
- reach_unit: int32 [4, 8192], P('level', 'basin'), may hold values from 0 to 8191
- rates: float32 [2, 8192], P(None, ('level', 'basin')), may hold values from 0.02 to 1
- cotangent: float32 [4, 64, 8192], P('level', None, 'basin'), may hold values from -6 to 6
Outputs:
- flows: float32 [4, 64, 8192], P('level', None, 'basin')
- rate_grads: float32 [2, 8192], P(None, ('level', 'basin'))
The draws below stay inside these ranges and needn't reach their ends.
Inputs may be any that keep to these rules, and one draw needn't show every extreme that they name: Each reach's downstream reach lies later in its own aligned block of 128 reaches, at most 8 positions on; the last reach of a block holds -1 and is the block's only outlet. `inflow_src`: in every level group each outlet number 0 to 63 is held by exactly one reach; every other reach holds -1.
All inputs are finite; a program needn't handle non-finite values.
Results may differ from the reference program's by a relative error of at most 0.00014.
Values sent between devices are 32-bit elements; how exact they have to be, the bound alone decides.
No kernel may reach another device: no remote copies, remote signals or barrier semaphores. Data moves between devices by JAX's collectives and lax.ppermute only.
A program may use at most 128 MiB of HBM per device.

```python
import math
import jax
import jax.numpy as jnp
from jax import lax

BLK = 128
STEPS = 64
TSTEP = 16
LEVELS = 4
REACHES_LVL = 8192
OUTLETS_LVL = 64
UNITS = 8192


def draw_downstream(key, part):
    places = (jnp.arange(REACHES_LVL) % BLK).astype(jnp.int32)
    spans = jnp.maximum(jnp.minimum(8, BLK - 1 - places), 1).astype(jnp.int32)
    raw = jax.random.randint(key, (LEVELS, REACHES_LVL), 0, 1 << 20).astype(jnp.int32)
    downs = places[None, :] + 1 + raw % spans[None, :]
    return jnp.where(places[None, :] == BLK - 1, -1, downs).astype(jnp.int32)


def draw_inflow_src(key, part):

    def one_level(level_key):
        order = jax.random.permutation(level_key, REACHES_LVL)
        filled = jnp.full((REACHES_LVL,), -1, jnp.int32)
        return filled.at[order[:OUTLETS_LVL]].set(jnp.arange(OUTLETS_LVL).astype(jnp.int32))
    level_keys = jax.random.split(key, LEVELS)
    return jax.vmap(one_level)(level_keys).astype(jnp.int32)


def place_ends(drawn, rng, smallest, largest):
    dims = drawn.shape
    index_at = [jax.random.randint(jax.random.fold_in(rng, axis), (), 0, dims[axis]) for axis in range(len(dims))]
    drawn = drawn.at[tuple(index_at)].set(smallest)
    longest = dims.index(max(dims))
    index_at[longest] = (index_at[longest] + 1) % dims[longest]
    return drawn.at[tuple(index_at)].set(largest)


def block_levels(stream_key, dims, shards, least, largest):
    gain, own = 1.0, jax.random.fold_in(stream_key, 6)
    for axis_at, blocks in shards:
        heights = jnp.exp(jax.random.uniform(jax.random.fold_in(own, axis_at), (blocks,), jnp.float32, least / len(shards), largest / len(shards)))
        gain = gain * jnp.repeat(heights, dims[axis_at] // blocks).reshape([-1 if axis == axis_at else 1 for axis in range(len(dims))])
    return gain


def scatter_about(stream_key, shape, deviation, bound, cuts=(), held_as=jnp.bfloat16):
    factor_of = block_levels(stream_key, shape, cuts, -0.22, 0.18) if cuts else 1.0
    values = jax.random.normal(stream_key, shape, jnp.float32) * deviation * factor_of
    return jnp.minimum(jnp.maximum(values, -bound), bound).astype(held_as)


def setup_inputs(seed: int = 0) -> dict:
    splits = jax.random.split(jax.random.key(seed), 8)
    runoff = jnp.clip(0.1 * jax.random.uniform(splits[0], (LEVELS, STEPS, REACHES_LVL), jnp.float32) ** block_levels(splits[0], (LEVELS, STEPS, REACHES_LVL), ((0, 4), (2, 8)), -0.2, 0.2), 0.0, 0.1)
    travel = jnp.clip(jnp.exp(math.log(8.0) - 2.0794415 * jax.random.uniform(splits[1], (LEVELS, REACHES_LVL), jnp.float32) ** block_levels(splits[1], (LEVELS, REACHES_LVL), ((0, 4), (1, 8)), -0.2, 0.2)), 1.0, 8.0)
    downstream = draw_downstream(jax.random.fold_in(splits[7], 71), 0)
    inflow_src = draw_inflow_src(jax.random.fold_in(splits[7], 71), 0)
    reach_unit = place_ends(jax.random.randint(splits[4], (LEVELS, REACHES_LVL), 0, UNITS), jax.random.fold_in(splits[4], 1), 0, UNITS - 1).astype(jnp.int32)
    rates = jnp.clip(jnp.exp(math.log(1.0) - 3.912023 * jax.random.uniform(splits[5], (2, UNITS), jnp.float32) ** block_levels(splits[5], (2, UNITS), ((1, 32),), -0.2, 0.2)), 0.02, 1.0)
    cotangent = scatter_about(splits[6], (LEVELS, STEPS, REACHES_LVL), 1.0, 6.0, ((0, 4), (2, 8)), jnp.float32)
    return {"runoff": runoff, "travel": travel, "downstream": downstream, "inflow_src": inflow_src, "reach_unit": reach_unit, "rates": rates, "cotangent": cotangent}


SPLIT_FAST = 0.6
MUSK_X = 0.2
HIGHEST = lax.Precision.HIGHEST

def coefficients(travel_row, down_row):
    blocks = down_row.shape[0] // BLK
    twokx = 2.0 * travel_row * MUSK_X
    denom = 2.0 * travel_row * (1.0 - MUSK_X) + 1.0
    coef_in = (1.0 - twokx) / denom
    coef_prev = (1.0 + twokx) / denom
    coef_keep = (2.0 * travel_row * (1.0 - MUSK_X) - 1.0) / denom
    downs = down_row.reshape(blocks, BLK)
    places = jnp.arange(BLK).astype(jnp.int32)
    adjacency = (downs[:, None, :] == places[None, :, None]).astype(jnp.float32)
    identity = jnp.eye(BLK, dtype=jnp.float32)
    system = identity[None] - coef_in.reshape(blocks, BLK)[:, :, None] * adjacency
    inverse = jax.vmap(lambda matrix: jax.scipy.linalg.solve_triangular(matrix, identity, lower=True))(system)
    mixing = coef_prev.reshape(blocks, BLK)[:, :, None] * adjacency + identity[None] * coef_keep.reshape(blocks, BLK)[:, :, None]
    transfer = jnp.einsum('bik,bkj->bij', inverse, mixing, precision=HIGHEST)
    return (coef_in, coef_prev, coef_keep, inverse, transfer)

def reservoirs(rain_block, fast_rate, slow_rate, fast_flow, slow_flow):
    fast_keep = jnp.exp(-fast_rate)
    slow_keep = jnp.exp(-slow_rate)
    fast_in = (1.0 - fast_keep) * SPLIT_FAST * rain_block
    slow_in = (1.0 - slow_keep) * (1.0 - SPLIT_FAST) * rain_block
    length, reaches = rain_block.shape
    groups = length // TSTEP

    def advance(state, inputs):
        fast_now, slow_now = state
        fast_part, slow_part = inputs
        rows = []
        for inner in range(TSTEP):
            fast_now = fast_keep * fast_now + fast_part[inner]
            slow_now = slow_keep * slow_now + slow_part[inner]
            rows.append(fast_now + slow_now)
        return ((fast_now, slow_now), jnp.stack(rows))
    inputs = (fast_in.reshape(groups, TSTEP, reaches), slow_in.reshape(groups, TSTEP, reaches))
    (fast_flow, slow_flow), lateral = lax.scan(advance, (fast_flow, slow_flow), inputs)
    return (fast_flow, slow_flow, lateral.reshape(length, reaches))

def route(state_in, rain_block, inflow, fast_rate, slow_rate, coefs):
    fast_flow, slow_flow, flow_last, inflow_last = state_in
    coef_in, coef_prev, coef_keep, inverse, transfer = coefs
    length, reaches = rain_block.shape
    blocks = reaches // BLK
    groups = length // TSTEP
    fast_flow, slow_flow, lateral = reservoirs(rain_block, fast_rate, slow_rate, fast_flow, slow_flow)
    before = jnp.concatenate([inflow_last[None, :], inflow[:-1]], axis=0)
    driving = coef_in * inflow + coef_prev * before + (1.0 - coef_keep) * lateral
    driven = jnp.einsum('bij,tbj->tbi', inverse, driving.reshape(length, blocks, BLK), precision=HIGHEST)

    def advance(flow_now, inputs):
        rows = []
        for inner in range(TSTEP):
            flow_now = inputs[inner] + jnp.einsum('bij,bj->bi', transfer, flow_now, precision=HIGHEST)
            rows.append(flow_now)
        return (flow_now, jnp.stack(rows))
    flow_end, flows = lax.scan(advance, flow_last.reshape(blocks, BLK), driven.reshape(groups, TSTEP, blocks, BLK))
    return ((fast_flow, slow_flow, flow_end.reshape(reaches), inflow[-1]), flows.reshape(length, reaches))

def reference(runoff, travel, downstream, inflow_src, reach_unit, rates, cotangent):
    levels, steps_all, reaches = runoff.shape
    coefs_all = [coefficients(travel[level_num], downstream[level_num]) for level_num in range(levels)]

    def forward(rate_all):
        outputs = []
        previous = None
        for level_num in range(levels):
            fast_rate = rate_all[0][reach_unit[level_num]]
            slow_rate = rate_all[1][reach_unit[level_num]]
            if level_num == 0:
                inflow = jnp.zeros((steps_all, reaches), jnp.float32)
            else:
                outlets = previous[:, BLK - 1::BLK]
                source_ids = inflow_src[level_num]
                inflow = jnp.where(source_ids >= 0, outlets[:, jnp.maximum(source_ids, 0)], jnp.float32(0.0))
            zeros_r = jnp.zeros((reaches,), jnp.float32)
            state_in = (zeros_r, zeros_r, zeros_r, zeros_r)
            _, flows = route(state_in, runoff[level_num], inflow, fast_rate, slow_rate, coefs_all[level_num])
            outputs.append(flows)
            previous = flows
        return jnp.stack(outputs)
    flows, pullback = jax.vjp(forward, rates)
    grads, = pullback(cotangent)
    return (flows, grads)
```

```python
import jax
import jax.numpy as jnp
from jax import lax
from jax.experimental import pallas as pl
from jax.experimental.pallas import tpu as pltpu
from jax.sharding import PartitionSpec as P

BLK = 128
SPLIT_FAST = 0.6
MUSK_X = 0.2
LEVELS_AXES = ("level", "basin")
F32 = jnp.float32
BF16 = jnp.bfloat16
NN = (((1,), (0,)), ((), ()))
NT = (((1,), (1,)), ((), ()))
TN = (((0,), (0,)), ((), ()))
VMEM_LIMIT = 48 << 20


def mm(left, right, dims):
    return lax.dot_general(left, right, dims, preferred_element_type=F32)


def split2(value):
    high = value.astype(BF16)
    return high, (value - high.astype(F32)).astype(BF16)


def split3(value):
    high = value.astype(BF16)
    rest = value - high.astype(F32)
    mid = rest.astype(BF16)
    return high, mid, (rest - mid.astype(F32)).astype(BF16)


def mm3(left, right, dims):
    return (
        mm(left[0], right[0], dims) + mm(left[0], right[1], dims) + mm(left[1], right[0], dims)
    )


def pick(value, onehot, dims):
    high, mid, low = split3(value)
    return mm(high, onehot, dims) + mm(mid, onehot, dims) + mm(low, onehot, dims)


def pick_right(onehot, value, dims):
    high, mid, low = split3(value)
    return mm(onehot, high, dims) + mm(onehot, mid, dims) + mm(onehot, low, dims)


def iota(shape, axis):
    return lax.broadcasted_iota(jnp.int32, shape, axis)


def coefficients(travel):
    twokx = 2.0 * travel * MUSK_X
    denom = 2.0 * travel * (1.0 - MUSK_X) + 1.0
    coef_in = (1.0 - twokx) / denom
    coef_prev = (1.0 + twokx) / denom
    coef_keep = (2.0 * travel * (1.0 - MUSK_X) - 1.0) / denom
    return coef_in, coef_prev, coef_keep


def shift_up(value, steps):
    rows = value.shape[0]
    if steps % 8 == 0:
        return jnp.concatenate([value[steps:], jnp.zeros((steps, value.shape[1]), F32)], axis=0)
    moved = pltpu.roll(value, rows - steps, 0)
    return jnp.where(iota(value.shape, 0) < rows - steps, moved, 0.0)


def shift_down(value, steps):
    rows = value.shape[0]
    if steps % 8 == 0:
        return jnp.concatenate(
            [jnp.zeros((steps, value.shape[1]), F32), value[: rows - steps]], axis=0
        )
    moved = pltpu.roll(value, steps, 0)
    return jnp.where(iota(value.shape, 0) >= steps, moved, 0.0)


def blocks_kernel(travel_ref, down_ref, src_ref, cot_ref,
                  inv_ref, pow_ref, grad_ref, resp_ref, slot_ref, ids_ref):
    steps, reaches = cot_ref.shape
    blocks = reaches // BLK
    slots = slot_ref.shape[0]
    lanes = ids_ref.shape[1]
    coef_in, coef_prev, coef_keep = coefficients(travel_ref[...])
    eye_mask = iota((BLK, BLK), 0) == iota((BLK, BLK), 1)
    eye = eye_mask.astype(F32)
    each = range(blocks)

    def part(row, b):
        return row[:, b * BLK : (b + 1) * BLK]

    down = down_ref[...].astype(F32)
    downs = jnp.concatenate([part(down, b) for b in each], axis=0)
    columns = mm(eye.astype(BF16), downs.astype(BF16), NT)
    place = iota((BLK, BLK), 1).astype(F32)
    linked = [jnp.broadcast_to(columns[:, b : b + 1], (BLK, BLK)) == place for b in each]
    base = [jnp.where(linked[b], part(coef_in, b), 0.0) for b in each]
    mixing = [
        jnp.where(linked[b], part(coef_prev, b), 0.0) + jnp.where(eye_mask, part(coef_keep, b), 0.0)
        for b in each
    ]
    total = [eye + base[b] for b in each]
    halves = [split2(base[b]) for b in each]
    power = [mm3(halves[b], halves[b], NN) for b in each]
    for level in range(2, 8):
        last = level == 7
        for b in each:
            joined = total[b] if last else jnp.concatenate([power[b], total[b]], axis=1)
            if level <= 3:
                product = mm3(split2(power[b]), split2(joined), NN)
            else:
                product = mm(power[b].astype(BF16), joined.astype(BF16), NN)
            if last:
                total[b] = total[b] + product
            else:
                power[b] = product[:, :BLK]
                total[b] = total[b] + product[:, BLK:]
    inverse = [split2(total[b]) for b in each]
    for b in each:
        inv_ref[0, b] = inverse[b][0]
        inv_ref[1, b] = inverse[b][1]
    moves = [split2(mm3(split2(mixing[b]), inverse[b], NN)) for b in each]
    state = [cot_ref[:, b * BLK : (b + 1) * BLK] for b in each]
    unit = jnp.where((iota((8, BLK), 0) == 0) & (iota((8, BLK), 1) == BLK - 1), 1.0, 0.0)
    rows = [unit for b in each]
    count = steps.bit_length() - 1
    for level in range(count):
        size = 1 << level
        for b in each:
            pow_ref[level, 0, b] = moves[b][0]
            pow_ref[level, 1, b] = moves[b][1]
            keep = steps - size
            if size < 8:
                left = jnp.concatenate([shift_up(state[b], size), shift_down(rows[b], size)], axis=0)
                out = mm3(split2(left), moves[b], NT)
                state[b] = state[b] + out[:steps]
                rows[b] = rows[b] + out[steps:]
            else:
                left = jnp.concatenate([state[b][size:], rows[b]], axis=0)
                out = mm3(split2(left), moves[b], NT)
                state[b] = jnp.concatenate(
                    [state[b][:keep] + out[:keep], state[b][keep:]], axis=0
                )
                rows[b] = jnp.concatenate([rows[b], out[keep:]], axis=0)
        if level + 1 < count:
            moves = [split2(mm3(moves[b], moves[b], NN)) for b in each]
    chosen = (
        jnp.broadcast_to(src_ref[...], (lanes, reaches)) == iota((lanes, reaches), 0)
    ).astype(BF16)
    gathered = jnp.zeros((slots, 2 * steps), F32)
    for b in each:
        both = mm3(split2(jnp.concatenate([state[b], rows[b]], axis=0)), inverse[b], NT)
        grad = both[:steps]
        resp = both[steps:]
        grad_ref[:, b * BLK : (b + 1) * BLK] = grad
        resp_ref[b] = resp
        now = part(coef_in, b)
        before = part(coef_prev, b)
        sent = jnp.concatenate(
            [now * grad + before * shift_up(grad, 1), now * resp + before * shift_down(resp, 1)],
            axis=0,
        )
        gathered = gathered + pick_right(chosen[:slots, b * BLK : (b + 1) * BLK], sent, NT)
    slot_ref[...] = gathered
    numbers = (iota((8, reaches), 1) // BLK + 1).astype(BF16)
    ids_ref[...] = mm(numbers, chosen, NT)


def lag_sum(out_rows, weight_ref, level, padded_ref, forward):
    steps = out_rows
    total = jnp.zeros((steps, padded_ref.shape[1]), F32)
    for lag in range(steps):
        start = steps - lag if forward else lag
        total = total + weight_ref[level, lag : lag + 1, :] * padded_ref[start : start + steps, :]
    return total


def lookup_rows(unit, units_here, halves, width):
    lane = BLK
    owner = unit // units_here
    inside = unit - owner * units_here
    half = inside // lane
    low = inside - half * lane
    row = 8 * owner + half
    return row, row + halves, low


def grads_kernel(where_ref, got_ref, rain_ref, travel_ref, unit_ref, grad_ref, resp_ref,
                 send_ref, drive_ref, weight_ref, ids_ref,
                 lateral_ref, fast_ref, slow_ref, padded_ref, *, levels, basins, units_here):
    steps, reaches = rain_ref.shape
    blocks = reaches // BLK
    devices = levels * basins
    lanes = ids_ref.shape[2]
    outlets = basins * blocks
    halves = units_here // BLK
    level_id = where_ref[0]
    basin_id = where_ref[1]
    _, _, coef_keep = coefficients(travel_ref[...])
    fast_row, slow_row, low = lookup_rows(unit_ref[...], units_here, halves, reaches)
    places = (iota((BLK, reaches), 0) == jnp.broadcast_to(low, (BLK, reaches))).astype(BF16)
    table = got_ref[:, 8:16, :].reshape(devices * 8, BLK)
    spread = pick(table, places, NN)
    row_of = iota((devices * 8, reaches), 0)
    fast_at = row_of == fast_row
    slow_at = row_of == slow_row
    fast_rate = jnp.sum(jnp.where(fast_at, spread, 0.0), axis=0, keepdims=True)
    slow_rate = jnp.sum(jnp.where(slow_at, spread, 0.0), axis=0, keepdims=True)
    fast_keep = jnp.exp(-fast_rate)
    slow_keep = jnp.exp(-slow_rate)
    fast_in = (1.0 - fast_keep) * SPLIT_FAST
    slow_in = (1.0 - slow_keep) * (1.0 - SPLIT_FAST)
    zero = jnp.zeros((1, reaches), F32)
    fast, slow, fast_sens, slow_sens = zero, zero, zero, zero
    for step in range(steps):
        rain = rain_ref[step : step + 1, :]
        fast_sens = fast_keep * fast_sens + (fast - SPLIT_FAST * rain)
        slow_sens = slow_keep * slow_sens + (slow - (1.0 - SPLIT_FAST) * rain)
        fast = fast_keep * fast + fast_in * rain
        slow = slow_keep * slow + slow_in * rain
        lateral_ref[step : step + 1, :] = fast + slow
        fast_ref[step : step + 1, :] = fast_sens
        slow_ref[step : step + 1, :] = slow_sens
    drive = (1.0 - coef_keep) * lateral_ref[...]
    drive_ref[...] = drive
    local = []
    for b in range(blocks):
        padded = jnp.concatenate(
            [drive[:, b * BLK : (b + 1) * BLK], jnp.zeros((BLK - steps, BLK), F32)], axis=0
        )
        product = mm3(split2(resp_ref[b]), split2(padded), NT)
        skewed = pltpu.roll(product, 0, 1, stride=1, stride_axis=0)
        local.append(jnp.sum(skewed, axis=0, keepdims=True))
    padded_ref[steps:, :] = jnp.zeros((steps, lanes), F32)
    back = []
    for l in range(levels):
        first = l * basins
        data = got_ref[first : first + basins, 0:8, :].reshape(outlets, 2 * steps)
        if lanes > outlets:
            data = jnp.concatenate([data, jnp.zeros((lanes - outlets, 2 * steps), F32)], axis=0)
        turned = jnp.transpose(data)
        back.append(turned[:steps])
        weight_ref[l] = turned[steps:]
        number = jnp.zeros((1, lanes), F32)
        for d in range(basins):
            pieces = [
                got_ref[first + d, 8 + 2 * halves + k : 9 + 2 * halves + k, :]
                for k in range(lanes // BLK)
            ]
            row = pieces[0] if len(pieces) == 1 else jnp.concatenate(pieces, axis=1)
            number = number + jnp.where(row > 0.5, row + float(blocks * d), 0.0)
        ids_ref[l] = jnp.broadcast_to(number, (8, lanes))
    returned = back[levels - 1]
    mine = jnp.where(level_id == levels - 2, returned, 0.0)
    for l in range(levels - 2, 0, -1):
        member = (
            iota((lanes, lanes), 0).astype(F32) + 1.0
            == jnp.broadcast_to(ids_ref[l, 0:1, :], (lanes, lanes))
        ).astype(BF16)
        padded_ref[:steps, :] = pick(returned, member, NN)
        returned = back[l] + lag_sum(steps, weight_ref, l, padded_ref, False)
        mine = mine + jnp.where(level_id == l - 1, returned, 0.0)
    own = (iota((8, lanes), 1) == iota((8, lanes), 0) + basin_id * blocks).astype(BF16)
    if steps < BLK:
        mine = jnp.concatenate([mine, jnp.zeros((BLK - steps, lanes), F32)], axis=0)
    mine = pick_right(own, mine, NT)
    fast_sum = []
    slow_sum = []
    for b in range(blocks):
        spreadout = jnp.broadcast_to(mine[b : b + 1, :], (steps, BLK))
        at = iota((steps, BLK), 0)
        for bit in range(steps.bit_length() - 1):
            moved = pltpu.roll(spreadout, BLK - (1 << bit), 1)
            spreadout = jnp.where((at & (1 << bit)) != 0, moved, spreadout)
        resp = jnp.concatenate([resp_ref[b], jnp.zeros((BLK - steps, BLK), F32)], axis=0)
        grad = grad_ref[:, b * BLK : (b + 1) * BLK] + mm3(split2(spreadout), split2(resp), NN)
        side = slice(b * BLK, (b + 1) * BLK)
        fast_sum.append(jnp.sum(grad * fast_ref[:, side], axis=0, keepdims=True))
        slow_sum.append(jnp.sum(grad * slow_ref[:, side], axis=0, keepdims=True))
    scale = 1.0 - coef_keep
    fast_grad = -fast_keep * scale * jnp.concatenate(fast_sum, axis=1)
    slow_grad = -slow_keep * scale * jnp.concatenate(slow_sum, axis=1)
    terms = jnp.where(fast_at, fast_grad, 0.0) + jnp.where(slow_at, slow_grad, 0.0)
    send_ref[...] = pick(terms, places, NT).reshape(devices, 8, BLK)
    half = blocks // 2
    for i in range(half):
        pair = jnp.concatenate([local[i][:, :steps], local[i + half][:, :steps]], axis=1)
        send_ref[:, 8 - half + i, :] = jnp.broadcast_to(pair, (devices, BLK))


def flows_kernel(where_ref, got_ref, travel_ref, src_ref, drive_ref, weight_ref, ids_ref,
                 inv_ref, pow_ref, flow_ref, rate_ref, padded_ref, *, levels, basins):
    steps, reaches = drive_ref.shape
    blocks = reaches // BLK
    half = blocks // 2
    lanes = ids_ref.shape[2]
    level_id = where_ref[0]
    coef_in, coef_prev, _ = coefficients(travel_ref[...])
    rate_ref[...] = jnp.sum(got_ref[...], axis=0)
    padded_ref[:steps, :] = jnp.zeros((steps, lanes), F32)
    rows = basins * 8
    row = iota((rows, lanes), 0)
    column = iota((rows, lanes), 1)
    inner = row % 8
    left = ((inner >= 8 - half) & (column == (row // 8) * blocks + inner - (8 - half))).astype(BF16)
    right = ((inner >= 8 - half) & (column == (row // 8) * blocks + inner - (8 - half) + half)).astype(BF16)
    outlet = None
    chosen = jnp.zeros((steps, lanes), F32)
    for l in range(levels - 1):
        block = got_ref[l * basins : (l + 1) * basins].reshape(rows, BLK)
        block = jnp.where(iota((rows, BLK), 0) % 8 >= 8 - half, block, 0.0)
        local = pick(block, left, TN)[:steps] + pick(block, right, TN)[steps:]
        if l == 0:
            outlet = local
        else:
            padded_ref[steps:, :] = outlet
            arriving = lag_sum(steps, weight_ref, l, padded_ref, True)
            member = (
                iota((lanes, lanes), 0).astype(F32) + 1.0
                == jnp.broadcast_to(ids_ref[l, 0:1, :], (lanes, lanes))
            ).astype(BF16)
            outlet = local + pick(arriving, member, NT)
        chosen = chosen + jnp.where(level_id == l + 1, outlet, 0.0)
    source = (iota((lanes, reaches), 0) == jnp.broadcast_to(src_ref[...], (lanes, reaches))).astype(BF16)
    inflow = pick(chosen, source, NN)
    driving = coef_in * inflow + coef_prev * shift_down(inflow, 1) + drive_ref[...]
    each = range(blocks)
    state = [
        mm3(split2(driving[:, b * BLK : (b + 1) * BLK]), (inv_ref[0, b], inv_ref[1, b]), NN)
        for b in each
    ]
    for level in range(steps.bit_length() - 1):
        size = 1 << level
        for b in each:
            move = (pow_ref[level, 0, b], pow_ref[level, 1, b])
            if size < 8:
                state[b] = state[b] + mm3(split2(shift_down(state[b], size)), move, NN)
            else:
                out = mm3(split2(state[b][: steps - size]), move, NN)
                state[b] = jnp.concatenate([state[b][:size], state[b][size:] + out], axis=0)
    for b in each:
        flow_ref[:, b * BLK : (b + 1) * BLK] = state[b]


def per_device(runoff, travel, downstream, inflow_src, reach_unit, rates, cotangent):
    _, steps, reaches = runoff.shape
    blocks = reaches // BLK
    levels = lax.axis_size("level")
    basins = lax.axis_size("basin")
    devices = levels * basins
    outlets = basins * blocks
    lanes = -(-outlets // BLK) * BLK
    units_here = rates.shape[1]
    halves = units_here // BLK
    count = steps.bit_length() - 1
    shape = jax.ShapeDtypeStruct
    smem = pl.BlockSpec(memory_space=pltpu.SMEM)
    vmem = pl.BlockSpec(memory_space=pltpu.VMEM)
    params = pltpu.CompilerParams(vmem_limit_bytes=VMEM_LIMIT)
    where = jnp.stack([lax.axis_index("level"), lax.axis_index("basin")]).astype(jnp.int32)
    inverse, powers, grad, resp, slot, ids = pl.pallas_call(
        blocks_kernel,
        out_shape=(
            shape((2, blocks, BLK, BLK), BF16),
            shape((count, 2, blocks, BLK, BLK), BF16),
            shape((steps, reaches), F32),
            shape((blocks, steps, BLK), F32),
            shape((outlets, 2 * steps), F32),
            shape((8, lanes), F32),
        ),
        in_specs=[vmem] * 4,
        out_specs=(vmem,) * 6,
        compiler_params=params,
        name="blocks",
    )(travel, downstream, inflow_src, cotangent[0])
    parts = lax.all_to_all(slot.reshape(basins, blocks, 2 * steps), "basin", 0, 0)
    used = 2 * halves + lanes // BLK
    packet = jnp.concatenate(
        [
            jnp.sum(parts, axis=0),
            rates.reshape(2 * halves, BLK),
            ids[0].reshape(lanes // BLK, BLK),
            jnp.zeros((8 - used, BLK), F32),
        ],
        axis=0,
    )
    got = lax.all_to_all(jnp.broadcast_to(packet[None], (devices, 16, BLK)), LEVELS_AXES, 0, 0)
    sent, drive, weights, numbers = pl.pallas_call(
        lambda *refs: grads_kernel(*refs, levels=levels, basins=basins, units_here=units_here),
        out_shape=(
            shape((devices, 8, BLK), F32),
            shape((steps, reaches), F32),
            shape((levels, steps, lanes), F32),
            shape((levels, 8, lanes), F32),
        ),
        in_specs=[smem] + [vmem] * 6,
        out_specs=(vmem,) * 4,
        scratch_shapes=[pltpu.VMEM((steps, reaches), F32)] * 3 + [pltpu.VMEM((2 * steps, lanes), F32)],
        compiler_params=params,
        name="grads",
    )(where, got, runoff[0], travel, reach_unit, grad, resp)
    swapped = lax.all_to_all(sent, LEVELS_AXES, 0, 0)
    flows, totals = pl.pallas_call(
        lambda *refs: flows_kernel(*refs, levels=levels, basins=basins),
        out_shape=(shape((steps, reaches), F32), shape((8, BLK), F32)),
        in_specs=[smem] + [vmem] * 8,
        out_specs=(vmem,) * 2,
        scratch_shapes=[pltpu.VMEM((2 * steps, lanes), F32)],
        compiler_params=params,
        name="flows",
    )(where, swapped, travel, inflow_src, drive, weights, numbers, inverse, powers)
    return flows[None], totals[: 2 * halves].reshape(2, units_here)


def solution(mesh):
    placed = (
        P("level", None, "basin"),
        P("level", "basin"),
        P("level", "basin"),
        P("level", "basin"),
        P("level", "basin"),
        P(None, ("level", "basin")),
        P("level", None, "basin"),
    )
    return jax.shard_map(
        per_device,
        mesh=mesh,
        in_specs=placed,
        out_specs=(P("level", None, "basin"), P(None, ("level", "basin"))),
        check_vma=False,
    )
```

```python
import jax
import jax.numpy as jnp
from jax import lax
from jax.experimental import pallas as pl
from jax.experimental.pallas import tpu as pltpu
from jax.sharding import PartitionSpec as P

BLK = 128
SPLIT_FAST = 0.6
MUSK_X = 0.2
LEVELS_AXES = ("level", "basin")
F32 = jnp.float32
BF16 = jnp.bfloat16
NN = (((1,), (0,)), ((), ()))
NT = (((1,), (1,)), ((), ()))
TN = (((0,), (0,)), ((), ()))
VMEM_LIMIT = 48 << 20
CAP = 16


def mm(left, right, dims):
    return lax.dot_general(left, right, dims, preferred_element_type=F32)


def split2(value):
    high = value.astype(BF16)
    return high, (value - high.astype(F32)).astype(BF16)


def split3(value):
    high = value.astype(BF16)
    rest = value - high.astype(F32)
    mid = rest.astype(BF16)
    return high, mid, (rest - mid.astype(F32)).astype(BF16)


def mm3(left, right, dims):
    return (
        mm(left[0], right[0], dims) + mm(left[0], right[1], dims) + mm(left[1], right[0], dims)
    )


def mm6(left, right, dims):
    small = mm(left[1], right[1], dims) + mm(left[0], right[2], dims) + mm(left[2], right[0], dims)
    return mm(left[0], right[0], dims) + (
        mm(left[0], right[1], dims) + mm(left[1], right[0], dims) + small
    )


def pick(value, onehot, dims):
    high, mid, low = split3(value)
    return mm(high, onehot, dims) + mm(mid, onehot, dims) + mm(low, onehot, dims)


def pick_right(onehot, value, dims):
    high, mid, low = split3(value)
    return mm(onehot, high, dims) + mm(onehot, mid, dims) + mm(onehot, low, dims)


def iota(shape, axis):
    return lax.broadcasted_iota(jnp.int32, shape, axis)


def coefficients(travel):
    twokx = 2.0 * travel * MUSK_X
    denom = 2.0 * travel * (1.0 - MUSK_X) + 1.0
    coef_in = (1.0 - twokx) / denom
    coef_prev = (1.0 + twokx) / denom
    coef_keep = (2.0 * travel * (1.0 - MUSK_X) - 1.0) / denom
    return coef_in, coef_prev, coef_keep


def shift_up(value, steps):
    rows = value.shape[0]
    if steps % 8 == 0:
        return jnp.concatenate([value[steps:], jnp.zeros((steps, value.shape[1]), F32)], axis=0)
    moved = pltpu.roll(value, rows - steps, 0)
    return jnp.where(iota(value.shape, 0) < rows - steps, moved, 0.0)


def shift_down(value, steps):
    rows = value.shape[0]
    if steps % 8 == 0:
        return jnp.concatenate(
            [jnp.zeros((steps, value.shape[1]), F32), value[: rows - steps]], axis=0
        )
    moved = pltpu.roll(value, steps, 0)
    return jnp.where(iota(value.shape, 0) >= steps, moved, 0.0)


def copies(pairs, sems):
    started = []
    for at, (source, target) in enumerate(pairs):
        copy = pltpu.make_async_copy(source, target, sems.at[at])
        copy.start()
        started.append(copy)
    return started


def stacked(row, blocks):
    return jnp.concatenate([row[:, b * BLK : (b + 1) * BLK] for b in range(blocks)], axis=0)


def blocks_kernel(where_ref, travel_hbm, down_hbm, src_hbm, rates_hbm, cot_hbm,
                  packet_ref, grad_hbm, resp_hbm, move_hbm,
                  travel_ref, down_ref, src_ref, rates_ref, cot_ref,
                  grad_ref, resp_ref, move_ref, in_sems, out_sems, *, basins):
    steps, reaches = cot_ref.shape
    blocks = reaches // BLK
    devices, height, _ = packet_ref.shape
    width = (height - CAP) // 8 * BLK
    each = range(blocks)
    loads = copies(
        [(travel_hbm, travel_ref), (down_hbm, down_ref), (src_hbm, src_ref),
         (rates_hbm, rates_ref), (cot_hbm.at[0], cot_ref)], in_sems
    )
    for copy in loads[:4]:
        copy.wait()
    coef_in, coef_prev, coef_keep = coefficients(travel_ref[...])
    eye_mask = iota((BLK, BLK), 0) == iota((BLK, BLK), 1)
    eye = eye_mask.astype(F32)

    def part(row, b):
        return row[:, b * BLK : (b + 1) * BLK]

    downs = stacked(down_ref[...].astype(F32), blocks)
    columns = mm(eye.astype(BF16), downs.astype(BF16), NT)
    place = iota((BLK, BLK), 1).astype(F32)
    turned = [
        pick_right(eye.astype(BF16), stacked(row, blocks), NT)
        for row in (coef_in, coef_prev, coef_keep)
    ]
    linked = [jnp.broadcast_to(columns[:, b : b + 1], (BLK, BLK)) == place for b in each]
    base = [jnp.where(linked[b], part(coef_in, b), 0.0) for b in each]
    hops = [linked[b].astype(BF16) for b in each]
    total = [eye + base[b] for b in each]
    power = base
    for level in range(1, 8):
        for b in each:
            if level == 1:
                joined = power[b]
            elif level == 7:
                joined = total[b]
            else:
                joined = jnp.concatenate([power[b], total[b]], axis=1)
            if level <= 3:
                scale = jnp.sum(power[b], axis=1, keepdims=True)
                product = scale * pick_right(hops[b], joined, NN)
            else:
                product = mm(power[b].astype(BF16), joined.astype(BF16), NN)
            if level <= 2:
                hops[b] = mm(hops[b], hops[b], NN).astype(BF16)
            if level == 1:
                power[b] = product
            elif level == 7:
                total[b] = total[b] + product
            else:
                power[b] = product[:, :BLK]
                total[b] = total[b] + product[:, BLK:]
    inverse = [split2(total[b]) for b in each]
    stores = []

    def publish(at, moves):
        for b in each:
            move_ref[at, 0, b] = moves[b][0]
            move_ref[at, 1, b] = moves[b][1]
        copy = pltpu.make_async_copy(move_ref.at[at], move_hbm.at[at], out_sems.at[at])
        copy.start()
        stores.append(copy)

    publish(0, inverse)
    following = [
        pick_right(linked[b].astype(BF16), turned[1][:, b : b + 1] * total[b], NN)
        + turned[2][:, b : b + 1] * total[b]
        for b in each
    ]
    moves = [split3(following[b]) for b in each]
    loads[4].wait()
    state = [cot_ref[:, b * BLK : (b + 1) * BLK] for b in each]
    unit = jnp.where((iota((8, BLK), 0) == 0) & (iota((8, BLK), 1) == BLK - 1), 1.0, 0.0)
    rows = [unit for b in each]
    count = steps.bit_length() - 1
    for level in range(count):
        size = 1 << level
        publish(level + 1, moves)
        keep = steps - size
        for b in each:
            if size < 8:
                left = jnp.concatenate([shift_up(state[b], size), shift_down(rows[b], size)], axis=0)
                out = mm3(split2(left), moves[b], NT)
                state[b] = state[b] + out[:steps]
                rows[b] = rows[b] + out[steps:]
            else:
                left = jnp.concatenate([state[b][size:], rows[b]], axis=0)
                out = mm3(split2(left), moves[b], NT)
                state[b] = jnp.concatenate(
                    [state[b][:keep] + out[:keep], state[b][keep:]], axis=0
                )
                rows[b] = jnp.concatenate([rows[b], out[keep:]], axis=0)
        if level + 1 < count:
            if level < 2:
                moves = [split3(mm6(moves[b], moves[b], NN)) for b in each]
            else:
                moves = [split2(mm3(moves[b], moves[b], NN)) for b in each]
    sources = stacked(src_ref[...], blocks)
    held = sources >= 0
    upper = (iota((BLK, BLK), 0) <= iota((BLK, BLK), 1)).astype(BF16)
    ranks = mm(held.astype(BF16), upper, NN)
    basin_id = where_ref[1]
    offset = jnp.zeros((1, 1), F32)
    packed = jnp.zeros((CAP, 2 * steps), F32)
    labels = jnp.zeros((8, width), F32)
    responses = []
    for b in each:
        both = mm3(split2(jnp.concatenate([state[b], rows[b]], axis=0)), inverse[b], NT)
        grad_ref[:, b * BLK : (b + 1) * BLK] = both[:steps]
        resp_ref[b] = both[steps:]
        responses.append(both)
    for copy in copies([(grad_ref, grad_hbm), (resp_ref, resp_hbm)], out_sems.at[pl.ds(count + 1, 2)]):
        stores.append(copy)
    for b in each:
        rank = jnp.where(held[b : b + 1], ranks[b : b + 1] + offset, 0.0)
        offset = offset + ranks[b : b + 1, BLK - 1 : BLK]
        row_at = iota((CAP, BLK), 0).astype(F32) + 1.0
        chosen = (jnp.broadcast_to(rank, (CAP, BLK)) == row_at).astype(BF16)
        grad = responses[b][:steps]
        resp = responses[b][steps:]
        now = part(coef_in, b)
        before = part(coef_prev, b)
        sent = jnp.concatenate(
            [now * grad + before * shift_up(grad, 1), now * resp + before * shift_down(resp, 1)],
            axis=0,
        )
        packed = packed + pick_right(chosen, sent, NT)
        lane_at = iota((width, BLK), 0) - basin_id * CAP
        wide = (
            (jnp.broadcast_to(rank, (width, BLK)) == lane_at.astype(F32) + 1.0) & (lane_at < CAP)
        ).astype(BF16)
        which = jnp.broadcast_to((sources[b : b + 1] + 1).astype(F32), (8, BLK))
        block_at = (basin_id * blocks + (b + 1)).astype(F32)
        values = jnp.where(iota((8, BLK), 0) == 0, which, block_at)
        labels = labels + mm(values.astype(BF16), wide, NT)
    labels = jnp.where(iota((8, width), 0) == 2, jnp.broadcast_to(offset, (8, width)), labels)
    parts = rates_ref.shape[1] // BLK
    rate_rows = [rates_ref[k : k + 1, h * BLK : (h + 1) * BLK] for k in range(2) for h in range(parts)]
    for group in range(width // BLK):
        rows_here = labels[:4, group * BLK : (group + 1) * BLK]
        first = CAP + 8 * group
        if group == 0:
            tail = rate_rows + [jnp.zeros((1, BLK), F32)] * (4 - len(rate_rows))
        else:
            tail = [jnp.zeros((4, BLK), F32)]
        piece = jnp.concatenate([rows_here] + tail, axis=0)
        packet_ref[:, first : first + 8, :] = jnp.broadcast_to(piece[None], (devices, 8, BLK))
    packet_ref[:, :CAP, :] = jnp.broadcast_to(packed[None], (devices, CAP, BLK))
    for copy in stores:
        copy.wait()


def lag_sum(out_rows, weight_ref, level, padded_ref, forward):
    steps = out_rows
    total = jnp.zeros((steps, padded_ref.shape[1]), F32)
    for lag in range(steps):
        start = steps - lag if forward else lag
        total = total + weight_ref[level, lag : lag + 1, :] * padded_ref[start : start + steps, :]
    return total


def lookup_rows(unit, units_here, halves, width):
    lane = BLK
    owner = unit // units_here
    inside = unit - owner * units_here
    half = inside // lane
    low = inside - half * lane
    row = 8 * owner + 4 + half
    return row, row + halves, low


def grads_kernel(where_ref, got_ref, travel_hbm, unit_hbm, rain_hbm, grad_hbm, resp_hbm,
                 send_ref, drive_ref, weight_ref, ids_ref, full_ref,
                 travel_ref, unit_ref, rain_ref, grad_ref, resp_ref,
                 lateral_ref, fast_ref, slow_ref, padded_ref, sems, *, levels, basins, units_here):
    steps, reaches = rain_ref.shape
    loads = copies(
        [(travel_hbm, travel_ref), (unit_hbm, unit_ref), (rain_hbm.at[0], rain_ref),
         (resp_hbm, resp_ref), (grad_hbm, grad_ref)], sems
    )
    blocks = reaches // BLK
    devices = levels * basins
    lanes = ids_ref.shape[2]
    full_ref[0] = jnp.max(got_ref[basins:, CAP + 2 : CAP + 3, :]).astype(jnp.int32)
    outlets = basins * blocks
    halves = units_here // BLK
    level_id = where_ref[0]
    basin_id = where_ref[1]
    padded_ref[steps:, :] = jnp.zeros((steps, lanes), F32)
    back = [None]
    for l in range(1, levels):
        first = l * basins
        data = got_ref[first : first + basins, :CAP, :].reshape(basins * CAP, BLK)
        turned = jnp.transpose(data)
        labels = jnp.concatenate(
            [
                jnp.sum(got_ref[first : first + basins, CAP + 8 * g : CAP + 8 * g + 8, :], axis=0)
                for g in range((got_ref.shape[1] - CAP) // 8)
            ],
            axis=1,
        )[:, : basins * CAP]
        slot_of = (
            jnp.broadcast_to(labels[0:1], (lanes, basins * CAP))
            == iota((lanes, basins * CAP), 0).astype(F32) + 1.0
        ).astype(BF16)
        dense = pick(turned, slot_of, NT)
        back.append(dense[:steps])
        weight_ref[l] = dense[steps:]
        ids_ref[l] = mm(labels.astype(BF16), slot_of, NT)
    returned = back[levels - 1]
    mine = jnp.where(level_id == levels - 2, returned, 0.0)
    for l in range(levels - 2, 0, -1):
        member = (
            iota((lanes, lanes), 0).astype(F32) + 1.0
            == jnp.broadcast_to(ids_ref[l, 1:2, :], (lanes, lanes))
        ).astype(BF16)
        padded_ref[:steps, :] = pick(returned, member, NN)
        returned = back[l] + lag_sum(steps, weight_ref, l, padded_ref, False)
        mine = mine + jnp.where(level_id == l - 1, returned, 0.0)
    own = (iota((8, lanes), 1) == iota((8, lanes), 0) + basin_id * blocks).astype(BF16)
    if steps < BLK:
        mine = jnp.concatenate([mine, jnp.zeros((BLK - steps, lanes), F32)], axis=0)
    mine = pick_right(own, mine, NT)
    loads[0].wait()
    loads[1].wait()
    _, _, coef_keep = coefficients(travel_ref[...])
    fast_row, slow_row, low = lookup_rows(unit_ref[...], units_here, halves, reaches)
    places = (iota((BLK, reaches), 0) == jnp.broadcast_to(low, (BLK, reaches))).astype(BF16)
    table = got_ref[:, CAP : CAP + 8, :].reshape(devices * 8, BLK)
    spread = pick(table, places, NN)
    row_of = iota((devices * 8, reaches), 0)
    fast_at = row_of == fast_row
    slow_at = row_of == slow_row
    fast_rate = jnp.sum(jnp.where(fast_at, spread, 0.0), axis=0, keepdims=True)
    slow_rate = jnp.sum(jnp.where(slow_at, spread, 0.0), axis=0, keepdims=True)
    fast_keep = jnp.exp(-fast_rate)
    slow_keep = jnp.exp(-slow_rate)
    fast_in = (1.0 - fast_keep) * SPLIT_FAST
    slow_in = (1.0 - slow_keep) * (1.0 - SPLIT_FAST)
    loads[2].wait()
    zero = jnp.zeros((1, reaches), F32)
    fast, slow, fast_sens, slow_sens = zero, zero, zero, zero
    for step in range(steps):
        rain = rain_ref[step : step + 1, :]
        fast_sens = fast_keep * fast_sens + (fast - SPLIT_FAST * rain)
        slow_sens = slow_keep * slow_sens + (slow - (1.0 - SPLIT_FAST) * rain)
        fast = fast_keep * fast + fast_in * rain
        slow = slow_keep * slow + slow_in * rain
        lateral_ref[step : step + 1, :] = fast + slow
        fast_ref[step : step + 1, :] = fast_sens
        slow_ref[step : step + 1, :] = slow_sens
    drive = (1.0 - coef_keep) * lateral_ref[...]
    drive_ref[...] = drive
    loads[3].wait()
    local = []
    for b in range(blocks):
        padded = jnp.concatenate(
            [drive[:, b * BLK : (b + 1) * BLK], jnp.zeros((BLK - steps, BLK), F32)], axis=0
        )
        product = mm3(split2(resp_ref[b]), split2(padded), NT)
        skewed = pltpu.roll(product, 0, 1, stride=1, stride_axis=0)
        local.append(jnp.sum(skewed, axis=0, keepdims=True))
    loads[4].wait()
    fast_sum = []
    slow_sum = []
    for b in range(blocks):
        spreadout = jnp.broadcast_to(mine[b : b + 1, :], (steps, BLK))
        at = iota((steps, BLK), 0)
        for bit in range(steps.bit_length() - 1):
            moved = pltpu.roll(spreadout, BLK - (1 << bit), 1)
            spreadout = jnp.where((at & (1 << bit)) != 0, moved, spreadout)
        resp = jnp.concatenate([resp_ref[b], jnp.zeros((BLK - steps, BLK), F32)], axis=0)
        grad = grad_ref[:, b * BLK : (b + 1) * BLK] + mm3(split2(spreadout), split2(resp), NN)
        side = slice(b * BLK, (b + 1) * BLK)
        fast_sum.append(jnp.sum(grad * fast_ref[:, side], axis=0, keepdims=True))
        slow_sum.append(jnp.sum(grad * slow_ref[:, side], axis=0, keepdims=True))
    scale = 1.0 - coef_keep
    fast_grad = -fast_keep * scale * jnp.concatenate(fast_sum, axis=1)
    slow_grad = -slow_keep * scale * jnp.concatenate(slow_sum, axis=1)
    terms = jnp.where(fast_at, fast_grad, 0.0) + jnp.where(slow_at, slow_grad, 0.0)
    send_ref[...] = pick(terms, places, NT).reshape(devices, 8, BLK)
    half = blocks // 2
    for i in range(half):
        pair = jnp.concatenate([local[i][:, :steps], local[i + half][:, :steps]], axis=1)
        send_ref[:, i, :] = jnp.broadcast_to(pair, (devices, BLK))


def flows_kernel(where_ref, got_ref, travel_hbm, src_hbm, drive_ref, weight_ref, ids_ref, move_hbm,
                 flow_ref, rate_ref, travel_ref, src_ref, move_ref, padded_ref, sems, *, levels, basins):
    steps, reaches = drive_ref.shape
    count = steps.bit_length() - 1
    loads = copies(
        [(travel_hbm, travel_ref), (src_hbm, src_ref)]
        + [(move_hbm.at[k], move_ref.at[k]) for k in range(count + 1)], sems
    )
    blocks = reaches // BLK
    half = blocks // 2
    lanes = ids_ref.shape[2]
    level_id = where_ref[0]
    summed = jnp.sum(got_ref[...], axis=0)
    parts = rate_ref.shape[1] // BLK
    for k in range(2):
        for h in range(parts):
            at = 4 + k * parts + h
            rate_ref[k : k + 1, h * BLK : (h + 1) * BLK] = summed[at : at + 1]
    padded_ref[:steps, :] = jnp.zeros((steps, lanes), F32)
    rows = basins * 8
    row = iota((rows, lanes), 0)
    column = iota((rows, lanes), 1)
    inner = row % 8
    left = ((inner < half) & (column == (row // 8) * blocks + inner)).astype(BF16)
    right = ((inner < half) & (column == (row // 8) * blocks + inner + half)).astype(BF16)
    outlet = None
    chosen = jnp.zeros((steps, lanes), F32)
    for l in range(levels - 1):
        block = got_ref[l * basins : (l + 1) * basins].reshape(rows, BLK)
        block = jnp.where(iota((rows, BLK), 0) % 8 < half, block, 0.0)
        local = pick(block, left, TN)[:steps] + pick(block, right, TN)[steps:]
        if l == 0:
            outlet = local
        else:
            padded_ref[steps:, :] = outlet
            arriving = lag_sum(steps, weight_ref, l, padded_ref, True)
            member = (
                iota((lanes, lanes), 0).astype(F32) + 1.0
                == jnp.broadcast_to(ids_ref[l, 1:2, :], (lanes, lanes))
            ).astype(BF16)
            outlet = local + pick(arriving, member, NT)
        chosen = chosen + jnp.where(level_id == l + 1, outlet, 0.0)
    loads[0].wait()
    loads[1].wait()
    coef_in, coef_prev, _ = coefficients(travel_ref[...])
    source = (iota((lanes, reaches), 0) == jnp.broadcast_to(src_ref[...], (lanes, reaches))).astype(BF16)
    inflow = pick(chosen, source, NN)
    driving = coef_in * inflow + coef_prev * shift_down(inflow, 1) + drive_ref[...]
    each = range(blocks)
    loads[2].wait()
    state = [
        mm3(split2(driving[:, b * BLK : (b + 1) * BLK]), (move_ref[0, 0, b], move_ref[0, 1, b]), NN)
        for b in each
    ]
    for level in range(steps.bit_length() - 1):
        size = 1 << level
        loads[3 + level].wait()
        for b in each:
            move = (move_ref[level + 1, 0, b], move_ref[level + 1, 1, b])
            if size < 8:
                state[b] = state[b] + mm3(split2(shift_down(state[b], size)), move, NN)
            else:
                out = mm3(split2(state[b][: steps - size]), move, NN)
                state[b] = jnp.concatenate([state[b][:size], state[b][size:] + out], axis=0)
    for b in each:
        flow_ref[:, b * BLK : (b + 1) * BLK] = state[b]


def per_device(runoff, travel, downstream, inflow_src, reach_unit, rates, cotangent):
    _, steps, reaches = runoff.shape
    blocks = reaches // BLK
    levels = lax.axis_size("level")
    basins = lax.axis_size("basin")
    devices = levels * basins
    outlets = basins * blocks
    lanes = -(-outlets // BLK) * BLK
    units_here = rates.shape[1]
    halves = units_here // BLK
    count = steps.bit_length() - 1
    shape = jax.ShapeDtypeStruct
    smem = pl.BlockSpec(memory_space=pltpu.SMEM)
    vmem = pl.BlockSpec(memory_space=pltpu.VMEM)
    hbm = pl.BlockSpec(memory_space=pltpu.HBM)
    params = pltpu.CompilerParams(vmem_limit_bytes=VMEM_LIMIT)
    row_f32 = pltpu.VMEM((1, reaches), F32)
    row_i32 = pltpu.VMEM((1, reaches), jnp.int32)
    series = pltpu.VMEM((steps, reaches), F32)
    answers = pltpu.VMEM((blocks, steps, BLK), F32)
    moves_shape = (count + 1, 2, blocks, BLK, BLK)
    height = CAP + 8 * (-(-basins * CAP // BLK))
    where = jnp.stack([lax.axis_index("level"), lax.axis_index("basin")]).astype(jnp.int32)
    packet, grad, resp, moves = pl.pallas_call(
        lambda *refs: blocks_kernel(*refs, basins=basins),
        out_shape=(
            shape((devices, height, BLK), F32),
            shape((steps, reaches), F32),
            shape((blocks, steps, BLK), F32),
            shape(moves_shape, BF16),
        ),
        in_specs=[smem] + [hbm] * 5,
        out_specs=(vmem, hbm, hbm, hbm),
        scratch_shapes=[
            row_f32, row_i32, row_i32, pltpu.VMEM(rates.shape, F32), series,
            series, answers, pltpu.VMEM(moves_shape, BF16),
            pltpu.SemaphoreType.DMA((5,)), pltpu.SemaphoreType.DMA((count + 3,)),
        ],
        compiler_params=params,
        name="blocks",
    )(where, travel, downstream, inflow_src, rates, cotangent)
    got = lax.all_to_all(packet, LEVELS_AXES, 0, 0)

    def finish(got):
        sent, drive, weights, numbers, full = pl.pallas_call(
            lambda *refs: grads_kernel(*refs, levels=levels, basins=basins, units_here=units_here),
            out_shape=(
                shape((devices, 8, BLK), F32),
                shape((steps, reaches), F32),
                shape((levels, steps, lanes), F32),
                shape((levels, 8, lanes), F32),
                shape((1,), jnp.int32),
            ),
            in_specs=[smem, vmem] + [hbm] * 5,
            out_specs=(vmem,) * 4 + (smem,),
            scratch_shapes=[row_f32, row_i32, series, series, answers, series, series, series,
                            pltpu.VMEM((2 * steps, lanes), F32), pltpu.SemaphoreType.DMA((5,))],
            compiler_params=params,
            name="grads",
        )(where, got, travel, reach_unit, runoff, grad, resp)
        swapped = lax.all_to_all(sent, LEVELS_AXES, 0, 0)
        flows, totals = pl.pallas_call(
            lambda *refs: flows_kernel(*refs, levels=levels, basins=basins),
            out_shape=(shape((steps, reaches), F32), shape((2, units_here), F32)),
            in_specs=[smem, vmem, hbm, hbm, vmem, vmem, vmem, hbm],
            out_specs=(vmem,) * 2,
            scratch_shapes=[row_f32, row_i32, pltpu.VMEM(moves_shape, BF16),
                            pltpu.VMEM((2 * steps, lanes), F32), pltpu.SemaphoreType.DMA((count + 3,))],
            compiler_params=params,
            name="flows",
        )(where, swapped, travel, inflow_src, drive, weights, numbers, moves)
        return flows, totals, full[0]

    flows, totals, full = finish(got)
    flows, totals = lax.cond(
        full > CAP,
        lambda done: finish(spread_sources(got, grad, resp, travel, inflow_src))[:2],
        lambda done: done,
        (flows, totals),
    )
    return flows[None], totals


def spread_sources(got, grad, resp, travel, inflow_src):
    blocks, steps, _ = resp.shape
    basins = lax.axis_size("basin")
    basin_id = lax.axis_index("basin")
    outlets = basins * blocks
    reaches = blocks * BLK
    coef_in, coef_prev, _ = coefficients(travel)
    answer = resp.transpose(1, 0, 2).reshape(steps, reaches)
    zero = jnp.zeros((1, reaches), F32)
    back = coef_in * grad + coef_prev * jnp.concatenate([grad[1:], zero], axis=0)
    ahead = coef_in * answer + coef_prev * jnp.concatenate([zero, answer[:-1]], axis=0)
    block_of = (jnp.arange(reaches) // BLK + 1 + basin_id * blocks).astype(F32)
    table = jnp.concatenate([back, ahead, jnp.broadcast_to(block_of[None], (BLK, reaches))], axis=0)
    chosen = (inflow_src == jnp.arange(outlets)[:, None]).astype(F32)
    mine = lax.dot_general(chosen, table, NT, precision=lax.Precision.HIGHEST)
    parts = lax.all_to_all(mine.reshape(basins, blocks, 2 * steps + BLK), "basin", 0, 0).sum(axis=0)
    width = (got.shape[1] - CAP) // 8 * BLK
    place = jnp.arange(blocks) + basin_id * CAP
    onto = (jnp.arange(width)[None, :] == place[:, None]).astype(F32)
    slot_row = ((jnp.arange(blocks) + basin_id * blocks + 1).astype(F32)[:, None] * onto).sum(axis=0)
    block_row = (parts[:, 2 * steps : 2 * steps + 1] * onto).sum(axis=0)
    labels = jnp.concatenate(
        [slot_row[None], block_row[None], jnp.zeros((6, width), F32)], axis=0
    )
    labels = labels.reshape(8, width // BLK, BLK).transpose(1, 0, 2).reshape(-1, BLK)
    packet = jnp.concatenate(
        [parts[:, : 2 * steps], jnp.zeros((CAP - blocks, 2 * steps), F32), labels], axis=0
    )
    fresh = lax.all_to_all(
        jnp.broadcast_to(packet[None], got.shape), LEVELS_AXES, 0, 0
    )
    keep = jnp.arange(got.shape[1]) >= CAP + 4
    return jnp.where(keep[None, :, None], got, fresh)


def solution(mesh):
    placed = (
        P("level", None, "basin"),
        P("level", "basin"),
        P("level", "basin"),
        P("level", "basin"),
        P("level", "basin"),
        P(None, ("level", "basin")),
        P("level", None, "basin"),
    )
    return jax.shard_map(
        per_device,
        mesh=mesh,
        in_specs=placed,
        out_specs=(P("level", None, "basin"), P(None, ("level", "basin"))),
        check_vma=False,
    )
```

```python
import jax
import jax.numpy as jnp
from jax import lax
from jax.experimental import pallas as pl
from jax.experimental.pallas import tpu as pltpu
from jax.sharding import PartitionSpec as P

BLK = 128
SPLIT_FAST = 0.6
MUSK_X = 0.2
LEVELS_AXES = ("level", "basin")
F32 = jnp.float32
BF16 = jnp.bfloat16
NN = (((1,), (0,)), ((), ()))
NT = (((1,), (1,)), ((), ()))
TN = (((0,), (0,)), ((), ()))
VMEM_LIMIT = 48 << 20
CAP = 16


def mm(left, right, dims):
    return lax.dot_general(left, right, dims, preferred_element_type=F32)


def split2(value):
    high = value.astype(BF16)
    return high, (value - high.astype(F32)).astype(BF16)


def split3(value):
    high = value.astype(BF16)
    rest = value - high.astype(F32)
    mid = rest.astype(BF16)
    return high, mid, (rest - mid.astype(F32)).astype(BF16)


def beside(*parts):
    return jnp.concatenate(parts, axis=1)


def above(*parts):
    return jnp.concatenate(parts, axis=0)


def folded(product):
    half = product.shape[1] // 2
    return product[:, :half] + product[:, half:]


def mm3(left, right, dims):
    high, low = right[0], right[1]
    empty = jnp.zeros_like(high)
    wide = beside(left[0], left[1])
    if dims == NT:
        return folded(mm(wide, above(beside(high, high), beside(low, empty)), NT))
    return folded(mm(wide, above(beside(high, low), beside(high, empty)), NN))


def mm6(left, right):
    high, mid, low = right
    first = mm(beside(left[0], left[1]), above(beside(high, mid), beside(high, mid)), NN)
    return folded(first) + mm(beside(left[0], left[2]), above(low, high), NN)


def pick(value, onehot, dims):
    high, mid, low = split3(value)
    if dims == TN:
        return mm(high, onehot, TN) + mm(mid, onehot, TN) + mm(low, onehot, TN)
    if dims == NT:
        both = beside(onehot, onehot)
    else:
        both = above(onehot, onehot)
    return mm(beside(high, mid), both, dims) + mm(low, onehot, dims)


def pick_right(onehot, value, dims):
    high, mid, low = split3(value)
    empty = jnp.zeros_like(low)
    wide = beside(onehot, onehot)
    if dims == NT:
        return folded(mm(wide, above(beside(high, mid), beside(low, empty)), NT))
    return folded(mm(wide, above(beside(high, low), beside(mid, empty)), NN))


def iota(shape, axis):
    return lax.broadcasted_iota(jnp.int32, shape, axis)


def coefficients(travel):
    twokx = 2.0 * travel * MUSK_X
    denom = 2.0 * travel * (1.0 - MUSK_X) + 1.0
    coef_in = (1.0 - twokx) / denom
    coef_prev = (1.0 + twokx) / denom
    coef_keep = (2.0 * travel * (1.0 - MUSK_X) - 1.0) / denom
    return coef_in, coef_prev, coef_keep


def shift_up(value, steps):
    rows = value.shape[0]
    if steps % 8 == 0:
        return jnp.concatenate([value[steps:], jnp.zeros((steps, value.shape[1]), F32)], axis=0)
    moved = pltpu.roll(value, rows - steps, 0)
    return jnp.where(iota(value.shape, 0) < rows - steps, moved, 0.0)


def shift_down(value, steps):
    rows = value.shape[0]
    if steps % 8 == 0:
        return jnp.concatenate(
            [jnp.zeros((steps, value.shape[1]), F32), value[: rows - steps]], axis=0
        )
    moved = pltpu.roll(value, steps, 0)
    return jnp.where(iota(value.shape, 0) >= steps, moved, 0.0)


def copies(pairs, sems):
    started = []
    for at, (source, target) in enumerate(pairs):
        copy = pltpu.make_async_copy(source, target, sems.at[at])
        copy.start()
        started.append(copy)
    return started


def stacked(row, blocks):
    return jnp.concatenate([row[:, b * BLK : (b + 1) * BLK] for b in range(blocks)], axis=0)


def blocks_kernel(where_ref, travel_hbm, down_hbm, src_hbm, rates_hbm, cot_hbm,
                  packet_ref, grad_hbm, resp_hbm, move_hbm,
                  travel_ref, down_ref, src_ref, rates_ref, cot_ref,
                  grad_ref, resp_ref, move_ref, in_sems, out_sems, *, basins):
    steps, reaches = cot_ref.shape
    blocks = reaches // BLK
    devices, height, _ = packet_ref.shape
    width = (height - CAP) // 8 * BLK
    each = range(blocks)
    loads = copies(
        [(travel_hbm, travel_ref), (down_hbm, down_ref), (src_hbm, src_ref),
         (rates_hbm, rates_ref), (cot_hbm.at[0], cot_ref)], in_sems
    )
    for copy in loads[:4]:
        copy.wait()
    coef_in, coef_prev, coef_keep = coefficients(travel_ref[...])
    eye_mask = iota((BLK, BLK), 0) == iota((BLK, BLK), 1)
    eye = eye_mask.astype(F32)

    def part(row, b):
        return row[:, b * BLK : (b + 1) * BLK]

    downs = stacked(down_ref[...].astype(F32), blocks)
    columns = mm(eye.astype(BF16), downs.astype(BF16), NT)
    place = iota((BLK, BLK), 1).astype(F32)
    turned = [
        pick_right(eye.astype(BF16), stacked(row, blocks), NT)
        for row in (coef_in, coef_prev, coef_keep)
    ]
    linked = [jnp.broadcast_to(columns[:, b : b + 1], (BLK, BLK)) == place for b in each]
    base = [jnp.where(linked[b], part(coef_in, b), 0.0) for b in each]
    hops = [linked[b].astype(BF16) for b in each]
    total = [eye + base[b] for b in each]
    power = base
    for level in range(1, 8):
        for b in each:
            if level == 1:
                joined = power[b]
            elif level == 7:
                joined = total[b]
            else:
                joined = jnp.concatenate([power[b], total[b]], axis=1)
            if level <= 3:
                scale = jnp.sum(power[b], axis=1, keepdims=True)
                product = scale * pick_right(hops[b], joined, NN)
            else:
                product = mm(power[b].astype(BF16), joined.astype(BF16), NN)
            if level <= 2:
                hops[b] = mm(hops[b], hops[b], NN).astype(BF16)
            if level == 1:
                power[b] = product
            elif level == 7:
                total[b] = total[b] + product
            else:
                power[b] = product[:, :BLK]
                total[b] = total[b] + product[:, BLK:]
    inverse = [split2(total[b]) for b in each]
    stores = []

    def publish(at, moves):
        for b in each:
            move_ref[at, 0, b] = moves[b][0]
            move_ref[at, 1, b] = moves[b][1]
        copy = pltpu.make_async_copy(move_ref.at[at], move_hbm.at[at], out_sems.at[at])
        copy.start()
        stores.append(copy)

    publish(0, inverse)
    following = [
        pick_right(linked[b].astype(BF16), turned[1][:, b : b + 1] * total[b], NN)
        + turned[2][:, b : b + 1] * total[b]
        for b in each
    ]
    moves = [split3(following[b]) for b in each]
    loads[4].wait()
    state = [cot_ref[:, b * BLK : (b + 1) * BLK] for b in each]
    unit = jnp.where((iota((8, BLK), 0) == 0) & (iota((8, BLK), 1) == BLK - 1), 1.0, 0.0)
    rows = [unit for b in each]
    count = steps.bit_length() - 1
    for level in range(count):
        size = 1 << level
        publish(level + 1, moves)
        keep = steps - size
        for b in each:
            if size < 8:
                left = jnp.concatenate([shift_up(state[b], size), shift_down(rows[b], size)], axis=0)
                out = mm3(split2(left), moves[b], NT)
                state[b] = state[b] + out[:steps]
                rows[b] = rows[b] + out[steps:]
            else:
                left = jnp.concatenate([state[b][size:], rows[b]], axis=0)
                out = mm3(split2(left), moves[b], NT)
                state[b] = jnp.concatenate(
                    [state[b][:keep] + out[:keep], state[b][keep:]], axis=0
                )
                rows[b] = jnp.concatenate([rows[b], out[keep:]], axis=0)
        if level + 1 < count:
            if level < 2:
                moves = [split3(mm6(moves[b], moves[b])) for b in each]
            else:
                moves = [split2(mm3(moves[b], moves[b], NN)) for b in each]
    sources = stacked(src_ref[...], blocks)
    held = sources >= 0
    upper = (iota((BLK, BLK), 0) <= iota((BLK, BLK), 1)).astype(BF16)
    ranks = mm(held.astype(BF16), upper, NN)
    basin_id = where_ref[1]
    offset = jnp.zeros((1, 1), F32)
    packed = jnp.zeros((CAP, 2 * steps), F32)
    labels = jnp.zeros((8, width), F32)
    responses = []
    for b in each:
        both = mm3(split2(jnp.concatenate([state[b], rows[b]], axis=0)), inverse[b], NT)
        grad_ref[:, b * BLK : (b + 1) * BLK] = both[:steps]
        resp_ref[b] = both[steps:]
        responses.append(both)
    for copy in copies([(grad_ref, grad_hbm), (resp_ref, resp_hbm)], out_sems.at[pl.ds(count + 1, 2)]):
        stores.append(copy)
    for b in each:
        rank = jnp.where(held[b : b + 1], ranks[b : b + 1] + offset, 0.0)
        offset = offset + ranks[b : b + 1, BLK - 1 : BLK]
        row_at = iota((CAP, BLK), 0).astype(F32) + 1.0
        chosen = (jnp.broadcast_to(rank, (CAP, BLK)) == row_at).astype(BF16)
        grad = responses[b][:steps]
        resp = responses[b][steps:]
        now = part(coef_in, b)
        before = part(coef_prev, b)
        sent = jnp.concatenate(
            [now * grad + before * shift_up(grad, 1), now * resp + before * shift_down(resp, 1)],
            axis=0,
        )
        packed = packed + pick_right(chosen, sent, NT)
        lane_at = iota((width, BLK), 0) - basin_id * CAP
        wide = (
            (jnp.broadcast_to(rank, (width, BLK)) == lane_at.astype(F32) + 1.0) & (lane_at < CAP)
        ).astype(BF16)
        which = jnp.broadcast_to((sources[b : b + 1] + 1).astype(F32), (8, BLK))
        block_at = (basin_id * blocks + (b + 1)).astype(F32)
        values = jnp.where(iota((8, BLK), 0) == 0, which, block_at)
        labels = labels + mm(values.astype(BF16), wide, NT)
    labels = jnp.where(iota((8, width), 0) == 2, jnp.broadcast_to(offset, (8, width)), labels)
    parts = rates_ref.shape[1] // BLK
    rate_rows = [rates_ref[k : k + 1, h * BLK : (h + 1) * BLK] for k in range(2) for h in range(parts)]
    for group in range(width // BLK):
        rows_here = labels[:4, group * BLK : (group + 1) * BLK]
        first = CAP + 8 * group
        if group == 0:
            tail = rate_rows + [jnp.zeros((1, BLK), F32)] * (4 - len(rate_rows))
        else:
            tail = [jnp.zeros((4, BLK), F32)]
        piece = jnp.concatenate([rows_here] + tail, axis=0)
        packet_ref[:, first : first + 8, :] = jnp.broadcast_to(piece[None], (devices, 8, BLK))
    packet_ref[:, :CAP, :] = jnp.broadcast_to(packed[None], (devices, CAP, BLK))
    for copy in stores:
        copy.wait()


def lag_sum(out_rows, weight_ref, level, padded_ref, forward):
    steps = out_rows
    total = jnp.zeros((steps, padded_ref.shape[1]), F32)
    for lag in range(steps):
        start = steps - lag if forward else lag
        total = total + weight_ref[level, lag : lag + 1, :] * padded_ref[start : start + steps, :]
    return total


def lookup_rows(unit, units_here, halves, width):
    lane = BLK
    owner = unit // units_here
    inside = unit - owner * units_here
    half = inside // lane
    low = inside - half * lane
    row = 8 * owner + 4 + half
    return row, row + halves, low


def grads_kernel(where_ref, got_ref, travel_hbm, unit_hbm, rain_hbm, grad_hbm, resp_hbm,
                 send_ref, drive_ref, weight_ref, ids_ref, full_ref,
                 travel_ref, unit_ref, rain_ref, grad_ref, resp_ref,
                 lateral_ref, fast_ref, slow_ref, padded_ref, sems, *, levels, basins, units_here):
    steps, reaches = rain_ref.shape
    loads = copies(
        [(travel_hbm, travel_ref), (unit_hbm, unit_ref), (rain_hbm.at[0], rain_ref),
         (resp_hbm, resp_ref), (grad_hbm, grad_ref)], sems
    )
    blocks = reaches // BLK
    devices = levels * basins
    lanes = ids_ref.shape[2]
    full_ref[0] = jnp.max(got_ref[basins:, CAP + 2 : CAP + 3, :]).astype(jnp.int32)
    outlets = basins * blocks
    halves = units_here // BLK
    level_id = where_ref[0]
    basin_id = where_ref[1]
    padded_ref[steps:, :] = jnp.zeros((steps, lanes), F32)
    back = [None]
    for l in range(1, levels):
        first = l * basins
        data = got_ref[first : first + basins, :CAP, :].reshape(basins * CAP, BLK)
        turned = jnp.transpose(data)
        labels = jnp.concatenate(
            [
                jnp.sum(got_ref[first : first + basins, CAP + 8 * g : CAP + 8 * g + 8, :], axis=0)
                for g in range((got_ref.shape[1] - CAP) // 8)
            ],
            axis=1,
        )[:, : basins * CAP]
        slot_of = (
            jnp.broadcast_to(labels[0:1], (lanes, basins * CAP))
            == iota((lanes, basins * CAP), 0).astype(F32) + 1.0
        ).astype(BF16)
        dense = pick(turned, slot_of, NT)
        back.append(dense[:steps])
        weight_ref[l] = dense[steps:]
        ids_ref[l] = mm(labels.astype(BF16), slot_of, NT)
    returned = back[levels - 1]
    mine = jnp.where(level_id == levels - 2, returned, 0.0)
    for l in range(levels - 2, 0, -1):
        member = (
            iota((lanes, lanes), 0).astype(F32) + 1.0
            == jnp.broadcast_to(ids_ref[l, 1:2, :], (lanes, lanes))
        ).astype(BF16)
        padded_ref[:steps, :] = pick(returned, member, NN)
        returned = back[l] + lag_sum(steps, weight_ref, l, padded_ref, False)
        mine = mine + jnp.where(level_id == l - 1, returned, 0.0)
    own = (iota((8, lanes), 1) == iota((8, lanes), 0) + basin_id * blocks).astype(BF16)
    if steps < BLK:
        mine = jnp.concatenate([mine, jnp.zeros((BLK - steps, lanes), F32)], axis=0)
    mine = pick_right(own, mine, NT)
    loads[0].wait()
    loads[1].wait()
    _, _, coef_keep = coefficients(travel_ref[...])
    fast_row, slow_row, low = lookup_rows(unit_ref[...], units_here, halves, reaches)
    places = (iota((BLK, reaches), 0) == jnp.broadcast_to(low, (BLK, reaches))).astype(BF16)
    table = got_ref[:, CAP : CAP + 8, :].reshape(devices * 8, BLK)
    spread = pick(table, places, NN)
    row_of = iota((devices * 8, reaches), 0)
    fast_at = row_of == fast_row
    slow_at = row_of == slow_row
    fast_rate = jnp.sum(jnp.where(fast_at, spread, 0.0), axis=0, keepdims=True)
    slow_rate = jnp.sum(jnp.where(slow_at, spread, 0.0), axis=0, keepdims=True)
    fast_keep = jnp.exp(-fast_rate)
    slow_keep = jnp.exp(-slow_rate)
    fast_in = (1.0 - fast_keep) * SPLIT_FAST
    slow_in = (1.0 - slow_keep) * (1.0 - SPLIT_FAST)
    loads[2].wait()
    zero = jnp.zeros((1, reaches), F32)
    fast, slow, fast_sens, slow_sens = zero, zero, zero, zero
    for step in range(steps):
        rain = rain_ref[step : step + 1, :]
        fast_sens = fast_keep * fast_sens + (fast - SPLIT_FAST * rain)
        slow_sens = slow_keep * slow_sens + (slow - (1.0 - SPLIT_FAST) * rain)
        fast = fast_keep * fast + fast_in * rain
        slow = slow_keep * slow + slow_in * rain
        lateral_ref[step : step + 1, :] = fast + slow
        fast_ref[step : step + 1, :] = fast_sens
        slow_ref[step : step + 1, :] = slow_sens
    drive = (1.0 - coef_keep) * lateral_ref[...]
    drive_ref[...] = drive
    loads[3].wait()
    local = []
    for b in range(blocks):
        padded = jnp.concatenate(
            [drive[:, b * BLK : (b + 1) * BLK], jnp.zeros((BLK - steps, BLK), F32)], axis=0
        )
        product = mm3(split2(resp_ref[b]), split2(padded), NT)
        skewed = pltpu.roll(product, 0, 1, stride=1, stride_axis=0)
        local.append(jnp.sum(skewed, axis=0, keepdims=True))
    loads[4].wait()
    fast_sum = []
    slow_sum = []
    for b in range(blocks):
        spreadout = jnp.broadcast_to(mine[b : b + 1, :], (steps, BLK))
        at = iota((steps, BLK), 0)
        for bit in range(steps.bit_length() - 1):
            moved = pltpu.roll(spreadout, BLK - (1 << bit), 1)
            spreadout = jnp.where((at & (1 << bit)) != 0, moved, spreadout)
        resp = jnp.concatenate([resp_ref[b], jnp.zeros((BLK - steps, BLK), F32)], axis=0)
        grad = grad_ref[:, b * BLK : (b + 1) * BLK] + mm3(split2(spreadout), split2(resp), NN)
        side = slice(b * BLK, (b + 1) * BLK)
        fast_sum.append(jnp.sum(grad * fast_ref[:, side], axis=0, keepdims=True))
        slow_sum.append(jnp.sum(grad * slow_ref[:, side], axis=0, keepdims=True))
    scale = 1.0 - coef_keep
    fast_grad = -fast_keep * scale * jnp.concatenate(fast_sum, axis=1)
    slow_grad = -slow_keep * scale * jnp.concatenate(slow_sum, axis=1)
    terms = jnp.where(fast_at, fast_grad, 0.0) + jnp.where(slow_at, slow_grad, 0.0)
    send_ref[...] = pick(terms, places, NT).reshape(devices, 8, BLK)
    half = blocks // 2
    for i in range(half):
        pair = jnp.concatenate([local[i][:, :steps], local[i + half][:, :steps]], axis=1)
        send_ref[:, i, :] = jnp.broadcast_to(pair, (devices, BLK))


def flows_kernel(where_ref, got_ref, travel_hbm, src_hbm, drive_ref, weight_ref, ids_ref, move_hbm,
                 flow_hbm, rate_ref, travel_ref, src_ref, move_ref, padded_ref, flow_ref, sems, out_sems, *, levels, basins):
    steps, reaches = drive_ref.shape
    count = steps.bit_length() - 1
    loads = copies(
        [(travel_hbm, travel_ref), (src_hbm, src_ref)]
        + [(move_hbm.at[k], move_ref.at[k]) for k in range(count + 1)], sems
    )
    blocks = reaches // BLK
    half = blocks // 2
    lanes = ids_ref.shape[2]
    level_id = where_ref[0]
    summed = jnp.sum(got_ref[...], axis=0)
    parts = rate_ref.shape[1] // BLK
    for k in range(2):
        for h in range(parts):
            at = 4 + k * parts + h
            rate_ref[k : k + 1, h * BLK : (h + 1) * BLK] = summed[at : at + 1]
    padded_ref[:steps, :] = jnp.zeros((steps, lanes), F32)
    rows = basins * 8
    row = iota((rows, lanes), 0)
    column = iota((rows, lanes), 1)
    inner = row % 8
    left = ((inner < half) & (column == (row // 8) * blocks + inner)).astype(BF16)
    right = ((inner < half) & (column == (row // 8) * blocks + inner + half)).astype(BF16)
    outlet = None
    chosen = jnp.zeros((steps, lanes), F32)
    for l in range(levels - 1):
        block = got_ref[l * basins : (l + 1) * basins].reshape(rows, BLK)
        block = jnp.where(iota((rows, BLK), 0) % 8 < half, block, 0.0)
        local = pick(block, left, TN)[:steps] + pick(block, right, TN)[steps:]
        if l == 0:
            outlet = local
        else:
            padded_ref[steps:, :] = outlet
            arriving = lag_sum(steps, weight_ref, l, padded_ref, True)
            member = (
                iota((lanes, lanes), 0).astype(F32) + 1.0
                == jnp.broadcast_to(ids_ref[l, 1:2, :], (lanes, lanes))
            ).astype(BF16)
            outlet = local + pick(arriving, member, NT)
        chosen = chosen + jnp.where(level_id == l + 1, outlet, 0.0)
    loads[0].wait()
    loads[1].wait()
    coef_in, coef_prev, _ = coefficients(travel_ref[...])
    source = (iota((lanes, reaches), 0) == jnp.broadcast_to(src_ref[...], (lanes, reaches))).astype(BF16)
    inflow = pick(chosen, source, NN)
    driving = coef_in * inflow + coef_prev * shift_down(inflow, 1) + drive_ref[...]
    each = range(blocks)
    loads[2].wait()
    state = [
        mm3(split2(driving[:, b * BLK : (b + 1) * BLK]), (move_ref[0, 0, b], move_ref[0, 1, b]), NN)
        for b in each
    ]
    for level in range(steps.bit_length() - 1):
        size = 1 << level
        loads[3 + level].wait()
        for b in each:
            move = (move_ref[level + 1, 0, b], move_ref[level + 1, 1, b])
            if size < 8:
                state[b] = state[b] + mm3(split2(shift_down(state[b], size)), move, NN)
            else:
                out = mm3(split2(state[b][: steps - size]), move, NN)
                state[b] = jnp.concatenate([state[b][:size], state[b][size:] + out], axis=0)
    stores = []
    for b in each:
        flow_ref[:, b * BLK : (b + 1) * BLK] = state[b]
        side = pl.ds(b * BLK, BLK)
        copy = pltpu.make_async_copy(flow_ref.at[:, side], flow_hbm.at[0, :, side], out_sems.at[b])
        copy.start()
        stores.append(copy)
    for copy in stores:
        copy.wait()


def per_device(runoff, travel, downstream, inflow_src, reach_unit, rates, cotangent):
    _, steps, reaches = runoff.shape
    blocks = reaches // BLK
    levels = lax.axis_size("level")
    basins = lax.axis_size("basin")
    devices = levels * basins
    outlets = basins * blocks
    lanes = -(-outlets // BLK) * BLK
    units_here = rates.shape[1]
    halves = units_here // BLK
    count = steps.bit_length() - 1
    shape = jax.ShapeDtypeStruct
    smem = pl.BlockSpec(memory_space=pltpu.SMEM)
    vmem = pl.BlockSpec(memory_space=pltpu.VMEM)
    hbm = pl.BlockSpec(memory_space=pltpu.HBM)
    params = pltpu.CompilerParams(vmem_limit_bytes=VMEM_LIMIT)
    row_f32 = pltpu.VMEM((1, reaches), F32)
    row_i32 = pltpu.VMEM((1, reaches), jnp.int32)
    series = pltpu.VMEM((steps, reaches), F32)
    answers = pltpu.VMEM((blocks, steps, BLK), F32)
    moves_shape = (count + 1, 2, blocks, BLK, BLK)
    height = CAP + 8 * (-(-basins * CAP // BLK))
    still = lambda *values: [pltpu.with_memory_space_constraint(value, pltpu.HBM) for value in values]
    where = jnp.stack([lax.axis_index("level"), lax.axis_index("basin")]).astype(jnp.int32)
    packet, grad, resp, moves = pl.pallas_call(
        lambda *refs: blocks_kernel(*refs, basins=basins),
        out_shape=(
            shape((devices, height, BLK), F32),
            shape((steps, reaches), F32),
            shape((blocks, steps, BLK), F32),
            shape(moves_shape, BF16),
        ),
        in_specs=[smem] + [hbm] * 5,
        out_specs=(vmem, hbm, hbm, hbm),
        scratch_shapes=[
            row_f32, row_i32, row_i32, pltpu.VMEM(rates.shape, F32), series,
            series, answers, pltpu.VMEM(moves_shape, BF16),
            pltpu.SemaphoreType.DMA((5,)), pltpu.SemaphoreType.DMA((count + 3,)),
        ],
        compiler_params=params,
        name="blocks",
    )(where, *still(travel, downstream, inflow_src, rates, cotangent))
    got = lax.all_to_all(packet, LEVELS_AXES, 0, 0)

    def finish(got):
        sent, drive, weights, numbers, full = pl.pallas_call(
            lambda *refs: grads_kernel(*refs, levels=levels, basins=basins, units_here=units_here),
            out_shape=(
                shape((devices, 8, BLK), F32),
                shape((steps, reaches), F32),
                shape((levels, steps, lanes), F32),
                shape((levels, 8, lanes), F32),
                shape((1,), jnp.int32),
            ),
            in_specs=[smem, vmem] + [hbm] * 5,
            out_specs=(vmem,) * 4 + (smem,),
            scratch_shapes=[row_f32, row_i32, series, series, answers, series, series, series,
                            pltpu.VMEM((2 * steps, lanes), F32), pltpu.SemaphoreType.DMA((5,))],
            compiler_params=params,
            name="grads",
        )(where, got, *still(travel, reach_unit, runoff, grad, resp))
        swapped = lax.all_to_all(sent, LEVELS_AXES, 0, 0)
        flows, totals = pl.pallas_call(
            lambda *refs: flows_kernel(*refs, levels=levels, basins=basins),
            out_shape=(shape((1, steps, reaches), F32), shape((2, units_here), F32)),
            in_specs=[smem, vmem, hbm, hbm, vmem, vmem, vmem, hbm],
            out_specs=(hbm, vmem),
            scratch_shapes=[row_f32, row_i32, pltpu.VMEM(moves_shape, BF16),
                            pltpu.VMEM((2 * steps, lanes), F32), series,
                            pltpu.SemaphoreType.DMA((count + 3,)), pltpu.SemaphoreType.DMA((blocks,))],
            compiler_params=params,
            name="flows",
        )(where, swapped, *still(travel, inflow_src), drive, weights, numbers, *still(moves))
        return flows, totals, full[0]

    flows, totals, full = finish(got)
    flows, totals = lax.cond(
        full > CAP,
        lambda done: finish(spread_sources(got, grad, resp, travel, inflow_src))[:2],
        lambda done: done,
        (flows, totals),
    )
    return flows, totals


def spread_sources(got, grad, resp, travel, inflow_src):
    blocks, steps, _ = resp.shape
    basins = lax.axis_size("basin")
    basin_id = lax.axis_index("basin")
    outlets = basins * blocks
    reaches = blocks * BLK
    coef_in, coef_prev, _ = coefficients(travel)
    answer = resp.transpose(1, 0, 2).reshape(steps, reaches)
    zero = jnp.zeros((1, reaches), F32)
    back = coef_in * grad + coef_prev * jnp.concatenate([grad[1:], zero], axis=0)
    ahead = coef_in * answer + coef_prev * jnp.concatenate([zero, answer[:-1]], axis=0)
    block_of = (jnp.arange(reaches) // BLK + 1 + basin_id * blocks).astype(F32)
    table = jnp.concatenate([back, ahead, jnp.broadcast_to(block_of[None], (BLK, reaches))], axis=0)
    chosen = (inflow_src == jnp.arange(outlets)[:, None]).astype(F32)
    mine = lax.dot_general(chosen, table, NT, precision=lax.Precision.HIGHEST)
    parts = lax.all_to_all(mine.reshape(basins, blocks, 2 * steps + BLK), "basin", 0, 0).sum(axis=0)
    width = (got.shape[1] - CAP) // 8 * BLK
    place = jnp.arange(blocks) + basin_id * CAP
    onto = (jnp.arange(width)[None, :] == place[:, None]).astype(F32)
    slot_row = ((jnp.arange(blocks) + basin_id * blocks + 1).astype(F32)[:, None] * onto).sum(axis=0)
    block_row = (parts[:, 2 * steps : 2 * steps + 1] * onto).sum(axis=0)
    labels = jnp.concatenate(
        [slot_row[None], block_row[None], jnp.zeros((6, width), F32)], axis=0
    )
    labels = labels.reshape(8, width // BLK, BLK).transpose(1, 0, 2).reshape(-1, BLK)
    packet = jnp.concatenate(
        [parts[:, : 2 * steps], jnp.zeros((CAP - blocks, 2 * steps), F32), labels], axis=0
    )
    fresh = lax.all_to_all(
        jnp.broadcast_to(packet[None], got.shape), LEVELS_AXES, 0, 0
    )
    keep = jnp.arange(got.shape[1]) >= CAP + 4
    return jnp.where(keep[None, :, None], got, fresh)


def solution(mesh):
    placed = (
        P("level", None, "basin"),
        P("level", "basin"),
        P("level", "basin"),
        P("level", "basin"),
        P("level", "basin"),
        P(None, ("level", "basin")),
        P("level", None, "basin"),
    )
    return jax.shard_map(
        per_device,
        mesh=mesh,
        in_specs=placed,
        out_specs=(P("level", None, "basin"), P(None, ("level", "basin"))),
        check_vma=False,
    )
```

```python
import jax
import jax.numpy as jnp
from jax import lax
from jax.experimental import pallas as pl
from jax.experimental.pallas import tpu as pltpu
from jax.sharding import PartitionSpec as P

BLK = 128
SPLIT_FAST = 0.6
MUSK_X = 0.2
LEVELS_AXES = ("level", "basin")
F32 = jnp.float32
BF16 = jnp.bfloat16
NN = (((1,), (0,)), ((), ()))
NT = (((1,), (1,)), ((), ()))
TN = (((0,), (0,)), ((), ()))
VMEM_LIMIT = 48 << 20
CAP = 16
NEAR = 5


def mm(left, right, dims):
    return lax.dot_general(left, right, dims, preferred_element_type=F32)


def split2(value):
    high = value.astype(BF16)
    return high, (value - high.astype(F32)).astype(BF16)


def split3(value):
    high = value.astype(BF16)
    rest = value - high.astype(F32)
    mid = rest.astype(BF16)
    return high, mid, (rest - mid.astype(F32)).astype(BF16)


def beside(*parts):
    return jnp.concatenate(parts, axis=1)


def above(*parts):
    return jnp.concatenate(parts, axis=0)


def folded(product):
    half = product.shape[1] // 2
    return product[:, :half] + product[:, half:]


def mm3(left, right, dims):
    high, low = right[0], right[1]
    empty = jnp.zeros_like(high)
    wide = beside(left[0], left[1])
    if dims == NT:
        return folded(mm(wide, above(beside(high, high), beside(low, empty)), NT))
    return folded(mm(wide, above(beside(high, low), beside(high, empty)), NN))


def mm6(left, right):
    high, mid, low = right
    first = mm(beside(left[0], left[1]), above(beside(high, mid), beside(high, mid)), NN)
    return folded(first) + mm(beside(left[0], left[2]), above(low, high), NN)


def pick(value, onehot, dims):
    high, mid, low = split3(value)
    if dims == TN:
        return mm(high, onehot, TN) + mm(mid, onehot, TN) + mm(low, onehot, TN)
    if dims == NT:
        both = beside(onehot, onehot)
    else:
        both = above(onehot, onehot)
    return mm(beside(high, mid), both, dims) + mm(low, onehot, dims)


def pick_right(onehot, value, dims):
    high, mid, low = split3(value)
    empty = jnp.zeros_like(low)
    wide = beside(onehot, onehot)
    if dims == NT:
        return folded(mm(wide, above(beside(high, mid), beside(low, empty)), NT))
    return folded(mm(wide, above(beside(high, low), beside(mid, empty)), NN))


def iota(shape, axis):
    return lax.broadcasted_iota(jnp.int32, shape, axis)


def coefficients(travel):
    twokx = 2.0 * travel * MUSK_X
    denom = 2.0 * travel * (1.0 - MUSK_X) + 1.0
    coef_in = (1.0 - twokx) / denom
    coef_prev = (1.0 + twokx) / denom
    coef_keep = (2.0 * travel * (1.0 - MUSK_X) - 1.0) / denom
    return coef_in, coef_prev, coef_keep


def shift_up(value, steps):
    rows = value.shape[0]
    if steps % 8 == 0:
        return jnp.concatenate([value[steps:], jnp.zeros((steps, value.shape[1]), F32)], axis=0)
    moved = pltpu.roll(value, rows - steps, 0)
    return jnp.where(iota(value.shape, 0) < rows - steps, moved, 0.0)


def shift_down(value, steps):
    rows = value.shape[0]
    if steps % 8 == 0:
        return jnp.concatenate(
            [jnp.zeros((steps, value.shape[1]), F32), value[: rows - steps]], axis=0
        )
    moved = pltpu.roll(value, steps, 0)
    return jnp.where(iota(value.shape, 0) >= steps, moved, 0.0)


def copies(pairs, sems):
    started = []
    for at, (source, target) in enumerate(pairs):
        copy = pltpu.make_async_copy(source, target, sems.at[at])
        copy.start()
        started.append(copy)
    return started


def stacked(row, blocks):
    return jnp.concatenate([row[:, b * BLK : (b + 1) * BLK] for b in range(blocks)], axis=0)


def still(*values):
    return [pltpu.with_memory_space_constraint(value, pltpu.HBM) for value in values]


def relay_kernel(*refs):
    half = len(refs) // 2
    for copy in copies(list(zip(refs[:half], refs[half:-1])), refs[-1]):
        copy.wait()


def blocks_kernel(where_ref, travel_hbm, down_hbm, src_hbm, rates_hbm, cot_hbm,
                  packet_ref, grad_hbm, resp_hbm, move_hbm,
                  travel_ref, down_ref, src_ref, rates_ref, cot_ref,
                  grad_ref, resp_ref, move_ref, in_sems, out_sems, *, basins):
    steps, reaches = cot_ref.shape
    blocks = reaches // BLK
    devices, height, _ = packet_ref.shape
    width = (height - CAP) // 8 * BLK
    each = range(blocks)
    loads = copies(
        [(travel_hbm, travel_ref), (down_hbm, down_ref), (src_hbm, src_ref),
         (rates_hbm, rates_ref), (cot_hbm.at[0], cot_ref)], in_sems
    )
    for copy in loads[:4]:
        copy.wait()
    coef_in, coef_prev, coef_keep = coefficients(travel_ref[...])
    eye_mask = iota((BLK, BLK), 0) == iota((BLK, BLK), 1)
    eye = eye_mask.astype(F32)

    def part(row, b):
        return row[:, b * BLK : (b + 1) * BLK]

    downs = stacked(down_ref[...].astype(F32), blocks)
    columns = mm(eye.astype(BF16), downs.astype(BF16), NT)
    place = iota((BLK, BLK), 1).astype(F32)
    turned = [
        pick_right(eye.astype(BF16), stacked(row, blocks), NT)
        for row in (coef_in, coef_prev, coef_keep)
    ]
    linked = [jnp.broadcast_to(columns[:, b : b + 1], (BLK, BLK)) == place for b in each]
    base = [jnp.where(linked[b], part(coef_in, b), 0.0) for b in each]
    hops = [linked[b].astype(BF16) for b in each]
    total = [eye + base[b] for b in each]
    power = base
    for level in range(1, 8):
        for b in each:
            if level == 1:
                joined = power[b]
            elif level == 7:
                joined = total[b]
            else:
                joined = jnp.concatenate([power[b], total[b]], axis=1)
            if level <= 3:
                scale = jnp.sum(power[b], axis=1, keepdims=True)
                product = scale * pick_right(hops[b], joined, NN)
            else:
                product = mm(power[b].astype(BF16), joined.astype(BF16), NN)
            if level <= 2:
                hops[b] = mm(hops[b], hops[b], NN).astype(BF16)
            if level == 1:
                power[b] = product
            elif level == 7:
                total[b] = total[b] + product
            else:
                power[b] = product[:, :BLK]
                total[b] = total[b] + product[:, BLK:]
    inverse = [split2(total[b]) for b in each]
    stores = []

    def publish(at, moves):
        for b in each:
            move_ref[at, 0, b] = moves[b][0]
            move_ref[at, 1, b] = moves[b][1]
        copy = pltpu.make_async_copy(move_ref.at[at], move_hbm.at[at], out_sems.at[at])
        copy.start()
        stores.append(copy)

    publish(0, inverse)
    following = [
        pick_right(linked[b].astype(BF16), turned[1][:, b : b + 1] * total[b], NN)
        + turned[2][:, b : b + 1] * total[b]
        for b in each
    ]
    moves = [split3(following[b]) for b in each]
    loads[4].wait()
    state = [cot_ref[:, b * BLK : (b + 1) * BLK] for b in each]
    unit = jnp.where((iota((8, BLK), 0) == 0) & (iota((8, BLK), 1) == BLK - 1), 1.0, 0.0)
    rows = [unit for b in each]
    count = steps.bit_length() - 1
    for level in range(count):
        size = 1 << level
        publish(level + 1, moves)
        keep = steps - size
        for b in each:
            if size < 8:
                left = jnp.concatenate([shift_up(state[b], size), shift_down(rows[b], size)], axis=0)
                out = mm3(split2(left), moves[b], NT)
                state[b] = state[b] + out[:steps]
                rows[b] = rows[b] + out[steps:]
            else:
                left = jnp.concatenate([state[b][size:], rows[b]], axis=0)
                out = mm3(split2(left), moves[b], NT)
                state[b] = jnp.concatenate(
                    [state[b][:keep] + out[:keep], state[b][keep:]], axis=0
                )
                rows[b] = jnp.concatenate([rows[b], out[keep:]], axis=0)
        if level + 1 < count:
            if level < 2:
                moves = [split3(mm6(moves[b], moves[b])) for b in each]
            else:
                moves = [split2(mm3(moves[b], moves[b], NN)) for b in each]
    sources = stacked(src_ref[...], blocks)
    held = sources >= 0
    upper = (iota((BLK, BLK), 0) <= iota((BLK, BLK), 1)).astype(BF16)
    ranks = mm(held.astype(BF16), upper, NN)
    basin_id = where_ref[1]
    offset = jnp.zeros((1, 1), F32)
    packed = jnp.zeros((CAP, 2 * steps), F32)
    labels = jnp.zeros((8, width), F32)
    responses = []
    for b in each:
        both = mm3(split2(jnp.concatenate([state[b], rows[b]], axis=0)), inverse[b], NT)
        grad_ref[:, b * BLK : (b + 1) * BLK] = both[:steps]
        resp_ref[b] = both[steps:]
        responses.append(both)
    for copy in copies([(grad_ref, grad_hbm), (resp_ref, resp_hbm)], out_sems.at[pl.ds(count + 1, 2)]):
        stores.append(copy)
    for b in each:
        rank = jnp.where(held[b : b + 1], ranks[b : b + 1] + offset, 0.0)
        offset = offset + ranks[b : b + 1, BLK - 1 : BLK]
        row_at = iota((CAP, BLK), 0).astype(F32) + 1.0
        chosen = (jnp.broadcast_to(rank, (CAP, BLK)) == row_at).astype(BF16)
        grad = responses[b][:steps]
        resp = responses[b][steps:]
        now = part(coef_in, b)
        before = part(coef_prev, b)
        sent = jnp.concatenate(
            [now * grad + before * shift_up(grad, 1), now * resp + before * shift_down(resp, 1)],
            axis=0,
        )
        packed = packed + pick_right(chosen, sent, NT)
        lane_at = iota((width, BLK), 0) - basin_id * CAP
        wide = (
            (jnp.broadcast_to(rank, (width, BLK)) == lane_at.astype(F32) + 1.0) & (lane_at < CAP)
        ).astype(BF16)
        which = jnp.broadcast_to((sources[b : b + 1] + 1).astype(F32), (8, BLK))
        block_at = (basin_id * blocks + (b + 1)).astype(F32)
        values = jnp.where(iota((8, BLK), 0) == 0, which, block_at)
        labels = labels + mm(values.astype(BF16), wide, NT)
    labels = jnp.where(iota((8, width), 0) == 2, jnp.broadcast_to(offset, (8, width)), labels)
    parts = rates_ref.shape[1] // BLK
    rate_rows = [rates_ref[k : k + 1, h * BLK : (h + 1) * BLK] for k in range(2) for h in range(parts)]
    for group in range(width // BLK):
        rows_here = labels[:4, group * BLK : (group + 1) * BLK]
        first = CAP + 8 * group
        if group == 0:
            tail = rate_rows + [jnp.zeros((1, BLK), F32)] * (4 - len(rate_rows))
        else:
            tail = [jnp.zeros((4, BLK), F32)]
        piece = jnp.concatenate([rows_here] + tail, axis=0)
        packet_ref[:, first : first + 8, :] = jnp.broadcast_to(piece[None], (devices, 8, BLK))
    packet_ref[:, :CAP, :] = jnp.broadcast_to(packed[None], (devices, CAP, BLK))
    for copy in stores:
        copy.wait()


def lag_sum(steps, weight_ref, level, padded_ref, forward):
    tiles = steps // 8
    total = [jnp.zeros((8, padded_ref.shape[1]), F32)] * tiles
    for lag in range(steps):
        weight = weight_ref[level, lag : lag + 1, :]
        if forward:
            first, last = lag // 8, tiles
            start = steps - lag + 8 * first
        else:
            first, last = 0, tiles - lag // 8
            start = lag
        shifted = padded_ref[start : start + 8 * (last - first), :]
        for at in range(first, last):
            total[at] = total[at] + weight * shifted[8 * (at - first) : 8 * (at - first) + 8]
    return jnp.concatenate(total, axis=0)


def grads_kernel(where_ref, got_ref, travel_hbm, unit_hbm, rain_hbm, grad_hbm, resp_hbm,
                 send_ref, drive_ref, weight_ref, ids_ref,
                 travel_ref, unit_ref, rain_ref, grad_ref, resp_ref,
                 lateral_ref, fast_ref, slow_ref, padded_ref, sems, *, levels, basins, units_here):
    steps, reaches = grad_ref.shape
    blocks = reaches // BLK
    pitch = steps + 8
    rains = [
        (rain_hbm.at[0, :, pl.ds(b * BLK, BLK)], rain_ref.at[pl.ds(b * pitch, steps)])
        for b in range(blocks)
    ]
    loads = copies(
        [(travel_hbm, travel_ref), (unit_hbm, unit_ref)] + rains
        + [(resp_hbm, resp_ref), (grad_hbm, grad_ref)], sems
    )
    devices = levels * basins
    lanes = ids_ref.shape[2]
    most = jnp.max(got_ref[basins:, CAP : CAP + 8, :], axis=0)[2:3, :]
    ids_ref[0] = jnp.broadcast_to(jnp.max(most, axis=1, keepdims=True), (8, lanes))
    outlets = basins * blocks
    halves = units_here // BLK
    level_id = where_ref[0]
    basin_id = where_ref[1]
    padded_ref[steps:, :] = jnp.zeros((steps, lanes), F32)
    back = [None]
    for l in range(1, levels):
        first = l * basins
        data = got_ref[first : first + basins, :CAP, :].reshape(basins * CAP, BLK)
        turned = jnp.transpose(data)
        labels = jnp.concatenate(
            [
                jnp.sum(got_ref[first : first + basins, CAP + 8 * g : CAP + 8 * g + 8, :], axis=0)
                for g in range((got_ref.shape[1] - CAP) // 8)
            ],
            axis=1,
        )[:, : basins * CAP]
        slot_of = (
            jnp.broadcast_to(labels[0:1], (lanes, basins * CAP))
            == iota((lanes, basins * CAP), 0).astype(F32) + 1.0
        ).astype(BF16)
        dense = pick(turned, slot_of, NT)
        back.append(dense[:steps])
        weight_ref[l] = dense[steps:]
        ids_ref[l] = mm(labels.astype(BF16), slot_of, NT)
    returned = back[levels - 1]
    mine = jnp.where(level_id == levels - 2, returned, 0.0)
    for l in range(levels - 2, 0, -1):
        member = (
            iota((lanes, lanes), 0).astype(F32) + 1.0
            == jnp.broadcast_to(ids_ref[l, 1:2, :], (lanes, lanes))
        ).astype(BF16)
        padded_ref[:steps, :] = pick(returned, member, NN)
        returned = back[l] + lag_sum(steps, weight_ref, l, padded_ref, False)
        mine = mine + jnp.where(level_id == l - 1, returned, 0.0)
    own = (iota((8, lanes), 1) == iota((8, lanes), 0) + basin_id * blocks).astype(BF16)
    if steps < BLK:
        mine = jnp.concatenate([mine, jnp.zeros((BLK - steps, lanes), F32)], axis=0)
    mine = pick_right(own, mine, NT)
    loads[0].wait()
    loads[1].wait()
    _, _, coef_keep = coefficients(travel_ref[...])
    unit_row = unit_ref[...] // BLK
    low = unit_ref[...] - unit_row * BLK
    places = (iota((BLK, reaches), 0) == jnp.broadcast_to(low, (BLK, reaches))).astype(BF16)
    owned = devices * halves
    at = iota((2 * owned, devices * 8), 0)
    kind = at // owned
    inside = at - kind * owned
    line = inside // halves * 8 + 4 + kind * halves + inside % halves
    compact = (iota((2 * owned, devices * 8), 1) == line).astype(BF16)
    table = got_ref[:, CAP : CAP + 8, :].reshape(devices * 8, BLK)
    spread = pick(pick_right(compact, table, NN), places, NN)
    row_at = iota((owned, reaches), 0) == jnp.broadcast_to(unit_row, (owned, reaches))
    fast_rate = jnp.sum(jnp.where(row_at, spread[:owned], 0.0), axis=0, keepdims=True)
    slow_rate = jnp.sum(jnp.where(row_at, spread[owned:], 0.0), axis=0, keepdims=True)
    fast_keep = jnp.exp(-fast_rate)
    slow_keep = jnp.exp(-slow_rate)
    for copy in loads[2 : 2 + blocks]:
        copy.wait()
    fast_by = stacked(fast_keep, blocks)
    slow_by = stacked(slow_keep, blocks)
    fast_gain = (1.0 - fast_by) * SPLIT_FAST
    slow_gain = (1.0 - slow_by) * (1.0 - SPLIT_FAST)
    zero = jnp.zeros((blocks, BLK), F32)
    fast, slow, fast_sens, slow_sens = zero, zero, zero, zero
    for step in range(steps):
        at = pl.ds(step, blocks, stride=pitch)
        rain = rain_ref[at, :]
        fast_sens = fast_by * fast_sens + (fast - SPLIT_FAST * rain)
        slow_sens = slow_by * slow_sens + (slow - (1.0 - SPLIT_FAST) * rain)
        fast = fast_by * fast + fast_gain * rain
        slow = slow_by * slow + slow_gain * rain
        lateral_ref[at, :] = fast + slow
        fast_ref[at, :] = fast_sens
        slow_ref[at, :] = slow_sens
    scale = 1.0 - coef_keep
    drives = []
    for b in range(blocks):
        drives.append(scale[:, b * BLK : (b + 1) * BLK] * lateral_ref[b * pitch : b * pitch + steps, :])
        drive_ref[b] = drives[b]
    loads[2 + blocks].wait()
    local = []
    for b in range(blocks):
        padded = jnp.concatenate(
            [drives[b], jnp.zeros((BLK - steps, BLK), F32)], axis=0
        )
        product = mm3(split2(resp_ref[b]), split2(padded), NT)
        skewed = pltpu.roll(product, 0, 1, stride=1, stride_axis=0)
        local.append(jnp.sum(skewed, axis=0, keepdims=True))
    loads[3 + blocks].wait()
    fast_sum = []
    slow_sum = []
    for b in range(blocks):
        spreadout = jnp.broadcast_to(mine[b : b + 1, :], (steps, BLK))
        at = iota((steps, BLK), 0)
        for bit in range(steps.bit_length() - 1):
            moved = pltpu.roll(spreadout, BLK - (1 << bit), 1)
            spreadout = jnp.where((at & (1 << bit)) != 0, moved, spreadout)
        resp = jnp.concatenate([resp_ref[b], jnp.zeros((BLK - steps, BLK), F32)], axis=0)
        grad = grad_ref[:, b * BLK : (b + 1) * BLK] + mm3(split2(spreadout), split2(resp), NN)
        side = slice(b * pitch, b * pitch + steps)
        fast_sum.append(jnp.sum(grad * fast_ref[side, :], axis=0, keepdims=True))
        slow_sum.append(jnp.sum(grad * slow_ref[side, :], axis=0, keepdims=True))
    fast_grad = -fast_keep * scale * jnp.concatenate(fast_sum, axis=1)
    slow_grad = -slow_keep * scale * jnp.concatenate(slow_sum, axis=1)
    terms = [
        jnp.where(row_at, jnp.broadcast_to(piece.astype(F32), (owned, reaches)), 0.0).astype(BF16)
        for pieces in zip(split3(fast_grad), split3(slow_grad))
        for piece in pieces
    ]
    parts = mm(jnp.concatenate(terms, axis=0), places, NT)
    summed = parts[: 2 * owned] + parts[2 * owned : 4 * owned] + parts[4 * owned :]
    at = iota((devices * 8, 2 * owned), 1)
    kind = at // owned
    inside = at - kind * owned
    line = inside // halves * 8 + 4 + kind * halves + inside % halves
    expand = (iota((devices * 8, 2 * owned), 0) == line).astype(BF16)
    send_ref[...] = pick_right(expand, summed, NN).reshape(devices, 8, BLK)
    half = blocks // 2
    for i in range(half):
        pair = jnp.concatenate([local[i][:, :steps], local[i + half][:, :steps]], axis=1)
        send_ref[:, i, :] = jnp.broadcast_to(pair, (devices, BLK))


def fetch_kernel(ids_ref, travel_hbm, src_hbm, move_hbm, *refs):
    move_refs = refs[:NEAR]
    coef_ref, source_ref, full_ref, travel_ref, src_ref, sems = refs[NEAR:]
    loads = copies(
        [(travel_hbm, travel_ref), (src_hbm, src_ref)]
        + [(move_hbm.at[k], move_refs[k]) for k in range(NEAR)], sems
    )
    full_ref[0] = jnp.max(ids_ref[0, 0:1, :]).astype(jnp.int32)
    loads[0].wait()
    loads[1].wait()
    coef_in, coef_prev, _ = coefficients(travel_ref[...])
    coef_ref[0:1, :] = coef_in
    coef_ref[1:2, :] = coef_prev
    lanes, reaches = source_ref.shape
    held = iota((lanes, reaches), 0) == jnp.broadcast_to(src_ref[...], (lanes, reaches))
    source_ref[...] = held.astype(BF16)
    for copy in loads[2:]:
        copy.wait()


def flows_kernel(where_ref, got_ref, coef_ref, source_ref, drive_ref, weight_ref, ids_ref, *refs,
                 levels, basins):
    near_refs = refs[:NEAR]
    move_hbm, flow_hbm, rate_hbm, far_ref, padded_ref, flow_ref, rate_ref, in_sems, out_sems = refs[NEAR:]
    blocks, steps, _ = drive_ref.shape
    far = move_hbm.shape[0] - NEAR
    loads = copies([(move_hbm.at[NEAR + k], far_ref.at[k]) for k in range(far)], in_sems)
    move_refs = [*near_refs] + [far_ref.at[k] for k in range(far)]
    reaches = blocks * BLK
    half = blocks // 2
    lanes = ids_ref.shape[2]
    level_id = where_ref[0]
    summed = jnp.sum(got_ref[...], axis=0)
    parts = rate_ref.shape[1] // BLK
    for k in range(2):
        for h in range(parts):
            at = 4 + k * parts + h
            rate_ref[k : k + 1, h * BLK : (h + 1) * BLK] = summed[at : at + 1]
    stores = [pltpu.make_async_copy(rate_ref, rate_hbm, out_sems.at[blocks])]
    stores[0].start()
    padded_ref[:steps, :] = jnp.zeros((steps, lanes), F32)
    rows = basins * 8
    row = iota((rows, lanes), 0)
    column = iota((rows, lanes), 1)
    inner = row % 8
    left = ((inner < half) & (column == (row // 8) * blocks + inner)).astype(BF16)
    right = ((inner < half) & (column == (row // 8) * blocks + inner + half)).astype(BF16)
    outlet = None
    chosen = jnp.zeros((steps, lanes), F32)
    for l in range(levels - 1):
        block = got_ref[l * basins : (l + 1) * basins].reshape(rows, BLK)
        block = jnp.where(iota((rows, BLK), 0) % 8 < half, block, 0.0)
        local = pick(block, left, TN)[:steps] + pick(block, right, TN)[steps:]
        if l == 0:
            outlet = local
        else:
            padded_ref[steps:, :] = outlet
            arriving = lag_sum(steps, weight_ref, l, padded_ref, True)
            member = (
                iota((lanes, lanes), 0).astype(F32) + 1.0
                == jnp.broadcast_to(ids_ref[l, 1:2, :], (lanes, lanes))
            ).astype(BF16)
            outlet = local + pick(arriving, member, NT)
        chosen = chosen + jnp.where(level_id == l + 1, outlet, 0.0)
    inflow = pick(chosen, source_ref[...], NN)
    driving = coef_ref[0:1, :] * inflow + coef_ref[1:2, :] * shift_down(inflow, 1)
    each = range(blocks)
    state = [
        mm3(split2(driving[:, b * BLK : (b + 1) * BLK] + drive_ref[b]), (move_refs[0][0, b], move_refs[0][1, b]), NN)
        for b in each
    ]
    for level in range(steps.bit_length() - 1):
        size = 1 << level
        for b in each:
            if b == 0 and level + 1 >= NEAR:
                loads[level + 1 - NEAR].wait()
            move = (move_refs[level + 1][0, b], move_refs[level + 1][1, b])
            if size < 8:
                state[b] = state[b] + mm3(split2(shift_down(state[b], size)), move, NN)
            else:
                out = mm3(split2(state[b][: steps - size]), move, NN)
                state[b] = jnp.concatenate([state[b][:size], state[b][size:] + out], axis=0)
    for b in each:
        flow_ref[:, b * BLK : (b + 1) * BLK] = state[b]
        side = pl.ds(b * BLK, BLK)
        copy = pltpu.make_async_copy(flow_ref.at[:, side], flow_hbm.at[0, :, side], out_sems.at[b])
        copy.start()
        stores.append(copy)
    for copy in stores:
        copy.wait()


def per_device(runoff, travel, downstream, inflow_src, reach_unit, rates, cotangent):
    _, steps, reaches = runoff.shape
    blocks = reaches // BLK
    levels = lax.axis_size("level")
    basins = lax.axis_size("basin")
    devices = levels * basins
    outlets = basins * blocks
    lanes = -(-outlets // BLK) * BLK
    units_here = rates.shape[1]
    halves = units_here // BLK
    count = steps.bit_length() - 1
    shape = jax.ShapeDtypeStruct
    smem = pl.BlockSpec(memory_space=pltpu.SMEM)
    vmem = pl.BlockSpec(memory_space=pltpu.VMEM)
    hbm = pl.BlockSpec(memory_space=pltpu.HBM)
    params = pltpu.CompilerParams(vmem_limit_bytes=VMEM_LIMIT)
    row_f32 = pltpu.VMEM((1, reaches), F32)
    row_i32 = pltpu.VMEM((1, reaches), jnp.int32)
    series = pltpu.VMEM((steps, reaches), F32)
    stack = pltpu.VMEM((blocks * (steps + 8), BLK), F32)
    answers = pltpu.VMEM((blocks, steps, BLK), F32)
    moves_shape = (count + 1, 2, blocks, BLK, BLK)
    height = CAP + 8 * (-(-basins * CAP // BLK))
    where = jnp.stack([lax.axis_index("level"), lax.axis_index("basin")]).astype(jnp.int32)
    packet, grad, resp, moves = pl.pallas_call(
        lambda *refs: blocks_kernel(*refs, basins=basins),
        out_shape=(
            shape((devices, height, BLK), F32),
            shape((steps, reaches), F32),
            shape((blocks, steps, BLK), F32),
            shape(moves_shape, BF16),
        ),
        in_specs=[smem] + [hbm] * 5,
        out_specs=(vmem, hbm, hbm, hbm),
        scratch_shapes=[
            row_f32, row_i32, row_i32, pltpu.VMEM(rates.shape, F32), series,
            series, answers, pltpu.VMEM(moves_shape, BF16),
            pltpu.SemaphoreType.DMA((5,)), pltpu.SemaphoreType.DMA((count + 3,)),
        ],
        compiler_params=params,
        name="blocks",
    )(where, *still(travel, downstream, inflow_src, rates, cotangent))
    got = lax.all_to_all(packet, LEVELS_AXES, 0, 0)

    def finish(got):
        sent, drive, weights, numbers = pl.pallas_call(
            lambda *refs: grads_kernel(*refs, levels=levels, basins=basins, units_here=units_here),
            out_shape=(
                shape((devices, 8, BLK), F32),
                shape((blocks, steps, BLK), F32),
                shape((levels, steps, lanes), F32),
                shape((levels, 8, lanes), F32),
            ),
            in_specs=[smem, vmem] + [hbm] * 5,
            out_specs=(vmem,) * 4,
            scratch_shapes=[row_f32, row_i32, stack, series, answers, stack, stack, stack,
                            pltpu.VMEM((2 * steps, lanes), F32), pltpu.SemaphoreType.DMA((blocks + 4,))],
            compiler_params=params,
            name="grads",
        )(where, got, *still(travel, reach_unit, runoff, grad, resp))
        swapped = lax.all_to_all(sent, LEVELS_AXES, 0, 0)
        *near_moves, coefs, source, full = pl.pallas_call(
            fetch_kernel,
            out_shape=(
                *[shape(moves_shape[1:], BF16)] * NEAR,
                shape((2, reaches), F32),
                shape((lanes, reaches), BF16),
                shape((1,), jnp.int32),
            ),
            in_specs=[vmem] + [hbm] * 3,
            out_specs=(vmem,) * (NEAR + 2) + (smem,),
            scratch_shapes=[row_f32, row_i32, pltpu.SemaphoreType.DMA((NEAR + 2,))],
            compiler_params=params,
            name="fetch",
        )(numbers, *still(travel, inflow_src, moves))
        near = lambda *values: [pltpu.with_memory_space_constraint(value, pltpu.VMEM) for value in values]
        flows, totals = pl.pallas_call(
            lambda *refs: flows_kernel(*refs, levels=levels, basins=basins),
            out_shape=(shape((1, steps, reaches), F32), shape((2, units_here), F32)),
            in_specs=[smem] + [vmem] * (6 + NEAR) + [hbm],
            out_specs=(hbm, hbm),
            scratch_shapes=[pltpu.VMEM((count + 1 - NEAR, *moves_shape[1:]), BF16),
                            pltpu.VMEM((2 * steps, lanes), F32), series,
                            pltpu.VMEM((2, units_here), F32),
                            pltpu.SemaphoreType.DMA((count + 1 - NEAR,)),
                            pltpu.SemaphoreType.DMA((blocks + 1,))],
            compiler_params=params,
            name="flows",
        )(where, swapped, *near(coefs, source), drive, weights, numbers, *near(*near_moves), *still(moves))
        return flows, totals, full[0]

    flows, totals, full = finish(got)
    flows, totals = lax.cond(
        full > CAP,
        lambda done: finish(spread_sources(got.shape, grad, resp, travel, inflow_src, rates))[:2],
        lambda done: done,
        (flows, totals),
    )
    return flows, totals


def spread_sources(packet_shape, grad, resp, travel, inflow_src, rates):
    values = (grad, resp, travel, inflow_src, rates)
    grad, resp, travel, inflow_src, rates = pl.pallas_call(
        relay_kernel,
        out_shape=tuple(jax.ShapeDtypeStruct(value.shape, value.dtype) for value in values),
        in_specs=[pl.BlockSpec(memory_space=pltpu.HBM)] * len(values),
        out_specs=(pl.BlockSpec(memory_space=pltpu.HBM),) * len(values),
        scratch_shapes=[pltpu.SemaphoreType.DMA((len(values),))],
        name="relay",
    )(*still(*values))
    blocks, steps, _ = resp.shape
    basins = lax.axis_size("basin")
    basin_id = lax.axis_index("basin")
    outlets = basins * blocks
    reaches = blocks * BLK
    coef_in, coef_prev, _ = coefficients(travel)
    answer = resp.transpose(1, 0, 2).reshape(steps, reaches)
    zero = jnp.zeros((1, reaches), F32)
    back = coef_in * grad + coef_prev * jnp.concatenate([grad[1:], zero], axis=0)
    ahead = coef_in * answer + coef_prev * jnp.concatenate([zero, answer[:-1]], axis=0)
    block_of = (jnp.arange(reaches) // BLK + 1 + basin_id * blocks).astype(F32)
    table = jnp.concatenate([back, ahead, jnp.broadcast_to(block_of[None], (BLK, reaches))], axis=0)
    chosen = (inflow_src == jnp.arange(outlets)[:, None]).astype(F32)
    mine = lax.dot_general(chosen, table, NT, precision=lax.Precision.HIGHEST)
    parts = lax.all_to_all(mine.reshape(basins, blocks, 2 * steps + BLK), "basin", 0, 0).sum(axis=0)
    width = (packet_shape[1] - CAP) // 8 * BLK
    place = jnp.arange(blocks) + basin_id * CAP
    onto = (jnp.arange(width)[None, :] == place[:, None]).astype(F32)
    slot_row = ((jnp.arange(blocks) + basin_id * blocks + 1).astype(F32)[:, None] * onto).sum(axis=0)
    block_row = (parts[:, 2 * steps : 2 * steps + 1] * onto).sum(axis=0)
    labels = jnp.concatenate(
        [slot_row[None], block_row[None], jnp.zeros((6, width), F32)], axis=0
    )
    rate_rows = rates.reshape(-1, BLK)
    labels = labels.at[4 : 4 + rate_rows.shape[0], :BLK].set(rate_rows)
    labels = labels.reshape(8, width // BLK, BLK).transpose(1, 0, 2).reshape(-1, BLK)
    packet = jnp.concatenate(
        [parts[:, : 2 * steps], jnp.zeros((CAP - blocks, 2 * steps), F32), labels], axis=0
    )
    return lax.all_to_all(jnp.broadcast_to(packet[None], packet_shape), LEVELS_AXES, 0, 0)


def solution(mesh):
    placed = (
        P("level", None, "basin"),
        P("level", "basin"),
        P("level", "basin"),
        P("level", "basin"),
        P("level", "basin"),
        P(None, ("level", "basin")),
        P("level", None, "basin"),
    )
    return jax.shard_map(
        per_device,
        mesh=mesh,
        in_specs=placed,
        out_specs=(P("level", None, "basin"), P(None, ("level", "basin"))),
        check_vma=False,
    )
```

```python
import jax
import jax.numpy as jnp
from jax import lax
from jax.experimental import pallas as pl
from jax.experimental.pallas import tpu as pltpu
from jax.sharding import PartitionSpec as P

BLK = 128
SPLIT_FAST = 0.6
MUSK_X = 0.2
BASIN_AXES = ("column", "core")
LEVELS_AXES = ("level", "column", "core")
F32 = jnp.float32
BF16 = jnp.bfloat16
NN = (((1,), (0,)), ((), ()))
NT = (((1,), (1,)), ((), ()))
TN = (((0,), (0,)), ((), ()))
VMEM_LIMIT = 48 << 20
CAP = 16
NEAR = 5


def mm(left, right, dims):
    return lax.dot_general(left, right, dims, preferred_element_type=F32)


def split2(value):
    high = value.astype(BF16)
    return high, (value - high.astype(F32)).astype(BF16)


def split3(value):
    high = value.astype(BF16)
    rest = value - high.astype(F32)
    mid = rest.astype(BF16)
    return high, mid, (rest - mid.astype(F32)).astype(BF16)


def beside(*parts):
    return jnp.concatenate(parts, axis=1)


def above(*parts):
    return jnp.concatenate(parts, axis=0)


def folded(product):
    half = product.shape[1] // 2
    return product[:, :half] + product[:, half:]


def mm3(left, right, dims):
    high, low = right[0], right[1]
    empty = jnp.zeros_like(high)
    wide = beside(left[0], left[1])
    if dims == NT:
        return folded(mm(wide, above(beside(high, high), beside(low, empty)), NT))
    return folded(mm(wide, above(beside(high, low), beside(high, empty)), NN))


def mm6(left, right):
    high, mid, low = right
    first = mm(beside(left[0], left[1]), above(beside(high, mid), beside(high, mid)), NN)
    return folded(first) + mm(beside(left[0], left[2]), above(low, high), NN)


def pick(value, onehot, dims):
    high, mid, low = split3(value)
    if dims == TN:
        return mm(high, onehot, TN) + mm(mid, onehot, TN) + mm(low, onehot, TN)
    if dims == NT:
        both = beside(onehot, onehot)
    else:
        both = above(onehot, onehot)
    return mm(beside(high, mid), both, dims) + mm(low, onehot, dims)


def pick_right(onehot, value, dims):
    high, mid, low = split3(value)
    empty = jnp.zeros_like(low)
    wide = beside(onehot, onehot)
    if dims == NT:
        return folded(mm(wide, above(beside(high, mid), beside(low, empty)), NT))
    return folded(mm(wide, above(beside(high, low), beside(mid, empty)), NN))


def iota(shape, axis):
    return lax.broadcasted_iota(jnp.int32, shape, axis)


def coefficients(travel):
    twokx = 2.0 * travel * MUSK_X
    denom = 2.0 * travel * (1.0 - MUSK_X) + 1.0
    coef_in = (1.0 - twokx) / denom
    coef_prev = (1.0 + twokx) / denom
    coef_keep = (2.0 * travel * (1.0 - MUSK_X) - 1.0) / denom
    return coef_in, coef_prev, coef_keep


def shift_up(value, steps):
    rows = value.shape[0]
    if steps % 8 == 0:
        return jnp.concatenate([value[steps:], jnp.zeros((steps, value.shape[1]), F32)], axis=0)
    moved = pltpu.roll(value, rows - steps, 0)
    return jnp.where(iota(value.shape, 0) < rows - steps, moved, 0.0)


def shift_down(value, steps):
    rows = value.shape[0]
    if steps % 8 == 0:
        return jnp.concatenate(
            [jnp.zeros((steps, value.shape[1]), F32), value[: rows - steps]], axis=0
        )
    moved = pltpu.roll(value, steps, 0)
    return jnp.where(iota(value.shape, 0) >= steps, moved, 0.0)


def copies(pairs, sems):
    started = []
    for at, (source, target) in enumerate(pairs):
        copy = pltpu.make_async_copy(source, target, sems.at[at])
        copy.start()
        started.append(copy)
    return started


def stacked(row, blocks):
    return jnp.concatenate([row[:, b * BLK : (b + 1) * BLK] for b in range(blocks)], axis=0)


def still(*values):
    return [pltpu.with_memory_space_constraint(value, pltpu.HBM) for value in values]


def label_lane(basin_id, basins):
    column = basin_id // 2
    return ((basin_id - 2 * column) * (basins // 2) + column) * CAP


def relay_kernel(*refs):
    half = len(refs) // 2
    for copy in copies(list(zip(refs[:half], refs[half:-1])), refs[-1]):
        copy.wait()


def blocks_kernel(where_ref, travel_hbm, down_hbm, src_hbm, rates_hbm, cot_hbm,
                  packet_ref, grad_hbm, resp_hbm, move_hbm,
                  travel_ref, down_ref, src_ref, rates_ref, cot_ref,
                  grad_ref, resp_ref, move_ref, in_sems, out_sems, *, basins):
    steps, reaches = cot_ref.shape
    blocks = reaches // BLK
    copies_out, height, _ = packet_ref.shape
    width = (height - CAP) // 8 * BLK
    each = range(blocks)
    loads = copies(
        [(travel_hbm, travel_ref), (down_hbm, down_ref), (src_hbm, src_ref),
         (rates_hbm, rates_ref), (cot_hbm.at[0], cot_ref)], in_sems
    )
    for copy in loads[:4]:
        copy.wait()
    coef_in, coef_prev, coef_keep = coefficients(travel_ref[...])
    eye_mask = iota((BLK, BLK), 0) == iota((BLK, BLK), 1)
    eye = eye_mask.astype(F32)

    def part(row, b):
        return row[:, b * BLK : (b + 1) * BLK]

    downs = stacked(down_ref[...].astype(F32), blocks)
    columns = mm(eye.astype(BF16), downs.astype(BF16), NT)
    place = iota((BLK, BLK), 1).astype(F32)
    turned = [
        pick_right(eye.astype(BF16), stacked(row, blocks), NT)
        for row in (coef_in, coef_prev, coef_keep)
    ]
    linked = [jnp.broadcast_to(columns[:, b : b + 1], (BLK, BLK)) == place for b in each]
    base = [jnp.where(linked[b], part(coef_in, b), 0.0) for b in each]
    hops = [linked[b].astype(BF16) for b in each]
    total = [eye + base[b] for b in each]
    power = base
    for level in range(1, 8):
        for b in each:
            if level == 1:
                joined = power[b]
            elif level == 7:
                joined = total[b]
            else:
                joined = jnp.concatenate([power[b], total[b]], axis=1)
            if level <= 3:
                scale = jnp.sum(power[b], axis=1, keepdims=True)
                product = scale * pick_right(hops[b], joined, NN)
            else:
                product = mm(power[b].astype(BF16), joined.astype(BF16), NN)
            if level <= 2:
                hops[b] = mm(hops[b], hops[b], NN).astype(BF16)
            if level == 1:
                power[b] = product
            elif level == 7:
                total[b] = total[b] + product
            else:
                power[b] = product[:, :BLK]
                total[b] = total[b] + product[:, BLK:]
    inverse = [split2(total[b]) for b in each]
    stores = []

    def publish(at, moves):
        for b in each:
            move_ref[at, 0, b] = moves[b][0]
            move_ref[at, 1, b] = moves[b][1]
        copy = pltpu.make_async_copy(move_ref.at[at], move_hbm.at[at], out_sems.at[at])
        copy.start()
        stores.append(copy)

    publish(0, inverse)
    following = [
        pick_right(linked[b].astype(BF16), turned[1][:, b : b + 1] * total[b], NN)
        + turned[2][:, b : b + 1] * total[b]
        for b in each
    ]
    moves = [split3(following[b]) for b in each]
    loads[4].wait()
    state = [cot_ref[:, b * BLK : (b + 1) * BLK] for b in each]
    unit = jnp.where((iota((8, BLK), 0) == 0) & (iota((8, BLK), 1) == BLK - 1), 1.0, 0.0)
    rows = [unit for b in each]
    count = steps.bit_length() - 1
    for level in range(count):
        size = 1 << level
        publish(level + 1, moves)
        keep = steps - size
        for b in each:
            if size < 8:
                left = jnp.concatenate([shift_up(state[b], size), shift_down(rows[b], size)], axis=0)
                out = mm3(split2(left), moves[b], NT)
                state[b] = state[b] + out[:steps]
                rows[b] = rows[b] + out[steps:]
            else:
                left = jnp.concatenate([state[b][size:], rows[b]], axis=0)
                out = mm3(split2(left), moves[b], NT)
                state[b] = jnp.concatenate(
                    [state[b][:keep] + out[:keep], state[b][keep:]], axis=0
                )
                rows[b] = jnp.concatenate([rows[b], out[keep:]], axis=0)
        if level + 1 < count:
            if level < 2:
                moves = [split3(mm6(moves[b], moves[b])) for b in each]
            else:
                moves = [split2(mm3(moves[b], moves[b], NN)) for b in each]
    sources = stacked(src_ref[...], blocks)
    held = sources >= 0
    upper = (iota((BLK, BLK), 0) <= iota((BLK, BLK), 1)).astype(BF16)
    ranks = mm(held.astype(BF16), upper, NN)
    basin_id = where_ref[1]
    first_lane = label_lane(basin_id, basins)
    offset = jnp.zeros((1, 1), F32)
    packed = jnp.zeros((CAP, 2 * steps), F32)
    labels = jnp.zeros((8, width), F32)
    responses = []
    for b in each:
        both = mm3(split2(jnp.concatenate([state[b], rows[b]], axis=0)), inverse[b], NT)
        grad_ref[:, b * BLK : (b + 1) * BLK] = both[:steps]
        resp_ref[b] = both[steps:]
        responses.append(both)
    for copy in copies([(grad_ref, grad_hbm), (resp_ref, resp_hbm)], out_sems.at[pl.ds(count + 1, 2)]):
        stores.append(copy)
    for b in each:
        rank = jnp.where(held[b : b + 1], ranks[b : b + 1] + offset, 0.0)
        offset = offset + ranks[b : b + 1, BLK - 1 : BLK]
        row_at = iota((CAP, BLK), 0).astype(F32) + 1.0
        chosen = (jnp.broadcast_to(rank, (CAP, BLK)) == row_at).astype(BF16)
        grad = responses[b][:steps]
        resp = responses[b][steps:]
        now = part(coef_in, b)
        before = part(coef_prev, b)
        sent = jnp.concatenate(
            [now * grad + before * shift_up(grad, 1), now * resp + before * shift_down(resp, 1)],
            axis=0,
        )
        packed = packed + pick_right(chosen, sent, NT)
        lane_at = iota((width, BLK), 0) - first_lane
        wide = (
            (jnp.broadcast_to(rank, (width, BLK)) == lane_at.astype(F32) + 1.0) & (lane_at < CAP)
        ).astype(BF16)
        which = jnp.broadcast_to((sources[b : b + 1] + 1).astype(F32), (8, BLK))
        block_at = (basin_id * blocks + (b + 1)).astype(F32)
        values = jnp.where(iota((8, BLK), 0) == 0, which, block_at)
        labels = labels + mm(values.astype(BF16), wide, NT)
    labels = jnp.where(iota((8, width), 0) == 2, jnp.broadcast_to(offset, (8, width)), labels)
    parts = rates_ref.shape[1] // BLK
    rate_rows = [rates_ref[k : k + 1, h * BLK : (h + 1) * BLK] for k in range(2) for h in range(parts)]
    for group in range(width // BLK):
        rows_here = labels[:4, group * BLK : (group + 1) * BLK]
        first = CAP + 8 * group
        if group == 0:
            tail = rate_rows + [jnp.zeros((1, BLK), F32)] * (4 - len(rate_rows))
        else:
            tail = [jnp.zeros((4, BLK), F32)]
        piece = jnp.concatenate([rows_here] + tail, axis=0)
        packet_ref[:, first : first + 8, :] = jnp.broadcast_to(piece[None], (copies_out, 8, BLK))
    packet_ref[:, :CAP, :] = jnp.broadcast_to(packed[None], (copies_out, CAP, BLK))
    for copy in stores:
        copy.wait()


def lag_sum(steps, weight_ref, level, padded_ref, forward):
    tiles = steps // 8
    total = [jnp.zeros((8, padded_ref.shape[1]), F32)] * tiles
    for lag in range(steps):
        weight = weight_ref[level, lag : lag + 1, :]
        if forward:
            first, last = lag // 8, tiles
            start = steps - lag + 8 * first
        else:
            first, last = 0, tiles - lag // 8
            start = lag
        shifted = padded_ref[start : start + 8 * (last - first), :]
        for at in range(first, last):
            total[at] = total[at] + weight * shifted[8 * (at - first) : 8 * (at - first) + 8]
    return jnp.concatenate(total, axis=0)


def grads_kernel(where_ref, own_ref, other_ref, travel_hbm, unit_hbm, rain_hbm, grad_hbm, resp_hbm,
                 send_ref, drive_ref, weight_ref, ids_ref,
                 travel_ref, unit_ref, rain_ref, grad_ref, resp_ref,
                 lateral_ref, fast_ref, slow_ref, padded_ref, sems, *, levels, basins, units_here):
    steps, reaches = grad_ref.shape
    blocks = reaches // BLK
    pitch = steps + 8
    rains = [
        (rain_hbm.at[0, :, pl.ds(b * BLK, BLK)], rain_ref.at[pl.ds(b * pitch, steps)])
        for b in range(blocks)
    ]
    loads = copies(
        [(travel_hbm, travel_ref), (unit_hbm, unit_ref)] + rains
        + [(resp_hbm, resp_ref), (grad_hbm, grad_ref)], sems
    )
    devices = levels * basins
    lanes = ids_ref.shape[2]
    columns = basins // 2
    core = where_ref[2]
    most = jnp.max(
        jnp.maximum(own_ref[columns:, CAP : CAP + 8, :], other_ref[columns:, CAP : CAP + 8, :]), axis=0
    )[2:3, :]
    ids_ref[0] = jnp.broadcast_to(jnp.max(most, axis=1, keepdims=True), (8, lanes))
    outlets = basins * blocks
    halves = units_here // BLK
    level_id = where_ref[0]
    basin_id = where_ref[1]
    padded_ref[steps:, :] = jnp.zeros((steps, lanes), F32)
    back = [None]
    for l in range(1, levels):
        group = slice(l * columns, (l + 1) * columns)
        data = jnp.concatenate(
            [ref[group, :CAP, :].reshape(columns * CAP, BLK) for ref in (own_ref, other_ref)], axis=0
        )
        turned = jnp.transpose(data)
        labels = jnp.concatenate(
            [
                jnp.sum(
                    own_ref[group, CAP + 8 * g : CAP + 8 * g + 8, :]
                    + other_ref[group, CAP + 8 * g : CAP + 8 * g + 8, :],
                    axis=0,
                )
                for g in range((own_ref.shape[1] - CAP) // 8)
            ],
            axis=1,
        )[:, : basins * CAP]
        labels = jnp.where(core == 1, pltpu.roll(labels, columns * CAP, 1), labels)
        slot_of = (
            jnp.broadcast_to(labels[0:1], (lanes, basins * CAP))
            == iota((lanes, basins * CAP), 0).astype(F32) + 1.0
        ).astype(BF16)
        dense = pick(turned, slot_of, NT)
        back.append(dense[:steps])
        weight_ref[l] = dense[steps:]
        ids_ref[l] = mm(labels.astype(BF16), slot_of, NT)
    returned = back[levels - 1]
    mine = jnp.where(level_id == levels - 2, returned, 0.0)
    for l in range(levels - 2, 0, -1):
        member = (
            iota((lanes, lanes), 0).astype(F32) + 1.0
            == jnp.broadcast_to(ids_ref[l, 1:2, :], (lanes, lanes))
        ).astype(BF16)
        padded_ref[:steps, :] = pick(returned, member, NN)
        returned = back[l] + lag_sum(steps, weight_ref, l, padded_ref, False)
        mine = mine + jnp.where(level_id == l - 1, returned, 0.0)
    own = (iota((8, lanes), 1) == iota((8, lanes), 0) + basin_id * blocks).astype(BF16)
    if steps < BLK:
        mine = jnp.concatenate([mine, jnp.zeros((BLK - steps, lanes), F32)], axis=0)
    mine = pick_right(own, mine, NT)
    loads[0].wait()
    loads[1].wait()
    _, _, coef_keep = coefficients(travel_ref[...])
    unit_row = unit_ref[...] // BLK
    low = unit_ref[...] - unit_row * BLK
    places = (iota((BLK, reaches), 0) == jnp.broadcast_to(low, (BLK, reaches))).astype(BF16)
    owned = devices * halves
    at = iota((2 * owned, devices * 8), 0)
    kind = at // owned
    inside = at - kind * owned
    owner = inside // halves
    line = owner // 2 * 8 + 4 + kind * halves + inside % halves
    line = line + (owner + core) % 2 * (devices * 4)
    compact = (iota((2 * owned, devices * 8), 1) == line).astype(BF16)
    table = jnp.concatenate(
        [ref[:, CAP : CAP + 8, :].reshape(devices * 4, BLK) for ref in (own_ref, other_ref)], axis=0
    )
    spread = pick(pick_right(compact, table, NN), places, NN)
    row_at = iota((owned, reaches), 0) == jnp.broadcast_to(unit_row, (owned, reaches))
    fast_rate = jnp.sum(jnp.where(row_at, spread[:owned], 0.0), axis=0, keepdims=True)
    slow_rate = jnp.sum(jnp.where(row_at, spread[owned:], 0.0), axis=0, keepdims=True)
    fast_keep = jnp.exp(-fast_rate)
    slow_keep = jnp.exp(-slow_rate)
    for copy in loads[2 : 2 + blocks]:
        copy.wait()
    fast_by = stacked(fast_keep, blocks)
    slow_by = stacked(slow_keep, blocks)
    fast_gain = (1.0 - fast_by) * SPLIT_FAST
    slow_gain = (1.0 - slow_by) * (1.0 - SPLIT_FAST)
    zero = jnp.zeros((blocks, BLK), F32)
    fast, slow, fast_sens, slow_sens = zero, zero, zero, zero
    for step in range(steps):
        at = pl.ds(step, blocks, stride=pitch)
        rain = rain_ref[at, :]
        fast_sens = fast_by * fast_sens + (fast - SPLIT_FAST * rain)
        slow_sens = slow_by * slow_sens + (slow - (1.0 - SPLIT_FAST) * rain)
        fast = fast_by * fast + fast_gain * rain
        slow = slow_by * slow + slow_gain * rain
        lateral_ref[at, :] = fast + slow
        fast_ref[at, :] = fast_sens
        slow_ref[at, :] = slow_sens
    scale = 1.0 - coef_keep
    drives = []
    for b in range(blocks):
        drives.append(scale[:, b * BLK : (b + 1) * BLK] * lateral_ref[b * pitch : b * pitch + steps, :])
        drive_ref[b] = drives[b]
    loads[2 + blocks].wait()
    local = []
    for b in range(blocks):
        padded = jnp.concatenate(
            [drives[b], jnp.zeros((BLK - steps, BLK), F32)], axis=0
        )
        product = mm3(split2(resp_ref[b]), split2(padded), NT)
        skewed = pltpu.roll(product, 0, 1, stride=1, stride_axis=0)
        local.append(jnp.sum(skewed, axis=0, keepdims=True))
    loads[3 + blocks].wait()
    fast_sum = []
    slow_sum = []
    for b in range(blocks):
        spreadout = jnp.broadcast_to(mine[b : b + 1, :], (steps, BLK))
        at = iota((steps, BLK), 0)
        for bit in range(steps.bit_length() - 1):
            moved = pltpu.roll(spreadout, BLK - (1 << bit), 1)
            spreadout = jnp.where((at & (1 << bit)) != 0, moved, spreadout)
        resp = jnp.concatenate([resp_ref[b], jnp.zeros((BLK - steps, BLK), F32)], axis=0)
        grad = grad_ref[:, b * BLK : (b + 1) * BLK] + mm3(split2(spreadout), split2(resp), NN)
        side = slice(b * pitch, b * pitch + steps)
        fast_sum.append(jnp.sum(grad * fast_ref[side, :], axis=0, keepdims=True))
        slow_sum.append(jnp.sum(grad * slow_ref[side, :], axis=0, keepdims=True))
    fast_grad = -fast_keep * scale * jnp.concatenate(fast_sum, axis=1)
    slow_grad = -slow_keep * scale * jnp.concatenate(slow_sum, axis=1)
    terms = [
        jnp.where(row_at, jnp.broadcast_to(piece.astype(F32), (owned, reaches)), 0.0).astype(BF16)
        for pieces in zip(split3(fast_grad), split3(slow_grad))
        for piece in pieces
    ]
    parts = mm(jnp.concatenate(terms, axis=0), places, NT)
    summed = parts[: 2 * owned] + parts[2 * owned : 4 * owned] + parts[4 * owned :]
    at = iota((devices * 8, 2 * owned), 1)
    kind = at // owned
    inside = at - kind * owned
    line = inside // halves * 8 + 4 + kind * halves + inside % halves
    expand = (iota((devices * 8, 2 * owned), 0) == line).astype(BF16)
    send_ref[...] = pick_right(expand, summed, NN).reshape(devices, 8, BLK)
    half = blocks // 2
    for i in range(half):
        pair = jnp.concatenate([local[i][:, :steps], local[i + half][:, :steps]], axis=1)
        send_ref[:, i, :] = jnp.broadcast_to(pair, (devices, BLK))


def fetch_kernel(ids_ref, travel_hbm, src_hbm, move_hbm, *refs):
    move_refs = refs[:NEAR]
    coef_ref, source_ref, full_ref, travel_ref, src_ref, sems = refs[NEAR:]
    loads = copies(
        [(travel_hbm, travel_ref), (src_hbm, src_ref)]
        + [(move_hbm.at[k], move_refs[k]) for k in range(NEAR)], sems
    )
    full_ref[0] = jnp.max(ids_ref[0, 0:1, :]).astype(jnp.int32)
    loads[0].wait()
    loads[1].wait()
    coef_in, coef_prev, _ = coefficients(travel_ref[...])
    coef_ref[0:1, :] = coef_in
    coef_ref[1:2, :] = coef_prev
    lanes, reaches = source_ref.shape
    held = iota((lanes, reaches), 0) == jnp.broadcast_to(src_ref[...], (lanes, reaches))
    source_ref[...] = held.astype(BF16)
    for copy in loads[2:]:
        copy.wait()


def flows_kernel(where_ref, got_ref, coef_ref, source_ref, drive_ref, weight_ref, ids_ref, *refs,
                 levels, basins):
    near_refs = refs[:NEAR]
    move_hbm, flow_hbm, rate_hbm, far_ref, padded_ref, flow_ref, rate_ref, in_sems, out_sems = refs[NEAR:]
    blocks, steps, _ = drive_ref.shape
    far = move_hbm.shape[0] - NEAR
    loads = copies([(move_hbm.at[NEAR + k], far_ref.at[k]) for k in range(far)], in_sems)
    move_refs = [*near_refs] + [far_ref.at[k] for k in range(far)]
    reaches = blocks * BLK
    half = blocks // 2
    lanes = ids_ref.shape[2]
    level_id = where_ref[0]
    summed = jnp.sum(got_ref[...], axis=0)
    parts = rate_ref.shape[1] // BLK
    for k in range(2):
        for h in range(parts):
            at = 4 + k * parts + h
            rate_ref[k : k + 1, h * BLK : (h + 1) * BLK] = summed[at : at + 1]
    stores = [pltpu.make_async_copy(rate_ref, rate_hbm, out_sems.at[blocks])]
    stores[0].start()
    padded_ref[:steps, :] = jnp.zeros((steps, lanes), F32)
    rows = basins * 8
    row = iota((rows, lanes), 0)
    column = iota((rows, lanes), 1)
    inner = row % 8
    left = ((inner < half) & (column == (row // 8) * blocks + inner)).astype(BF16)
    right = ((inner < half) & (column == (row // 8) * blocks + inner + half)).astype(BF16)
    outlet = None
    chosen = jnp.zeros((steps, lanes), F32)
    for l in range(levels - 1):
        block = got_ref[l * basins : (l + 1) * basins].reshape(rows, BLK)
        block = jnp.where(iota((rows, BLK), 0) % 8 < half, block, 0.0)
        local = pick(block, left, TN)[:steps] + pick(block, right, TN)[steps:]
        if l == 0:
            outlet = local
        else:
            padded_ref[steps:, :] = outlet
            arriving = lag_sum(steps, weight_ref, l, padded_ref, True)
            member = (
                iota((lanes, lanes), 0).astype(F32) + 1.0
                == jnp.broadcast_to(ids_ref[l, 1:2, :], (lanes, lanes))
            ).astype(BF16)
            outlet = local + pick(arriving, member, NT)
        chosen = chosen + jnp.where(level_id == l + 1, outlet, 0.0)
    inflow = pick(chosen, source_ref[...], NN)
    driving = coef_ref[0:1, :] * inflow + coef_ref[1:2, :] * shift_down(inflow, 1)
    each = range(blocks)
    state = [
        mm3(split2(driving[:, b * BLK : (b + 1) * BLK] + drive_ref[b]), (move_refs[0][0, b], move_refs[0][1, b]), NN)
        for b in each
    ]
    for level in range(steps.bit_length() - 1):
        size = 1 << level
        for b in each:
            if b == 0 and level + 1 >= NEAR:
                loads[level + 1 - NEAR].wait()
            move = (move_refs[level + 1][0, b], move_refs[level + 1][1, b])
            if size < 8:
                state[b] = state[b] + mm3(split2(shift_down(state[b], size)), move, NN)
            else:
                out = mm3(split2(state[b][: steps - size]), move, NN)
                state[b] = jnp.concatenate([state[b][:size], state[b][size:] + out], axis=0)
    for b in each:
        flow_ref[:, b * BLK : (b + 1) * BLK] = state[b]
        side = pl.ds(b * BLK, BLK)
        copy = pltpu.make_async_copy(flow_ref.at[:, side], flow_hbm.at[0, :, side], out_sems.at[b])
        copy.start()
        stores.append(copy)
    for copy in stores:
        copy.wait()


def per_device(runoff, travel, downstream, inflow_src, reach_unit, rates, cotangent):
    _, steps, reaches = runoff.shape
    blocks = reaches // BLK
    levels = lax.axis_size("level")
    basins = lax.axis_size("column") * lax.axis_size("core")
    devices = levels * basins
    outlets = basins * blocks
    lanes = -(-outlets // BLK) * BLK
    units_here = rates.shape[1]
    halves = units_here // BLK
    count = steps.bit_length() - 1
    shape = jax.ShapeDtypeStruct
    smem = pl.BlockSpec(memory_space=pltpu.SMEM)
    vmem = pl.BlockSpec(memory_space=pltpu.VMEM)
    hbm = pl.BlockSpec(memory_space=pltpu.HBM)
    params = pltpu.CompilerParams(vmem_limit_bytes=VMEM_LIMIT)
    row_f32 = pltpu.VMEM((1, reaches), F32)
    row_i32 = pltpu.VMEM((1, reaches), jnp.int32)
    series = pltpu.VMEM((steps, reaches), F32)
    stack = pltpu.VMEM((blocks * (steps + 8), BLK), F32)
    answers = pltpu.VMEM((blocks, steps, BLK), F32)
    moves_shape = (count + 1, 2, blocks, BLK, BLK)
    height = CAP + 8 * (-(-basins * CAP // BLK))
    where = jnp.stack(
        [lax.axis_index("level"), lax.axis_index(BASIN_AXES), lax.axis_index("core")]
    ).astype(jnp.int32)
    packet, grad, resp, moves = pl.pallas_call(
        lambda *refs: blocks_kernel(*refs, basins=basins),
        out_shape=(
            shape((devices // 2, height, BLK), F32),
            shape((steps, reaches), F32),
            shape((blocks, steps, BLK), F32),
            shape(moves_shape, BF16),
        ),
        in_specs=[smem] + [hbm] * 5,
        out_specs=(vmem, hbm, hbm, hbm),
        scratch_shapes=[
            row_f32, row_i32, row_i32, pltpu.VMEM(rates.shape, F32), series,
            series, answers, pltpu.VMEM(moves_shape, BF16),
            pltpu.SemaphoreType.DMA((5,)), pltpu.SemaphoreType.DMA((count + 3,)),
        ],
        compiler_params=params,
        name="blocks",
    )(where, *still(travel, downstream, inflow_src, rates, cotangent))
    got = exchange(packet)

    def finish(got):
        sent, drive, weights, numbers = pl.pallas_call(
            lambda *refs: grads_kernel(*refs, levels=levels, basins=basins, units_here=units_here),
            out_shape=(
                shape((devices, 8, BLK), F32),
                shape((blocks, steps, BLK), F32),
                shape((levels, steps, lanes), F32),
                shape((levels, 8, lanes), F32),
            ),
            in_specs=[smem, vmem, vmem] + [hbm] * 5,
            out_specs=(vmem,) * 4,
            scratch_shapes=[row_f32, row_i32, stack, series, answers, stack, stack, stack,
                            pltpu.VMEM((2 * steps, lanes), F32), pltpu.SemaphoreType.DMA((blocks + 4,))],
            compiler_params=params,
            name="grads",
        )(where, *got, *still(travel, reach_unit, runoff, grad, resp))
        swapped = lax.all_to_all(sent, LEVELS_AXES, 0, 0)
        *near_moves, coefs, source, full = pl.pallas_call(
            fetch_kernel,
            out_shape=(
                *[shape(moves_shape[1:], BF16)] * NEAR,
                shape((2, reaches), F32),
                shape((lanes, reaches), BF16),
                shape((1,), jnp.int32),
            ),
            in_specs=[vmem] + [hbm] * 3,
            out_specs=(vmem,) * (NEAR + 2) + (smem,),
            scratch_shapes=[row_f32, row_i32, pltpu.SemaphoreType.DMA((NEAR + 2,))],
            compiler_params=params,
            name="fetch",
        )(numbers, *still(travel, inflow_src, moves))
        near = lambda *values: [pltpu.with_memory_space_constraint(value, pltpu.VMEM) for value in values]
        flows, totals = pl.pallas_call(
            lambda *refs: flows_kernel(*refs, levels=levels, basins=basins),
            out_shape=(shape((1, steps, reaches), F32), shape((2, units_here), F32)),
            in_specs=[smem] + [vmem] * (6 + NEAR) + [hbm],
            out_specs=(hbm, hbm),
            scratch_shapes=[pltpu.VMEM((count + 1 - NEAR, *moves_shape[1:]), BF16),
                            pltpu.VMEM((2 * steps, lanes), F32), series,
                            pltpu.VMEM((2, units_here), F32),
                            pltpu.SemaphoreType.DMA((count + 1 - NEAR,)),
                            pltpu.SemaphoreType.DMA((blocks + 1,))],
            compiler_params=params,
            name="flows",
        )(where, swapped, *near(coefs, source), drive, weights, numbers, *near(*near_moves), *still(moves))
        return flows, totals, full[0]

    flows, totals, full = finish(got)
    flows, totals = lax.cond(
        full > CAP,
        lambda done: finish(spread_sources(packet.shape, grad, resp, travel, inflow_src, rates))[:2],
        lambda done: done,
        (flows, totals),
    )
    return flows, totals


def exchange(packet):
    own = lax.all_to_all(packet, ("level", "column"), 0, 0)
    return own, lax.ppermute(own, "core", [(0, 1), (1, 0)])


def spread_sources(packet_shape, grad, resp, travel, inflow_src, rates):
    values = (grad, resp, travel, inflow_src, rates)
    grad, resp, travel, inflow_src, rates = pl.pallas_call(
        relay_kernel,
        out_shape=tuple(jax.ShapeDtypeStruct(value.shape, value.dtype) for value in values),
        in_specs=[pl.BlockSpec(memory_space=pltpu.HBM)] * len(values),
        out_specs=(pl.BlockSpec(memory_space=pltpu.HBM),) * len(values),
        scratch_shapes=[pltpu.SemaphoreType.DMA((len(values),))],
        name="relay",
    )(*still(*values))
    blocks, steps, _ = resp.shape
    basins = lax.axis_size("column") * lax.axis_size("core")
    basin_id = lax.axis_index(BASIN_AXES)
    outlets = basins * blocks
    reaches = blocks * BLK
    coef_in, coef_prev, _ = coefficients(travel)
    answer = resp.transpose(1, 0, 2).reshape(steps, reaches)
    zero = jnp.zeros((1, reaches), F32)
    back = coef_in * grad + coef_prev * jnp.concatenate([grad[1:], zero], axis=0)
    ahead = coef_in * answer + coef_prev * jnp.concatenate([zero, answer[:-1]], axis=0)
    block_of = (jnp.arange(reaches) // BLK + 1 + basin_id * blocks).astype(F32)
    table = jnp.concatenate([back, ahead, jnp.broadcast_to(block_of[None], (BLK, reaches))], axis=0)
    chosen = (inflow_src == jnp.arange(outlets)[:, None]).astype(F32)
    mine = lax.dot_general(chosen, table, NT, precision=lax.Precision.HIGHEST)
    parts = lax.all_to_all(mine.reshape(basins, blocks, 2 * steps + BLK), BASIN_AXES, 0, 0).sum(axis=0)
    width = (packet_shape[1] - CAP) // 8 * BLK
    place = jnp.arange(blocks) + label_lane(basin_id, basins)
    onto = (jnp.arange(width)[None, :] == place[:, None]).astype(F32)
    slot_row = ((jnp.arange(blocks) + basin_id * blocks + 1).astype(F32)[:, None] * onto).sum(axis=0)
    block_row = (parts[:, 2 * steps : 2 * steps + 1] * onto).sum(axis=0)
    labels = jnp.concatenate(
        [slot_row[None], block_row[None], jnp.zeros((6, width), F32)], axis=0
    )
    rate_rows = rates.reshape(-1, BLK)
    labels = labels.at[4 : 4 + rate_rows.shape[0], :BLK].set(rate_rows)
    labels = labels.reshape(8, width // BLK, BLK).transpose(1, 0, 2).reshape(-1, BLK)
    packet = jnp.concatenate(
        [parts[:, : 2 * steps], jnp.zeros((CAP - blocks, 2 * steps), F32), labels], axis=0
    )
    return exchange(jnp.broadcast_to(packet[None], packet_shape))


def solution(mesh):
    fine = jax.sharding.Mesh(
        mesh.devices.reshape(mesh.shape["level"], -1, 2), ("level", "column", "core")
    )
    series = P("level", None, BASIN_AXES)
    row = P("level", BASIN_AXES)
    units = P(None, LEVELS_AXES)
    return jax.shard_map(
        per_device,
        mesh=fine,
        in_specs=(series, row, row, row, row, units, series),
        out_specs=(series, units),
        check_vma=False,
    )
```

```python
import jax
import jax.numpy as jnp
from jax import lax
from jax.experimental import pallas as pl
from jax.experimental.pallas import tpu as pltpu
from jax.sharding import PartitionSpec as P

BLK = 128
SPLIT_FAST = 0.6
MUSK_X = 0.2
BASIN_AXES = ("column", "core")
LEVELS_AXES = ("level", "column", "core")
F32 = jnp.float32
BF16 = jnp.bfloat16
NN = (((1,), (0,)), ((), ()))
NT = (((1,), (1,)), ((), ()))
TN = (((0,), (0,)), ((), ()))
VMEM_LIMIT = 48 << 20
CAP = 16
NEAR = 5


def mm(left, right, dims):
    return lax.dot_general(left, right, dims, preferred_element_type=F32)


def split2(value):
    high = value.astype(BF16)
    return high, (value - high.astype(F32)).astype(BF16)


def split3(value):
    high = value.astype(BF16)
    rest = value - high.astype(F32)
    mid = rest.astype(BF16)
    return high, mid, (rest - mid.astype(F32)).astype(BF16)


def beside(*parts):
    return jnp.concatenate(parts, axis=1)


def above(*parts):
    return jnp.concatenate(parts, axis=0)


def folded(product):
    half = product.shape[1] // 2
    return product[:, :half] + product[:, half:]


def mm3(left, right, dims):
    high, low = right[0], right[1]
    empty = jnp.zeros_like(high)
    wide = beside(left[0], left[1])
    if dims == NT:
        return folded(mm(wide, above(beside(high, high), beside(low, empty)), NT))
    return folded(mm(wide, above(beside(high, low), beside(high, empty)), NN))


def mm6(left, right):
    high, mid, low = right
    first = mm(beside(left[0], left[1]), above(beside(high, mid), beside(high, mid)), NN)
    return folded(first) + mm(beside(left[0], left[2]), above(low, high), NN)


def pick(value, onehot, dims):
    high, mid, low = split3(value)
    if dims == TN:
        return mm(high, onehot, TN) + mm(mid, onehot, TN) + mm(low, onehot, TN)
    if dims == NT:
        both = beside(onehot, onehot)
    else:
        both = above(onehot, onehot)
    return mm(beside(high, mid), both, dims) + mm(low, onehot, dims)


def pick_right(onehot, value, dims):
    high, mid, low = split3(value)
    empty = jnp.zeros_like(low)
    wide = beside(onehot, onehot)
    if dims == NT:
        return folded(mm(wide, above(beside(high, mid), beside(low, empty)), NT))
    return folded(mm(wide, above(beside(high, low), beside(mid, empty)), NN))


def iota(shape, axis):
    return lax.broadcasted_iota(jnp.int32, shape, axis)


def coefficients(travel):
    twokx = 2.0 * travel * MUSK_X
    denom = 2.0 * travel * (1.0 - MUSK_X) + 1.0
    coef_in = (1.0 - twokx) / denom
    coef_prev = (1.0 + twokx) / denom
    coef_keep = (2.0 * travel * (1.0 - MUSK_X) - 1.0) / denom
    return coef_in, coef_prev, coef_keep


def shift_up(value, steps):
    rows = value.shape[0]
    if steps % 8 == 0:
        return jnp.concatenate([value[steps:], jnp.zeros((steps, value.shape[1]), F32)], axis=0)
    moved = pltpu.roll(value, rows - steps, 0)
    return jnp.where(iota(value.shape, 0) < rows - steps, moved, 0.0)


def shift_down(value, steps):
    rows = value.shape[0]
    if steps % 8 == 0:
        return jnp.concatenate(
            [jnp.zeros((steps, value.shape[1]), F32), value[: rows - steps]], axis=0
        )
    moved = pltpu.roll(value, steps, 0)
    return jnp.where(iota(value.shape, 0) >= steps, moved, 0.0)


def copies(pairs, sems):
    started = []
    for at, (source, target) in enumerate(pairs):
        copy = pltpu.make_async_copy(source, target, sems.at[at])
        copy.start()
        started.append(copy)
    return started


def stacked(row, blocks):
    return jnp.concatenate([row[:, b * BLK : (b + 1) * BLK] for b in range(blocks)], axis=0)


def still(*values):
    return [pltpu.with_memory_space_constraint(value, pltpu.HBM) for value in values]


def label_lane(basin_id, basins):
    column = basin_id // 2
    return ((basin_id - 2 * column) * (basins // 2) + column) * CAP


def relay_kernel(*refs):
    half = len(refs) // 2
    for copy in copies(list(zip(refs[:half], refs[half:-1])), refs[-1]):
        copy.wait()


def blocks_kernel(where_ref, travel_hbm, down_hbm, src_hbm, rates_hbm, cot_hbm,
                  packet_ref, grad_hbm, resp_hbm, move_hbm,
                  travel_ref, down_ref, src_ref, rates_ref, cot_ref,
                  grad_ref, resp_ref, move_ref, in_sems, out_sems, *, basins):
    steps, reaches = cot_ref.shape
    blocks = reaches // BLK
    copies_out, height, _ = packet_ref.shape
    width = (height - CAP) // 8 * BLK
    each = range(blocks)
    loads = copies(
        [(travel_hbm, travel_ref), (down_hbm, down_ref), (src_hbm, src_ref),
         (rates_hbm, rates_ref), (cot_hbm.at[0], cot_ref)], in_sems
    )
    for copy in loads[:4]:
        copy.wait()
    coef_in, coef_prev, coef_keep = coefficients(travel_ref[...])
    eye_mask = iota((BLK, BLK), 0) == iota((BLK, BLK), 1)
    eye = eye_mask.astype(F32)

    def part(row, b):
        return row[:, b * BLK : (b + 1) * BLK]

    downs = stacked(down_ref[...].astype(F32), blocks)
    columns = mm(eye.astype(BF16), downs.astype(BF16), NT)
    place = iota((BLK, BLK), 1).astype(F32)
    turned = [
        pick_right(eye.astype(BF16), stacked(row, blocks), NT)
        for row in (coef_in, coef_prev, coef_keep)
    ]
    linked = [jnp.broadcast_to(columns[:, b : b + 1], (BLK, BLK)) == place for b in each]
    base = [jnp.where(linked[b], part(coef_in, b), 0.0) for b in each]
    hops = [linked[b].astype(BF16) for b in each]
    total = [eye + base[b] for b in each]
    power = base
    for level in range(1, 8):
        for b in each:
            if level == 1:
                joined = power[b]
            elif level == 7:
                joined = total[b]
            else:
                joined = jnp.concatenate([power[b], total[b]], axis=1)
            if level <= 3:
                scale = jnp.sum(power[b], axis=1, keepdims=True)
                product = scale * pick_right(hops[b], joined, NN)
            else:
                filled = BLK - (1 << (level - 1))
                product = mm(power[b][:filled].astype(BF16), joined.astype(BF16), NN)
                empty = jnp.zeros((BLK - filled, joined.shape[1]), F32)
                product = jnp.concatenate([product, empty], axis=0)
            if level <= 2:
                hops[b] = mm(hops[b], hops[b], NN).astype(BF16)
            if level == 1:
                power[b] = product
            elif level == 7:
                total[b] = total[b] + product
            else:
                power[b] = product[:, :BLK]
                total[b] = total[b] + product[:, BLK:]
    inverse = [split2(total[b]) for b in each]
    stores = []

    def publish(at, moves):
        for b in each:
            move_ref[at, 0, b] = moves[b][0]
            move_ref[at, 1, b] = moves[b][1]
        copy = pltpu.make_async_copy(move_ref.at[at], move_hbm.at[at], out_sems.at[at])
        copy.start()
        stores.append(copy)

    publish(0, inverse)
    following = [
        pick_right(linked[b].astype(BF16), turned[1][:, b : b + 1] * total[b], NN)
        + turned[2][:, b : b + 1] * total[b]
        for b in each
    ]
    moves = [split3(following[b]) for b in each]
    loads[4].wait()
    state = [cot_ref[:, b * BLK : (b + 1) * BLK] for b in each]
    unit = jnp.where((iota((8, BLK), 0) == 0) & (iota((8, BLK), 1) == BLK - 1), 1.0, 0.0)
    rows = [unit for b in each]
    count = steps.bit_length() - 1
    for level in range(count):
        size = 1 << level
        publish(level + 1, moves)
        keep = steps - size
        for b in each:
            if size < 8:
                left = jnp.concatenate([shift_up(state[b], size), shift_down(rows[b], size)], axis=0)
                out = mm3(split2(left), moves[b], NT)
                state[b] = state[b] + out[:steps]
                rows[b] = rows[b] + out[steps:]
            else:
                left = jnp.concatenate([state[b][size:], rows[b]], axis=0)
                out = mm3(split2(left), moves[b], NT)
                state[b] = jnp.concatenate(
                    [state[b][:keep] + out[:keep], state[b][keep:]], axis=0
                )
                rows[b] = jnp.concatenate([rows[b], out[keep:]], axis=0)
        if level + 1 < count:
            if level < 2:
                moves = [split3(mm6(moves[b], moves[b])) for b in each]
            else:
                moves = [split2(mm3(moves[b], moves[b], NN)) for b in each]
    sources = stacked(src_ref[...], blocks)
    held = sources >= 0
    upper = (iota((BLK, BLK), 0) <= iota((BLK, BLK), 1)).astype(BF16)
    ranks = mm(held.astype(BF16), upper, NN)
    basin_id = where_ref[1]
    first_lane = label_lane(basin_id, basins)
    offset = jnp.zeros((1, 1), F32)
    packed = jnp.zeros((CAP, 2 * steps), F32)
    labels = jnp.zeros((8, width), F32)
    responses = []
    for b in each:
        both = mm3(split2(jnp.concatenate([state[b], rows[b]], axis=0)), inverse[b], NT)
        grad_ref[:, b * BLK : (b + 1) * BLK] = both[:steps]
        resp_ref[b] = both[steps:]
        responses.append(both)
    for copy in copies([(grad_ref, grad_hbm), (resp_ref, resp_hbm)], out_sems.at[pl.ds(count + 1, 2)]):
        stores.append(copy)
    for b in each:
        rank = jnp.where(held[b : b + 1], ranks[b : b + 1] + offset, 0.0)
        offset = offset + ranks[b : b + 1, BLK - 1 : BLK]
        row_at = iota((CAP, BLK), 0).astype(F32) + 1.0
        chosen = (jnp.broadcast_to(rank, (CAP, BLK)) == row_at).astype(BF16)
        grad = responses[b][:steps]
        resp = responses[b][steps:]
        now = part(coef_in, b)
        before = part(coef_prev, b)
        sent = jnp.concatenate(
            [now * grad + before * shift_up(grad, 1), now * resp + before * shift_down(resp, 1)],
            axis=0,
        )
        packed = packed + pick_right(chosen, sent, NT)
        lane_at = iota((width, BLK), 0) - first_lane
        wide = (
            (jnp.broadcast_to(rank, (width, BLK)) == lane_at.astype(F32) + 1.0) & (lane_at < CAP)
        ).astype(BF16)
        which = jnp.broadcast_to((sources[b : b + 1] + 1).astype(F32), (8, BLK))
        block_at = (basin_id * blocks + (b + 1)).astype(F32)
        values = jnp.where(iota((8, BLK), 0) == 0, which, block_at)
        labels = labels + mm(values.astype(BF16), wide, NT)
    labels = jnp.where(iota((8, width), 0) == 2, jnp.broadcast_to(offset, (8, width)), labels)
    parts = rates_ref.shape[1] // BLK
    rate_rows = [rates_ref[k : k + 1, h * BLK : (h + 1) * BLK] for k in range(2) for h in range(parts)]
    for group in range(width // BLK):
        rows_here = labels[:4, group * BLK : (group + 1) * BLK]
        first = CAP + 8 * group
        if group == 0:
            tail = rate_rows + [jnp.zeros((1, BLK), F32)] * (4 - len(rate_rows))
        else:
            tail = [jnp.zeros((4, BLK), F32)]
        piece = jnp.concatenate([rows_here] + tail, axis=0)
        packet_ref[:, first : first + 8, :] = jnp.broadcast_to(piece[None], (copies_out, 8, BLK))
    packet_ref[:, :CAP, :] = jnp.broadcast_to(packed[None], (copies_out, CAP, BLK))
    for copy in stores:
        copy.wait()


def lag_sum(steps, weight_ref, level, padded_ref, forward):
    tiles = steps // 8
    total = [jnp.zeros((8, padded_ref.shape[1]), F32)] * tiles
    for lag in range(steps):
        weight = weight_ref[level, lag : lag + 1, :]
        if forward:
            first, last = lag // 8, tiles
            start = steps - lag + 8 * first
        else:
            first, last = 0, tiles - lag // 8
            start = lag
        shifted = padded_ref[start : start + 8 * (last - first), :]
        for at in range(first, last):
            total[at] = total[at] + weight * shifted[8 * (at - first) : 8 * (at - first) + 8]
    return jnp.concatenate(total, axis=0)


def grads_kernel(where_ref, own_ref, other_ref, travel_hbm, unit_hbm, rain_hbm, grad_hbm, resp_hbm,
                 send_ref, drive_ref, weight_ref, ids_ref,
                 travel_ref, unit_ref, rain_ref, grad_ref, resp_ref,
                 lateral_ref, fast_ref, slow_ref, padded_ref, sems, *, levels, basins, units_here):
    steps, reaches = grad_ref.shape
    blocks = reaches // BLK
    pitch = steps + 8
    rains = [
        (rain_hbm.at[0, :, pl.ds(b * BLK, BLK)], rain_ref.at[pl.ds(b * pitch, steps)])
        for b in range(blocks)
    ]
    loads = copies(
        [(travel_hbm, travel_ref), (unit_hbm, unit_ref)] + rains
        + [(resp_hbm, resp_ref), (grad_hbm, grad_ref)], sems
    )
    devices = levels * basins
    lanes = ids_ref.shape[2]
    columns = basins // 2
    core = where_ref[2]
    most = jnp.max(
        jnp.maximum(own_ref[columns:, CAP : CAP + 8, :], other_ref[columns:, CAP : CAP + 8, :]), axis=0
    )[2:3, :]
    ids_ref[0] = jnp.broadcast_to(jnp.max(most, axis=1, keepdims=True), (8, lanes))
    outlets = basins * blocks
    halves = units_here // BLK
    level_id = where_ref[0]
    basin_id = where_ref[1]
    padded_ref[steps:, :] = jnp.zeros((steps, lanes), F32)
    back = [None]
    for l in range(1, levels):
        group = slice(l * columns, (l + 1) * columns)
        data = jnp.concatenate(
            [ref[group, :CAP, :].reshape(columns * CAP, BLK) for ref in (own_ref, other_ref)], axis=0
        )
        turned = jnp.transpose(data)
        labels = jnp.concatenate(
            [
                jnp.sum(
                    own_ref[group, CAP + 8 * g : CAP + 8 * g + 8, :]
                    + other_ref[group, CAP + 8 * g : CAP + 8 * g + 8, :],
                    axis=0,
                )
                for g in range((own_ref.shape[1] - CAP) // 8)
            ],
            axis=1,
        )[:, : basins * CAP]
        labels = jnp.where(core == 1, pltpu.roll(labels, columns * CAP, 1), labels)
        slot_of = (
            jnp.broadcast_to(labels[0:1], (lanes, basins * CAP))
            == iota((lanes, basins * CAP), 0).astype(F32) + 1.0
        ).astype(BF16)
        dense = pick(turned, slot_of, NT)
        back.append(dense[:steps])
        weight_ref[l] = dense[steps:]
        ids_ref[l] = mm(labels.astype(BF16), slot_of, NT)
    returned = back[levels - 1]
    mine = jnp.where(level_id == levels - 2, returned, 0.0)
    for l in range(levels - 2, 0, -1):
        member = (
            iota((lanes, lanes), 0).astype(F32) + 1.0
            == jnp.broadcast_to(ids_ref[l, 1:2, :], (lanes, lanes))
        ).astype(BF16)
        padded_ref[:steps, :] = pick(returned, member, NN)
        returned = back[l] + lag_sum(steps, weight_ref, l, padded_ref, False)
        mine = mine + jnp.where(level_id == l - 1, returned, 0.0)
    own = (iota((8, lanes), 1) == iota((8, lanes), 0) + basin_id * blocks).astype(BF16)
    if steps < BLK:
        mine = jnp.concatenate([mine, jnp.zeros((BLK - steps, lanes), F32)], axis=0)
    mine = pick_right(own, mine, NT)
    loads[0].wait()
    loads[1].wait()
    _, _, coef_keep = coefficients(travel_ref[...])
    unit_row = unit_ref[...] // BLK
    low = unit_ref[...] - unit_row * BLK
    places = (iota((BLK, reaches), 0) == jnp.broadcast_to(low, (BLK, reaches))).astype(BF16)
    owned = devices * halves
    at = iota((2 * owned, devices * 8), 0)
    kind = at // owned
    inside = at - kind * owned
    owner = inside // halves
    line = owner // 2 * 8 + 4 + kind * halves + inside % halves
    line = line + (owner + core) % 2 * (devices * 4)
    compact = (iota((2 * owned, devices * 8), 1) == line).astype(BF16)
    table = jnp.concatenate(
        [ref[:, CAP : CAP + 8, :].reshape(devices * 4, BLK) for ref in (own_ref, other_ref)], axis=0
    )
    spread = pick(pick_right(compact, table, NN), places, NN)
    row_at = iota((owned, reaches), 0) == jnp.broadcast_to(unit_row, (owned, reaches))
    fast_rate = jnp.sum(jnp.where(row_at, spread[:owned], 0.0), axis=0, keepdims=True)
    slow_rate = jnp.sum(jnp.where(row_at, spread[owned:], 0.0), axis=0, keepdims=True)
    fast_keep = jnp.exp(-fast_rate)
    slow_keep = jnp.exp(-slow_rate)
    for copy in loads[2 : 2 + blocks]:
        copy.wait()
    fast_by = stacked(fast_keep, blocks)
    slow_by = stacked(slow_keep, blocks)
    fast_gain = (1.0 - fast_by) * SPLIT_FAST
    slow_gain = (1.0 - slow_by) * (1.0 - SPLIT_FAST)
    zero = jnp.zeros((blocks, BLK), F32)
    fast, slow, fast_sens, slow_sens = zero, zero, zero, zero
    for step in range(steps):
        at = pl.ds(step, blocks, stride=pitch)
        rain = rain_ref[at, :]
        fast_sens = fast_by * fast_sens + (fast - SPLIT_FAST * rain)
        slow_sens = slow_by * slow_sens + (slow - (1.0 - SPLIT_FAST) * rain)
        fast = fast_by * fast + fast_gain * rain
        slow = slow_by * slow + slow_gain * rain
        lateral_ref[at, :] = fast + slow
        fast_ref[at, :] = fast_sens
        slow_ref[at, :] = slow_sens
    scale = 1.0 - coef_keep
    drives = []
    for b in range(blocks):
        drives.append(scale[:, b * BLK : (b + 1) * BLK] * lateral_ref[b * pitch : b * pitch + steps, :])
        drive_ref[b] = drives[b]
    loads[2 + blocks].wait()
    local = []
    for b in range(blocks):
        padded = jnp.concatenate(
            [drives[b], jnp.zeros((BLK - steps, BLK), F32)], axis=0
        )
        product = mm3(split2(resp_ref[b]), split2(padded), NT)
        skewed = pltpu.roll(product, 0, 1, stride=1, stride_axis=0)
        local.append(jnp.sum(skewed, axis=0, keepdims=True))
    loads[3 + blocks].wait()
    fast_sum = []
    slow_sum = []
    for b in range(blocks):
        spreadout = jnp.broadcast_to(mine[b : b + 1, :], (steps, BLK))
        at = iota((steps, BLK), 0)
        for bit in range(steps.bit_length() - 1):
            moved = pltpu.roll(spreadout, BLK - (1 << bit), 1)
            spreadout = jnp.where((at & (1 << bit)) != 0, moved, spreadout)
        resp = jnp.concatenate([resp_ref[b], jnp.zeros((BLK - steps, BLK), F32)], axis=0)
        grad = grad_ref[:, b * BLK : (b + 1) * BLK] + mm3(split2(spreadout), split2(resp), NN)
        side = slice(b * pitch, b * pitch + steps)
        fast_sum.append(jnp.sum(grad * fast_ref[side, :], axis=0, keepdims=True))
        slow_sum.append(jnp.sum(grad * slow_ref[side, :], axis=0, keepdims=True))
    fast_grad = -fast_keep * scale * jnp.concatenate(fast_sum, axis=1)
    slow_grad = -slow_keep * scale * jnp.concatenate(slow_sum, axis=1)
    terms = [
        jnp.where(row_at, jnp.broadcast_to(piece.astype(F32), (owned, reaches)), 0.0).astype(BF16)
        for pieces in zip(split3(fast_grad), split3(slow_grad))
        for piece in pieces
    ]
    parts = mm(jnp.concatenate(terms, axis=0), places, NT)
    summed = parts[: 2 * owned] + parts[2 * owned : 4 * owned] + parts[4 * owned :]
    at = iota((devices * 8, 2 * owned), 1)
    kind = at // owned
    inside = at - kind * owned
    line = inside // halves * 8 + 4 + kind * halves + inside % halves
    expand = (iota((devices * 8, 2 * owned), 0) == line).astype(BF16)
    send_ref[...] = pick_right(expand, summed, NN).reshape(devices, 8, BLK)
    half = blocks // 2
    for i in range(half):
        pair = jnp.concatenate([local[i][:, :steps], local[i + half][:, :steps]], axis=1)
        send_ref[:, i, :] = jnp.broadcast_to(pair, (devices, BLK))


def fetch_kernel(ids_ref, travel_hbm, src_hbm, move_hbm, *refs):
    move_refs = refs[:NEAR]
    coef_ref, source_ref, full_ref, travel_ref, src_ref, sems = refs[NEAR:]
    loads = copies(
        [(travel_hbm, travel_ref), (src_hbm, src_ref)]
        + [(move_hbm.at[k], move_refs[k]) for k in range(NEAR)], sems
    )
    full_ref[0] = jnp.max(ids_ref[0, 0:1, :]).astype(jnp.int32)
    loads[0].wait()
    loads[1].wait()
    coef_in, coef_prev, _ = coefficients(travel_ref[...])
    coef_ref[0:1, :] = coef_in
    coef_ref[1:2, :] = coef_prev
    lanes, reaches = source_ref.shape
    held = iota((lanes, reaches), 0) == jnp.broadcast_to(src_ref[...], (lanes, reaches))
    source_ref[...] = held.astype(BF16)
    for copy in loads[2:]:
        copy.wait()


def flows_kernel(where_ref, got_ref, coef_ref, source_ref, drive_ref, weight_ref, ids_ref, *refs,
                 levels, basins):
    near_refs = refs[:NEAR]
    move_hbm, flow_hbm, rate_hbm, far_ref, padded_ref, flow_ref, rate_ref, in_sems, out_sems = refs[NEAR:]
    blocks, steps, _ = drive_ref.shape
    far = move_hbm.shape[0] - NEAR
    loads = copies([(move_hbm.at[NEAR + k], far_ref.at[k]) for k in range(far)], in_sems)
    move_refs = [*near_refs] + [far_ref.at[k] for k in range(far)]
    reaches = blocks * BLK
    half = blocks // 2
    lanes = ids_ref.shape[2]
    level_id = where_ref[0]
    summed = jnp.sum(got_ref[...], axis=0)
    parts = rate_ref.shape[1] // BLK
    for k in range(2):
        for h in range(parts):
            at = 4 + k * parts + h
            rate_ref[k : k + 1, h * BLK : (h + 1) * BLK] = summed[at : at + 1]
    stores = [pltpu.make_async_copy(rate_ref, rate_hbm, out_sems.at[blocks])]
    padded_ref[:steps, :] = jnp.zeros((steps, lanes), F32)
    rows = basins * 8
    row = iota((rows, lanes), 0)
    column = iota((rows, lanes), 1)
    inner = row % 8
    left = ((inner < half) & (column == (row // 8) * blocks + inner)).astype(BF16)
    right = ((inner < half) & (column == (row // 8) * blocks + inner + half)).astype(BF16)
    outlet = None
    chosen = jnp.zeros((steps, lanes), F32)
    for l in range(levels - 1):
        block = got_ref[l * basins : (l + 1) * basins].reshape(rows, BLK)
        block = jnp.where(iota((rows, BLK), 0) % 8 < half, block, 0.0)
        local = pick(block, left, TN)[:steps] + pick(block, right, TN)[steps:]
        if l == 0:
            outlet = local
        else:
            padded_ref[steps:, :] = outlet
            arriving = lag_sum(steps, weight_ref, l, padded_ref, True)
            member = (
                iota((lanes, lanes), 0).astype(F32) + 1.0
                == jnp.broadcast_to(ids_ref[l, 1:2, :], (lanes, lanes))
            ).astype(BF16)
            outlet = local + pick(arriving, member, NT)
        chosen = chosen + jnp.where(level_id == l + 1, outlet, 0.0)
    inflow = pick(chosen, source_ref[...], NN)
    driving = coef_ref[0:1, :] * inflow + coef_ref[1:2, :] * shift_down(inflow, 1)
    each = range(blocks)
    state = [
        mm3(split2(driving[:, b * BLK : (b + 1) * BLK] + drive_ref[b]), (move_refs[0][0, b], move_refs[0][1, b]), NN)
        for b in each
    ]
    for level in range(steps.bit_length() - 1):
        size = 1 << level
        for b in each:
            if b == 0 and level + 1 >= NEAR:
                loads[level + 1 - NEAR].wait()
            move = (move_refs[level + 1][0, b], move_refs[level + 1][1, b])
            if size < 8:
                state[b] = state[b] + mm3(split2(shift_down(state[b], size)), move, NN)
            else:
                out = mm3(split2(state[b][: steps - size]), move, NN)
                state[b] = jnp.concatenate([state[b][:size], state[b][size:] + out], axis=0)
    for b in each:
        flow_ref[:, b * BLK : (b + 1) * BLK] = state[b]
        side = pl.ds(b * BLK, BLK)
        copy = pltpu.make_async_copy(flow_ref.at[:, side], flow_hbm.at[0, :, side], out_sems.at[b])
        copy.start()
        stores.append(copy)
    stores[0].start()
    for copy in stores:
        copy.wait()


def per_device(runoff, travel, downstream, inflow_src, reach_unit, rates, cotangent):
    _, steps, reaches = runoff.shape
    blocks = reaches // BLK
    levels = lax.axis_size("level")
    basins = lax.axis_size("column") * lax.axis_size("core")
    devices = levels * basins
    outlets = basins * blocks
    lanes = -(-outlets // BLK) * BLK
    units_here = rates.shape[1]
    halves = units_here // BLK
    count = steps.bit_length() - 1
    shape = jax.ShapeDtypeStruct
    smem = pl.BlockSpec(memory_space=pltpu.SMEM)
    vmem = pl.BlockSpec(memory_space=pltpu.VMEM)
    hbm = pl.BlockSpec(memory_space=pltpu.HBM)
    params = pltpu.CompilerParams(vmem_limit_bytes=VMEM_LIMIT)
    row_f32 = pltpu.VMEM((1, reaches), F32)
    row_i32 = pltpu.VMEM((1, reaches), jnp.int32)
    series = pltpu.VMEM((steps, reaches), F32)
    stack = pltpu.VMEM((blocks * (steps + 8), BLK), F32)
    answers = pltpu.VMEM((blocks, steps, BLK), F32)
    moves_shape = (count + 1, 2, blocks, BLK, BLK)
    height = CAP + 8 * (-(-basins * CAP // BLK))
    where = jnp.stack(
        [lax.axis_index("level"), lax.axis_index(BASIN_AXES), lax.axis_index("core")]
    ).astype(jnp.int32)
    packet, grad, resp, moves = pl.pallas_call(
        lambda *refs: blocks_kernel(*refs, basins=basins),
        out_shape=(
            shape((devices // 2, height, BLK), F32),
            shape((steps, reaches), F32),
            shape((blocks, steps, BLK), F32),
            shape(moves_shape, BF16),
        ),
        in_specs=[smem] + [hbm] * 5,
        out_specs=(vmem, hbm, hbm, hbm),
        scratch_shapes=[
            row_f32, row_i32, row_i32, pltpu.VMEM(rates.shape, F32), series,
            series, answers, pltpu.VMEM(moves_shape, BF16),
            pltpu.SemaphoreType.DMA((5,)), pltpu.SemaphoreType.DMA((count + 3,)),
        ],
        compiler_params=params,
        name="blocks",
    )(where, *still(travel, downstream, inflow_src, rates, cotangent))
    got = exchange(packet)

    def finish(got):
        sent, drive, weights, numbers = pl.pallas_call(
            lambda *refs: grads_kernel(*refs, levels=levels, basins=basins, units_here=units_here),
            out_shape=(
                shape((devices, 8, BLK), F32),
                shape((blocks, steps, BLK), F32),
                shape((levels, steps, lanes), F32),
                shape((levels, 8, lanes), F32),
            ),
            in_specs=[smem, vmem, vmem] + [hbm] * 5,
            out_specs=(vmem,) * 4,
            scratch_shapes=[row_f32, row_i32, stack, series, answers, stack, stack, stack,
                            pltpu.VMEM((2 * steps, lanes), F32), pltpu.SemaphoreType.DMA((blocks + 4,))],
            compiler_params=params,
            name="grads",
        )(where, *got, *still(travel, reach_unit, runoff, grad, resp))
        swapped = lax.all_to_all(sent, LEVELS_AXES, 0, 0)
        *near_moves, coefs, source, full = pl.pallas_call(
            fetch_kernel,
            out_shape=(
                *[shape(moves_shape[1:], BF16)] * NEAR,
                shape((2, reaches), F32),
                shape((lanes, reaches), BF16),
                shape((1,), jnp.int32),
            ),
            in_specs=[vmem] + [hbm] * 3,
            out_specs=(vmem,) * (NEAR + 2) + (smem,),
            scratch_shapes=[row_f32, row_i32, pltpu.SemaphoreType.DMA((NEAR + 2,))],
            compiler_params=params,
            name="fetch",
        )(numbers, *still(travel, inflow_src, moves))
        near = lambda *values: [pltpu.with_memory_space_constraint(value, pltpu.VMEM) for value in values]
        flows, totals = pl.pallas_call(
            lambda *refs: flows_kernel(*refs, levels=levels, basins=basins),
            out_shape=(shape((1, steps, reaches), F32), shape((2, units_here), F32)),
            in_specs=[smem] + [vmem] * (6 + NEAR) + [hbm],
            out_specs=(hbm, hbm),
            scratch_shapes=[pltpu.VMEM((count + 1 - NEAR, *moves_shape[1:]), BF16),
                            pltpu.VMEM((2 * steps, lanes), F32), series,
                            pltpu.VMEM((2, units_here), F32),
                            pltpu.SemaphoreType.DMA((count + 1 - NEAR,)),
                            pltpu.SemaphoreType.DMA((blocks + 1,))],
            compiler_params=params,
            name="flows",
        )(where, swapped, *near(coefs, source), drive, weights, numbers, *near(*near_moves), *still(moves))
        return flows, totals, full[0]

    flows, totals, full = finish(got)
    flows, totals = lax.cond(
        full > CAP,
        lambda done: finish(spread_sources(packet.shape, grad, resp, travel, inflow_src, rates))[:2],
        lambda done: done,
        (flows, totals),
    )
    return flows, totals


def exchange(packet):
    own = lax.all_to_all(packet, ("level", "column"), 0, 0)
    return own, lax.ppermute(own, "core", [(0, 1), (1, 0)])


def spread_sources(packet_shape, grad, resp, travel, inflow_src, rates):
    values = (grad, resp, travel, inflow_src, rates)
    grad, resp, travel, inflow_src, rates = pl.pallas_call(
        relay_kernel,
        out_shape=tuple(jax.ShapeDtypeStruct(value.shape, value.dtype) for value in values),
        in_specs=[pl.BlockSpec(memory_space=pltpu.HBM)] * len(values),
        out_specs=(pl.BlockSpec(memory_space=pltpu.HBM),) * len(values),
        scratch_shapes=[pltpu.SemaphoreType.DMA((len(values),))],
        name="relay",
    )(*still(*values))
    blocks, steps, _ = resp.shape
    basins = lax.axis_size("column") * lax.axis_size("core")
    basin_id = lax.axis_index(BASIN_AXES)
    outlets = basins * blocks
    reaches = blocks * BLK
    coef_in, coef_prev, _ = coefficients(travel)
    answer = resp.transpose(1, 0, 2).reshape(steps, reaches)
    zero = jnp.zeros((1, reaches), F32)
    back = coef_in * grad + coef_prev * jnp.concatenate([grad[1:], zero], axis=0)
    ahead = coef_in * answer + coef_prev * jnp.concatenate([zero, answer[:-1]], axis=0)
    block_of = (jnp.arange(reaches) // BLK + 1 + basin_id * blocks).astype(F32)
    table = jnp.concatenate([back, ahead, jnp.broadcast_to(block_of[None], (BLK, reaches))], axis=0)
    chosen = (inflow_src == jnp.arange(outlets)[:, None]).astype(F32)
    mine = lax.dot_general(chosen, table, NT, precision=lax.Precision.HIGHEST)
    parts = lax.all_to_all(mine.reshape(basins, blocks, 2 * steps + BLK), BASIN_AXES, 0, 0).sum(axis=0)
    width = (packet_shape[1] - CAP) // 8 * BLK
    place = jnp.arange(blocks) + label_lane(basin_id, basins)
    onto = (jnp.arange(width)[None, :] == place[:, None]).astype(F32)
    slot_row = ((jnp.arange(blocks) + basin_id * blocks + 1).astype(F32)[:, None] * onto).sum(axis=0)
    block_row = (parts[:, 2 * steps : 2 * steps + 1] * onto).sum(axis=0)
    labels = jnp.concatenate(
        [slot_row[None], block_row[None], jnp.zeros((6, width), F32)], axis=0
    )
    rate_rows = rates.reshape(-1, BLK)
    labels = labels.at[4 : 4 + rate_rows.shape[0], :BLK].set(rate_rows)
    labels = labels.reshape(8, width // BLK, BLK).transpose(1, 0, 2).reshape(-1, BLK)
    packet = jnp.concatenate(
        [parts[:, : 2 * steps], jnp.zeros((CAP - blocks, 2 * steps), F32), labels], axis=0
    )
    return exchange(jnp.broadcast_to(packet[None], packet_shape))


def solution(mesh):
    fine = jax.sharding.Mesh(
        mesh.devices.reshape(mesh.shape["level"], -1, 2), ("level", "column", "core")
    )
    series = P("level", None, BASIN_AXES)
    row = P("level", BASIN_AXES)
    units = P(None, LEVELS_AXES)
    return jax.shard_map(
        per_device,
        mesh=fine,
        in_specs=(series, row, row, row, row, units, series),
        out_specs=(series, units),
        check_vma=False,
    )
```

```python
import jax
import jax.numpy as jnp
from jax import lax
from jax.experimental import pallas as pl
from jax.experimental.pallas import tpu as pltpu
from jax.sharding import PartitionSpec as P

BLK = 128
SPLIT_FAST = 0.6
MUSK_X = 0.2
BASIN_AXES = ("column", "core")
LEVELS_AXES = ("level", "column", "core")
F32 = jnp.float32
BF16 = jnp.bfloat16
NN = (((1,), (0,)), ((), ()))
NT = (((1,), (1,)), ((), ()))
TN = (((0,), (0,)), ((), ()))
VMEM_LIMIT = 48 << 20
CAP = 16
NEAR = 5


def mm(left, right, dims):
    return lax.dot_general(left, right, dims, preferred_element_type=F32)


def split2(value):
    high = value.astype(BF16)
    return high, (value - high.astype(F32)).astype(BF16)


def split3(value):
    high = value.astype(BF16)
    rest = value - high.astype(F32)
    mid = rest.astype(BF16)
    return high, mid, (rest - mid.astype(F32)).astype(BF16)


def beside(*parts):
    return jnp.concatenate(parts, axis=1)


def above(*parts):
    return jnp.concatenate(parts, axis=0)


def folded(product):
    half = product.shape[1] // 2
    return product[:, :half] + product[:, half:]


def mm3(left, right, dims):
    high, low = right[0], right[1]
    empty = jnp.zeros_like(high)
    wide = beside(left[0], left[1])
    if dims == NT:
        return folded(mm(wide, above(beside(high, high), beside(low, empty)), NT))
    return folded(mm(wide, above(beside(high, low), beside(high, empty)), NN))


def mm6(left, right):
    high, mid, low = right
    first = mm(beside(left[0], left[1]), above(beside(high, mid), beside(high, mid)), NN)
    return folded(first) + mm(beside(left[0], left[2]), above(low, high), NN)


def pick(value, onehot, dims):
    high, mid, low = split3(value)
    if dims == TN:
        return mm(high, onehot, TN) + mm(mid, onehot, TN) + mm(low, onehot, TN)
    if dims == NT:
        both = beside(onehot, onehot)
    else:
        both = above(onehot, onehot)
    return mm(beside(high, mid), both, dims) + mm(low, onehot, dims)


def pick_right(onehot, value, dims):
    high, mid, low = split3(value)
    empty = jnp.zeros_like(low)
    wide = beside(onehot, onehot)
    if dims == NT:
        return folded(mm(wide, above(beside(high, mid), beside(low, empty)), NT))
    return folded(mm(wide, above(beside(high, low), beside(mid, empty)), NN))


def iota(shape, axis):
    return lax.broadcasted_iota(jnp.int32, shape, axis)


def coefficients(travel):
    twokx = 2.0 * travel * MUSK_X
    denom = 2.0 * travel * (1.0 - MUSK_X) + 1.0
    coef_in = (1.0 - twokx) / denom
    coef_prev = (1.0 + twokx) / denom
    coef_keep = (2.0 * travel * (1.0 - MUSK_X) - 1.0) / denom
    return coef_in, coef_prev, coef_keep


def shift_up(value, steps):
    rows = value.shape[0]
    if steps % 8 == 0:
        return jnp.concatenate([value[steps:], jnp.zeros((steps, value.shape[1]), F32)], axis=0)
    moved = pltpu.roll(value, rows - steps, 0)
    return jnp.where(iota(value.shape, 0) < rows - steps, moved, 0.0)


def shift_down(value, steps):
    rows = value.shape[0]
    if steps % 8 == 0:
        return jnp.concatenate(
            [jnp.zeros((steps, value.shape[1]), F32), value[: rows - steps]], axis=0
        )
    moved = pltpu.roll(value, steps, 0)
    return jnp.where(iota(value.shape, 0) >= steps, moved, 0.0)


def copies(pairs, sems):
    started = []
    for at, (source, target) in enumerate(pairs):
        copy = pltpu.make_async_copy(source, target, sems.at[at])
        copy.start()
        started.append(copy)
    return started


def stacked(row, blocks):
    return jnp.concatenate([row[:, b * BLK : (b + 1) * BLK] for b in range(blocks)], axis=0)


def still(*values):
    return [pltpu.with_memory_space_constraint(value, pltpu.HBM) for value in values]


def label_lane(basin_id, basins):
    column = basin_id // 2
    return ((basin_id - 2 * column) * (basins // 2) + column) * CAP


def relay_kernel(*refs):
    half = len(refs) // 2
    for copy in copies(list(zip(refs[:half], refs[half:-1])), refs[-1]):
        copy.wait()


def blocks_kernel(where_ref, travel_hbm, down_hbm, src_hbm, rates_hbm, cot_hbm,
                  packet_ref, grad_hbm, resp_hbm, move_hbm,
                  travel_ref, down_ref, src_ref, rates_ref, cot_ref,
                  grad_ref, resp_ref, move_ref, in_sems, out_sems, *, basins):
    steps, reaches = cot_ref.shape
    blocks = reaches // BLK
    copies_out, height, _ = packet_ref.shape
    width = (height - CAP) // 8 * BLK
    each = range(blocks)
    loads = copies(
        [(travel_hbm, travel_ref), (down_hbm, down_ref), (src_hbm, src_ref),
         (rates_hbm, rates_ref), (cot_hbm.at[0], cot_ref)], in_sems
    )
    for copy in loads[:4]:
        copy.wait()
    coef_in, coef_prev, coef_keep = coefficients(travel_ref[...])
    eye_mask = iota((BLK, BLK), 0) == iota((BLK, BLK), 1)
    eye = eye_mask.astype(F32)

    def part(row, b):
        return row[:, b * BLK : (b + 1) * BLK]

    downs = stacked(down_ref[...].astype(F32), blocks)
    columns = mm(eye.astype(BF16), downs.astype(BF16), NT)
    place = iota((BLK, BLK), 1).astype(F32)
    turned = [
        pick_right(eye.astype(BF16), stacked(row, blocks), NT)
        for row in (coef_in, coef_prev, coef_keep)
    ]
    linked = [jnp.broadcast_to(columns[:, b : b + 1], (BLK, BLK)) == place for b in each]
    base = [jnp.where(linked[b], part(coef_in, b), 0.0) for b in each]
    hops = [linked[b].astype(BF16) for b in each]
    total = [eye + base[b] for b in each]
    power = base
    for level in range(1, 8):
        for b in each:
            if level == 1:
                joined = power[b]
            elif level == 7:
                joined = total[b]
            else:
                joined = jnp.concatenate([power[b], total[b]], axis=1)
            if level <= 3:
                scale = jnp.sum(power[b], axis=1, keepdims=True)
                product = scale * pick_right(hops[b], joined, NN)
            else:
                filled = BLK - (1 << (level - 1))
                product = mm(power[b][:filled].astype(BF16), joined.astype(BF16), NN)
                empty = jnp.zeros((BLK - filled, joined.shape[1]), F32)
                product = jnp.concatenate([product, empty], axis=0)
            if level <= 2:
                hops[b] = mm(hops[b], hops[b], NN).astype(BF16)
            if level == 1:
                power[b] = product
            elif level == 7:
                total[b] = total[b] + product
            else:
                power[b] = product[:, :BLK]
                total[b] = total[b] + product[:, BLK:]
    inverse = [split2(total[b]) for b in each]
    stores = []

    def publish(at, moves):
        for b in each:
            move_ref[at, 0, b] = moves[b][0]
            move_ref[at, 1, b] = moves[b][1]
        copy = pltpu.make_async_copy(move_ref.at[at], move_hbm.at[at], out_sems.at[at])
        copy.start()
        stores.append(copy)

    publish(0, inverse)
    following = [
        pick_right(linked[b].astype(BF16), turned[1][:, b : b + 1] * total[b], NN)
        + turned[2][:, b : b + 1] * total[b]
        for b in each
    ]
    moves = [split3(following[b]) for b in each]
    loads[4].wait()
    state = [cot_ref[:, b * BLK : (b + 1) * BLK] for b in each]
    unit = jnp.where((iota((8, BLK), 0) == 0) & (iota((8, BLK), 1) == BLK - 1), 1.0, 0.0)
    rows = [unit for b in each]
    count = steps.bit_length() - 1
    for level in range(count):
        size = 1 << level
        publish(level + 1, moves)
        keep = steps - size
        for b in each:
            if size < 8:
                left = jnp.concatenate([shift_up(state[b], size), shift_down(rows[b], size)], axis=0)
                out = mm3(split2(left), moves[b], NT)
                state[b] = state[b] + out[:steps]
                rows[b] = rows[b] + out[steps:]
            else:
                left = jnp.concatenate([state[b][size:], rows[b]], axis=0)
                out = mm3(split2(left), moves[b], NT)
                state[b] = jnp.concatenate(
                    [state[b][:keep] + out[:keep], state[b][keep:]], axis=0
                )
                rows[b] = jnp.concatenate([rows[b], out[keep:]], axis=0)
        if level + 1 < count:
            if level < 2:
                moves = [split3(mm6(moves[b], moves[b])) for b in each]
            else:
                moves = [split2(mm3(moves[b], moves[b], NN)) for b in each]
    sources = stacked(src_ref[...], blocks)
    held = sources >= 0
    upper = (iota((BLK, BLK), 0) <= iota((BLK, BLK), 1)).astype(BF16)
    ranks = mm(held.astype(BF16), upper, NN)
    basin_id = where_ref[1]
    first_lane = label_lane(basin_id, basins)
    offset = jnp.zeros((1, 1), F32)
    packed = jnp.zeros((CAP, 2 * steps), F32)
    labels = jnp.zeros((8, width), F32)
    responses = []
    for b in each:
        both = mm3(split2(jnp.concatenate([state[b], rows[b]], axis=0)), inverse[b], NT)
        grad_ref[:, b * BLK : (b + 1) * BLK] = both[:steps]
        resp_ref[b] = both[steps:]
        responses.append(both)
    for copy in copies([(grad_ref, grad_hbm), (resp_ref, resp_hbm)], out_sems.at[pl.ds(count + 1, 2)]):
        stores.append(copy)
    for b in each:
        rank = jnp.where(held[b : b + 1], ranks[b : b + 1] + offset, 0.0)
        offset = offset + ranks[b : b + 1, BLK - 1 : BLK]
        row_at = iota((CAP, BLK), 0).astype(F32) + 1.0
        chosen = (jnp.broadcast_to(rank, (CAP, BLK)) == row_at).astype(BF16)
        grad = responses[b][:steps]
        resp = responses[b][steps:]
        now = part(coef_in, b)
        before = part(coef_prev, b)
        sent = jnp.concatenate(
            [now * grad + before * shift_up(grad, 1), now * resp + before * shift_down(resp, 1)],
            axis=0,
        )
        packed = packed + pick_right(chosen, sent, NT)
        lane_at = iota((width, BLK), 0) - first_lane
        wide = (
            (jnp.broadcast_to(rank, (width, BLK)) == lane_at.astype(F32) + 1.0) & (lane_at < CAP)
        ).astype(BF16)
        which = jnp.broadcast_to((sources[b : b + 1] + 1).astype(F32), (8, BLK))
        block_at = (basin_id * blocks + (b + 1)).astype(F32)
        values = jnp.where(iota((8, BLK), 0) == 0, which, block_at)
        labels = labels + mm(values.astype(BF16), wide, NT)
    labels = jnp.where(iota((8, width), 0) == 2, jnp.broadcast_to(offset, (8, width)), labels)
    parts = rates_ref.shape[1] // BLK
    rate_rows = [rates_ref[k : k + 1, h * BLK : (h + 1) * BLK] for k in range(2) for h in range(parts)]
    for group in range(width // BLK):
        rows_here = labels[:4, group * BLK : (group + 1) * BLK]
        first = CAP + 8 * group
        if group == 0:
            tail = rate_rows + [jnp.zeros((1, BLK), F32)] * (4 - len(rate_rows))
        else:
            tail = [jnp.zeros((4, BLK), F32)]
        piece = jnp.concatenate([rows_here] + tail, axis=0)
        packet_ref[:, first : first + 8, :] = jnp.broadcast_to(piece[None], (copies_out, 8, BLK))
    packet_ref[:, :CAP, :] = jnp.broadcast_to(packed[None], (copies_out, CAP, BLK))
    for copy in stores:
        copy.wait()


def lag_sum(steps, weight_ref, level, padded_ref, forward):
    tiles = steps // 8
    total = [jnp.zeros((8, padded_ref.shape[1]), F32)] * tiles
    for lag in range(steps):
        weight = weight_ref[level, lag : lag + 1, :]
        if forward:
            first, last = lag // 8, tiles
            start = steps - lag + 8 * first
        else:
            first, last = 0, tiles - lag // 8
            start = lag
        shifted = padded_ref[start : start + 8 * (last - first), :]
        for at in range(first, last):
            total[at] = total[at] + weight * shifted[8 * (at - first) : 8 * (at - first) + 8]
    return jnp.concatenate(total, axis=0)


def grads_kernel(where_ref, own_ref, other_ref, travel_hbm, unit_hbm, rain_hbm, grad_hbm, resp_hbm,
                 send_ref, drive_ref, weight_ref, ids_ref,
                 travel_ref, unit_ref, rain_ref, grad_ref, resp_ref,
                 lateral_ref, fast_ref, slow_ref, padded_ref, sems, *, levels, basins, units_here):
    steps, reaches = grad_ref.shape
    blocks = reaches // BLK
    pitch = steps + 8
    rains = [
        (rain_hbm.at[0, :, pl.ds(b * BLK, BLK)], rain_ref.at[pl.ds(b * pitch, steps)])
        for b in range(blocks)
    ]
    loads = copies(
        [(travel_hbm, travel_ref), (unit_hbm, unit_ref)] + rains
        + [(resp_hbm, resp_ref), (grad_hbm, grad_ref)], sems
    )
    devices = levels * basins
    lanes = ids_ref.shape[2]
    columns = basins // 2
    core = where_ref[2]
    most = jnp.max(
        jnp.maximum(own_ref[columns:, CAP : CAP + 8, :], other_ref[columns:, CAP : CAP + 8, :]), axis=0
    )[2:3, :]
    ids_ref[0] = jnp.broadcast_to(jnp.concatenate([most] * (lanes // BLK), axis=1), (8, lanes))
    outlets = basins * blocks
    halves = units_here // BLK
    level_id = where_ref[0]
    basin_id = where_ref[1]
    padded_ref[steps:, :] = jnp.zeros((steps, lanes), F32)
    back = [None]
    for l in range(1, levels):
        group = slice(l * columns, (l + 1) * columns)
        data = jnp.concatenate(
            [ref[group, :CAP, :].reshape(columns * CAP, BLK) for ref in (own_ref, other_ref)], axis=0
        )
        turned = jnp.transpose(data)
        labels = jnp.concatenate(
            [
                jnp.sum(
                    own_ref[group, CAP + 8 * g : CAP + 8 * g + 8, :]
                    + other_ref[group, CAP + 8 * g : CAP + 8 * g + 8, :],
                    axis=0,
                )
                for g in range((own_ref.shape[1] - CAP) // 8)
            ],
            axis=1,
        )[:, : basins * CAP]
        labels = jnp.where(core == 1, pltpu.roll(labels, columns * CAP, 1), labels)
        slot_of = (
            jnp.broadcast_to(labels[0:1], (lanes, basins * CAP))
            == iota((lanes, basins * CAP), 0).astype(F32) + 1.0
        ).astype(BF16)
        dense = pick(turned, slot_of, NT)
        back.append(dense[:steps])
        weight_ref[l] = dense[steps:]
        ids_ref[l] = mm(labels.astype(BF16), slot_of, NT)
    returned = back[levels - 1]
    mine = jnp.where(level_id == levels - 2, returned, 0.0)
    for l in range(levels - 2, 0, -1):
        member = (
            iota((lanes, lanes), 0).astype(F32) + 1.0
            == jnp.broadcast_to(ids_ref[l, 1:2, :], (lanes, lanes))
        ).astype(BF16)
        padded_ref[:steps, :] = pick(returned, member, NN)
        returned = back[l] + lag_sum(steps, weight_ref, l, padded_ref, False)
        mine = mine + jnp.where(level_id == l - 1, returned, 0.0)
    own = (iota((8, lanes), 1) == iota((8, lanes), 0) + basin_id * blocks).astype(BF16)
    if steps < BLK:
        mine = jnp.concatenate([mine, jnp.zeros((BLK - steps, lanes), F32)], axis=0)
    mine = pick_right(own, mine, NT)
    loads[0].wait()
    loads[1].wait()
    _, _, coef_keep = coefficients(travel_ref[...])
    unit_row = unit_ref[...] // BLK
    low = unit_ref[...] - unit_row * BLK
    places = (iota((BLK, reaches), 0) == jnp.broadcast_to(low, (BLK, reaches))).astype(BF16)
    owned = devices * halves
    at = iota((2 * owned, devices * 8), 0)
    kind = at // owned
    inside = at - kind * owned
    owner = inside // halves
    line = owner // 2 * 8 + 4 + kind * halves + inside % halves
    line = line + (owner + core) % 2 * (devices * 4)
    compact = (iota((2 * owned, devices * 8), 1) == line).astype(BF16)
    table = jnp.concatenate(
        [ref[:, CAP : CAP + 8, :].reshape(devices * 4, BLK) for ref in (own_ref, other_ref)], axis=0
    )
    spread = pick(pick_right(compact, table, NN), places, NN)
    row_at = iota((owned, reaches), 0) == jnp.broadcast_to(unit_row, (owned, reaches))
    fast_rate = jnp.sum(jnp.where(row_at, spread[:owned], 0.0), axis=0, keepdims=True)
    slow_rate = jnp.sum(jnp.where(row_at, spread[owned:], 0.0), axis=0, keepdims=True)
    fast_keep = jnp.exp(-fast_rate)
    slow_keep = jnp.exp(-slow_rate)
    for copy in loads[2 : 2 + blocks]:
        copy.wait()
    fast_by = stacked(fast_keep, blocks)
    slow_by = stacked(slow_keep, blocks)
    fast_gain = (1.0 - fast_by) * SPLIT_FAST
    slow_gain = (1.0 - slow_by) * (1.0 - SPLIT_FAST)
    zero = jnp.zeros((blocks, BLK), F32)
    fast, slow, fast_sens, slow_sens = zero, zero, zero, zero
    for step in range(steps):
        at = pl.ds(step, blocks, stride=pitch)
        rain = rain_ref[at, :]
        fast_sens = fast_by * fast_sens + (fast - SPLIT_FAST * rain)
        slow_sens = slow_by * slow_sens + (slow - (1.0 - SPLIT_FAST) * rain)
        fast = fast_by * fast + fast_gain * rain
        slow = slow_by * slow + slow_gain * rain
        lateral_ref[at, :] = fast + slow
        fast_ref[at, :] = fast_sens
        slow_ref[at, :] = slow_sens
    scale = 1.0 - coef_keep
    drives = []
    for b in range(blocks):
        drives.append(scale[:, b * BLK : (b + 1) * BLK] * lateral_ref[b * pitch : b * pitch + steps, :])
        drive_ref[b] = drives[b]
    loads[2 + blocks].wait()
    local = []
    for b in range(blocks):
        padded = jnp.concatenate(
            [drives[b], jnp.zeros((BLK - steps, BLK), F32)], axis=0
        )
        product = mm3(split2(resp_ref[b]), split2(padded), NT)
        skewed = pltpu.roll(product, 0, 1, stride=1, stride_axis=0)
        local.append(jnp.sum(skewed, axis=0, keepdims=True))
    loads[3 + blocks].wait()
    fast_sum = []
    slow_sum = []
    for b in range(blocks):
        spreadout = jnp.broadcast_to(mine[b : b + 1, :], (steps, BLK))
        at = iota((steps, BLK), 0)
        for bit in range(steps.bit_length() - 1):
            moved = pltpu.roll(spreadout, BLK - (1 << bit), 1)
            spreadout = jnp.where((at & (1 << bit)) != 0, moved, spreadout)
        resp = jnp.concatenate([resp_ref[b], jnp.zeros((BLK - steps, BLK), F32)], axis=0)
        grad = grad_ref[:, b * BLK : (b + 1) * BLK] + mm3(split2(spreadout), split2(resp), NN)
        side = slice(b * pitch, b * pitch + steps)
        fast_sum.append(jnp.sum(grad * fast_ref[side, :], axis=0, keepdims=True))
        slow_sum.append(jnp.sum(grad * slow_ref[side, :], axis=0, keepdims=True))
    fast_grad = -fast_keep * scale * jnp.concatenate(fast_sum, axis=1)
    slow_grad = -slow_keep * scale * jnp.concatenate(slow_sum, axis=1)
    terms = [
        jnp.where(row_at, jnp.broadcast_to(piece.astype(F32), (owned, reaches)), 0.0).astype(BF16)
        for pieces in zip(split3(fast_grad), split3(slow_grad))
        for piece in pieces
    ]
    parts = mm(jnp.concatenate(terms, axis=0), places, NT)
    summed = parts[: 2 * owned] + parts[2 * owned : 4 * owned] + parts[4 * owned :]
    at = iota((devices * 8, 2 * owned), 1)
    kind = at // owned
    inside = at - kind * owned
    line = inside // halves * 8 + 4 + kind * halves + inside % halves
    expand = (iota((devices * 8, 2 * owned), 0) == line).astype(BF16)
    send_ref[...] = pick_right(expand, summed, NN).reshape(devices, 8, BLK)
    half = blocks // 2
    for i in range(half):
        pair = jnp.concatenate([local[i][:, :steps], local[i + half][:, :steps]], axis=1)
        send_ref[:, i, :] = jnp.broadcast_to(pair, (devices, BLK))


def fetch_kernel(ids_ref, travel_hbm, src_hbm, move_hbm, *refs):
    move_refs = refs[:NEAR]
    coef_ref, source_ref, full_ref, travel_ref, src_ref, sems = refs[NEAR:]
    loads = copies(
        [(travel_hbm, travel_ref), (src_hbm, src_ref)]
        + [(move_hbm.at[k], move_refs[k]) for k in range(NEAR)], sems
    )
    full_ref[0] = jnp.max(ids_ref[0, 0:1, :]).astype(jnp.int32)
    loads[0].wait()
    loads[1].wait()
    coef_in, coef_prev, _ = coefficients(travel_ref[...])
    coef_ref[0:1, :] = coef_in
    coef_ref[1:2, :] = coef_prev
    lanes, reaches = source_ref.shape
    held = iota((lanes, reaches), 0) == jnp.broadcast_to(src_ref[...], (lanes, reaches))
    source_ref[...] = held.astype(BF16)
    for copy in loads[2:]:
        copy.wait()


def flows_kernel(where_ref, got_ref, coef_ref, source_ref, drive_ref, weight_ref, ids_ref, *refs,
                 levels, basins):
    near_refs = refs[:NEAR]
    move_hbm, flow_hbm, rate_hbm, far_ref, padded_ref, flow_ref, rate_ref, in_sems, out_sems = refs[NEAR:]
    blocks, steps, _ = drive_ref.shape
    far = move_hbm.shape[0] - NEAR
    loads = copies([(move_hbm.at[NEAR + k], far_ref.at[k]) for k in range(far)], in_sems)
    move_refs = [*near_refs] + [far_ref.at[k] for k in range(far)]
    reaches = blocks * BLK
    half = blocks // 2
    lanes = ids_ref.shape[2]
    level_id = where_ref[0]
    summed = jnp.sum(got_ref[...], axis=0)
    parts = rate_ref.shape[1] // BLK
    for k in range(2):
        for h in range(parts):
            at = 4 + k * parts + h
            rate_ref[k : k + 1, h * BLK : (h + 1) * BLK] = summed[at : at + 1]
    stores = [pltpu.make_async_copy(rate_ref, rate_hbm, out_sems.at[blocks])]
    padded_ref[:steps, :] = jnp.zeros((steps, lanes), F32)
    rows = basins * 8
    row = iota((rows, lanes), 0)
    column = iota((rows, lanes), 1)
    inner = row % 8
    left = ((inner < half) & (column == (row // 8) * blocks + inner)).astype(BF16)
    right = ((inner < half) & (column == (row // 8) * blocks + inner + half)).astype(BF16)
    outlet = None
    chosen = jnp.zeros((steps, lanes), F32)
    for l in range(levels - 1):
        block = got_ref[l * basins : (l + 1) * basins].reshape(rows, BLK)
        block = jnp.where(iota((rows, BLK), 0) % 8 < half, block, 0.0)
        local = pick(block, left, TN)[:steps] + pick(block, right, TN)[steps:]
        if l == 0:
            outlet = local
        else:
            padded_ref[steps:, :] = outlet
            arriving = lag_sum(steps, weight_ref, l, padded_ref, True)
            member = (
                iota((lanes, lanes), 0).astype(F32) + 1.0
                == jnp.broadcast_to(ids_ref[l, 1:2, :], (lanes, lanes))
            ).astype(BF16)
            outlet = local + pick(arriving, member, NT)
        chosen = chosen + jnp.where(level_id == l + 1, outlet, 0.0)
    inflow = pick(chosen, source_ref[...], NN)
    driving = coef_ref[0:1, :] * inflow + coef_ref[1:2, :] * shift_down(inflow, 1)
    each = range(blocks)
    state = [
        mm3(split2(driving[:, b * BLK : (b + 1) * BLK] + drive_ref[b]), (move_refs[0][0, b], move_refs[0][1, b]), NN)
        for b in each
    ]
    for level in range(steps.bit_length() - 1):
        size = 1 << level
        for b in each:
            if b == 0 and level + 1 >= NEAR:
                loads[level + 1 - NEAR].wait()
            move = (move_refs[level + 1][0, b], move_refs[level + 1][1, b])
            if size < 8:
                state[b] = state[b] + mm3(split2(shift_down(state[b], size)), move, NN)
            else:
                out = mm3(split2(state[b][: steps - size]), move, NN)
                state[b] = jnp.concatenate([state[b][:size], state[b][size:] + out], axis=0)
    for b in each:
        flow_ref[:, b * BLK : (b + 1) * BLK] = state[b]
        side = pl.ds(b * BLK, BLK)
        copy = pltpu.make_async_copy(flow_ref.at[:, side], flow_hbm.at[0, :, side], out_sems.at[b])
        copy.start()
        stores.append(copy)
    stores[0].start()
    for copy in stores:
        copy.wait()


def per_device(runoff, travel, downstream, inflow_src, reach_unit, rates, cotangent):
    _, steps, reaches = runoff.shape
    blocks = reaches // BLK
    levels = lax.axis_size("level")
    basins = lax.axis_size("column") * lax.axis_size("core")
    devices = levels * basins
    outlets = basins * blocks
    lanes = -(-outlets // BLK) * BLK
    units_here = rates.shape[1]
    halves = units_here // BLK
    count = steps.bit_length() - 1
    shape = jax.ShapeDtypeStruct
    smem = pl.BlockSpec(memory_space=pltpu.SMEM)
    vmem = pl.BlockSpec(memory_space=pltpu.VMEM)
    hbm = pl.BlockSpec(memory_space=pltpu.HBM)
    params = pltpu.CompilerParams(vmem_limit_bytes=VMEM_LIMIT)
    row_f32 = pltpu.VMEM((1, reaches), F32)
    row_i32 = pltpu.VMEM((1, reaches), jnp.int32)
    series = pltpu.VMEM((steps, reaches), F32)
    stack = pltpu.VMEM((blocks * (steps + 8), BLK), F32)
    answers = pltpu.VMEM((blocks, steps, BLK), F32)
    moves_shape = (count + 1, 2, blocks, BLK, BLK)
    height = CAP + 8 * (-(-basins * CAP // BLK))
    where = jnp.stack(
        [lax.axis_index("level"), lax.axis_index(BASIN_AXES), lax.axis_index("core")]
    ).astype(jnp.int32)
    packet, grad, resp, moves = pl.pallas_call(
        lambda *refs: blocks_kernel(*refs, basins=basins),
        out_shape=(
            shape((devices // 2, height, BLK), F32),
            shape((steps, reaches), F32),
            shape((blocks, steps, BLK), F32),
            shape(moves_shape, BF16),
        ),
        in_specs=[smem] + [hbm] * 5,
        out_specs=(vmem, hbm, hbm, hbm),
        scratch_shapes=[
            row_f32, row_i32, row_i32, pltpu.VMEM(rates.shape, F32), series,
            series, answers, pltpu.VMEM(moves_shape, BF16),
            pltpu.SemaphoreType.DMA((5,)), pltpu.SemaphoreType.DMA((count + 3,)),
        ],
        compiler_params=params,
        name="blocks",
    )(where, *still(travel, downstream, inflow_src, rates, cotangent))
    got = exchange(packet)

    def finish(got):
        sent, drive, weights, numbers = pl.pallas_call(
            lambda *refs: grads_kernel(*refs, levels=levels, basins=basins, units_here=units_here),
            out_shape=(
                shape((devices, 8, BLK), F32),
                shape((blocks, steps, BLK), F32),
                shape((levels, steps, lanes), F32),
                shape((levels, 8, lanes), F32),
            ),
            in_specs=[smem, vmem, vmem] + [hbm] * 5,
            out_specs=(vmem,) * 4,
            scratch_shapes=[row_f32, row_i32, stack, series, answers, stack, stack, stack,
                            pltpu.VMEM((2 * steps, lanes), F32), pltpu.SemaphoreType.DMA((blocks + 4,))],
            compiler_params=params,
            name="grads",
        )(where, *got, *still(travel, reach_unit, runoff, grad, resp))
        swapped = lax.all_to_all(sent, LEVELS_AXES, 0, 0)
        *near_moves, coefs, source, full = pl.pallas_call(
            fetch_kernel,
            out_shape=(
                *[shape(moves_shape[1:], BF16)] * NEAR,
                shape((2, reaches), F32),
                shape((lanes, reaches), BF16),
                shape((1,), jnp.int32),
            ),
            in_specs=[vmem] + [hbm] * 3,
            out_specs=(vmem,) * (NEAR + 2) + (smem,),
            scratch_shapes=[row_f32, row_i32, pltpu.SemaphoreType.DMA((NEAR + 2,))],
            compiler_params=params,
            name="fetch",
        )(numbers, *still(travel, inflow_src, moves))
        near = lambda *values: [pltpu.with_memory_space_constraint(value, pltpu.VMEM) for value in values]
        flows, totals = pl.pallas_call(
            lambda *refs: flows_kernel(*refs, levels=levels, basins=basins),
            out_shape=(shape((1, steps, reaches), F32), shape((2, units_here), F32)),
            in_specs=[smem] + [vmem] * (6 + NEAR) + [hbm],
            out_specs=(hbm, hbm),
            scratch_shapes=[pltpu.VMEM((count + 1 - NEAR, *moves_shape[1:]), BF16),
                            pltpu.VMEM((2 * steps, lanes), F32), series,
                            pltpu.VMEM((2, units_here), F32),
                            pltpu.SemaphoreType.DMA((count + 1 - NEAR,)),
                            pltpu.SemaphoreType.DMA((blocks + 1,))],
            compiler_params=params,
            name="flows",
        )(where, swapped, *near(coefs, source), drive, weights, numbers, *near(*near_moves), *still(moves))
        return flows, totals, full[0]

    flows, totals, full = finish(got)
    flows, totals = lax.cond(
        full > CAP,
        lambda done: finish(spread_sources(packet.shape, grad, resp, travel, inflow_src, rates))[:2],
        lambda done: done,
        (flows, totals),
    )
    return flows, totals


def exchange(packet):
    own = lax.all_to_all(packet, ("level", "column"), 0, 0)
    return own, lax.ppermute(own, "core", [(0, 1), (1, 0)])


def spread_sources(packet_shape, grad, resp, travel, inflow_src, rates):
    values = (grad, resp, travel, inflow_src, rates)
    grad, resp, travel, inflow_src, rates = pl.pallas_call(
        relay_kernel,
        out_shape=tuple(jax.ShapeDtypeStruct(value.shape, value.dtype) for value in values),
        in_specs=[pl.BlockSpec(memory_space=pltpu.HBM)] * len(values),
        out_specs=(pl.BlockSpec(memory_space=pltpu.HBM),) * len(values),
        scratch_shapes=[pltpu.SemaphoreType.DMA((len(values),))],
        name="relay",
    )(*still(*values))
    blocks, steps, _ = resp.shape
    basins = lax.axis_size("column") * lax.axis_size("core")
    basin_id = lax.axis_index(BASIN_AXES)
    outlets = basins * blocks
    reaches = blocks * BLK
    coef_in, coef_prev, _ = coefficients(travel)
    answer = resp.transpose(1, 0, 2).reshape(steps, reaches)
    zero = jnp.zeros((1, reaches), F32)
    back = coef_in * grad + coef_prev * jnp.concatenate([grad[1:], zero], axis=0)
    ahead = coef_in * answer + coef_prev * jnp.concatenate([zero, answer[:-1]], axis=0)
    block_of = (jnp.arange(reaches) // BLK + 1 + basin_id * blocks).astype(F32)
    table = jnp.concatenate([back, ahead, jnp.broadcast_to(block_of[None], (BLK, reaches))], axis=0)
    chosen = (inflow_src == jnp.arange(outlets)[:, None]).astype(F32)
    mine = lax.dot_general(chosen, table, NT, precision=lax.Precision.HIGHEST)
    parts = lax.all_to_all(mine.reshape(basins, blocks, 2 * steps + BLK), BASIN_AXES, 0, 0).sum(axis=0)
    width = (packet_shape[1] - CAP) // 8 * BLK
    place = jnp.arange(blocks) + label_lane(basin_id, basins)
    onto = (jnp.arange(width)[None, :] == place[:, None]).astype(F32)
    slot_row = ((jnp.arange(blocks) + basin_id * blocks + 1).astype(F32)[:, None] * onto).sum(axis=0)
    block_row = (parts[:, 2 * steps : 2 * steps + 1] * onto).sum(axis=0)
    labels = jnp.concatenate(
        [slot_row[None], block_row[None], jnp.zeros((6, width), F32)], axis=0
    )
    rate_rows = rates.reshape(-1, BLK)
    labels = labels.at[4 : 4 + rate_rows.shape[0], :BLK].set(rate_rows)
    labels = labels.reshape(8, width // BLK, BLK).transpose(1, 0, 2).reshape(-1, BLK)
    packet = jnp.concatenate(
        [parts[:, : 2 * steps], jnp.zeros((CAP - blocks, 2 * steps), F32), labels], axis=0
    )
    return exchange(jnp.broadcast_to(packet[None], packet_shape))


def solution(mesh):
    fine = jax.sharding.Mesh(
        mesh.devices.reshape(mesh.shape["level"], -1, 2), ("level", "column", "core")
    )
    series = P("level", None, BASIN_AXES)
    row = P("level", BASIN_AXES)
    units = P(None, LEVELS_AXES)
    return jax.shard_map(
        per_device,
        mesh=fine,
        in_specs=(series, row, row, row, row, units, series),
        out_specs=(series, units),
        check_vma=False,
    )
```
